32 devices in a mesh: role: 2 (over x), seq: 4 (over y, core), mp: 4 (over z).
Axes of the slice: x: 2, y: 2, z: 4, core: 2. Of those that a mesh axis runs over, the one named last changes fastest.
Arguments:
- rollout: bfloat16 [2, 1536, 64], P('role', 'seq'), may hold values from -6.5 to 6.5
- w_embed: bfloat16 [64, 5120], replicated, may hold values from -0.75 to 0.75
- w_qkv: bfloat16 [5120, 3, 2560], P('seq', None, 'mp'), may hold values from -0.5 to 0.5
- w_out: bfloat16 [2560, 64], P('mp'), may hold values from -0.5 to 0.5
- momentum: float32 [2560, 2, 3, 2560], P('seq', 'role', None, 'mp'), may hold values from -3 to 3
- rewards: float32 [32], replicated, may hold values from 0 to 1
- group_ids: int32 [32], replicated, may hold values from 0 to 3
- timestep: int32 [1], replicated, may hold values from 10 to 40
Outputs:
- new_momentum: float32 [2560, 2, 3, 2560], P('seq', 'role', None, 'mp')
- new_w_qkv: bfloat16 [5120, 3, 2560], P('seq', None, 'mp')
The draws below stay inside these ranges and needn't reach their ends.
All inputs are finite; a program needn't handle non-finite values.
Results may differ from the reference program's by a relative error of at most 0.0075.
Values may be sent and summed in bfloat16 or wider, within the bound.
No kernel may reach another device: no remote copies, remote signals or barrier semaphores. Data moves between devices by JAX's collectives and lax.ppermute only.
A program may use at most 128 MiB of HBM per device.

```python
import jax
import jax.numpy as jnp
from jax import lax

D = 5120
H = 20
HD = 128
CH = 64
TILE = 192
TOK_DEV = 384
STEPS = 50
ROLLOUTS = 32
GROUPS = 4
TOKENS = 1536
N_SEQ = 4


def draw_w_qkv(key, part):
    own_key = jax.random.fold_in(key, 17)
    base_key = jax.random.fold_in(own_key, 0)
    columns_all = H * HD
    entries = jnp.clip(jax.random.normal(base_key, (D, 3, columns_all), jnp.float32), -6.0, 6.0)
    return jnp.clip(entries * D ** (-0.5), -0.5, 0.5).astype(jnp.bfloat16)


def draw_w_out(key, part):
    own_key = jax.random.fold_in(key, 29)
    head_place = jnp.arange(H, dtype=jnp.float32) / max(H - 1, 1)
    entries = jnp.clip(jax.random.normal(own_key, (H * HD, CH), jnp.float32), -6.0, 6.0)
    head_scale = 0.5 + 1.5 * head_place
    row_scale = jnp.repeat(head_scale, HD)
    return jnp.clip(entries * row_scale[:, None] * (H * HD) ** (-0.5), -0.5, 0.5).astype(jnp.bfloat16)


def draw_rollout(key, part):
    own_key = jax.random.fold_in(key, 41)
    now_key, noise_key = jax.random.split(own_key, 2)
    now_rows = jnp.clip(jax.random.normal(now_key, (TOKENS, CH), jnp.float32), -6.0, 6.0)
    noise = jnp.clip(jax.random.normal(noise_key, (TOKENS, CH), jnp.float32), -6.0, 6.0)
    next_rows = now_rows + 0.01 * noise
    return jnp.stack([now_rows, next_rows], axis=0).astype(jnp.bfloat16)


def set_ends(values, key, low, largest):
    index_at = [jax.random.randint(jax.random.fold_in(key, axis), (), 0, length) for axis, length in enumerate(values.shape)]
    main_axis = values.shape.index(max(values.shape))
    next_to = index_at[:main_axis] + [(index_at[main_axis] + 1) % values.shape[main_axis]] + index_at[main_axis + 1:]
    return values.at[tuple(index_at)].set(low).at[tuple(next_to)].set(largest)


def shard_levels(key, shape, cuts, smallest, high):
    loudness = 1.0
    for position, parts in cuts:
        draws = jax.random.uniform(jax.random.fold_in(jax.random.fold_in(key, 6), position), (parts,), jnp.float32, smallest / len(cuts), high / len(cuts))
        loudness = loudness * jnp.repeat(jnp.exp(draws), shape[position] // parts).reshape((-1,) + (1,) * (len(shape) - 1 - position))
    return loudness


def normal_values(key, dims, deviation, bound, cuts=(), kind=jnp.bfloat16):
    result = jax.random.normal(key, dims, jnp.float32) * deviation
    if len(cuts) > 0:
        result = shard_levels(key, dims, cuts, -0.22, 0.18) * result
    return jnp.clip(result, min=-bound, max=bound).astype(kind)


def setup_inputs(seed: int = 0) -> dict:
    key_list = jax.random.split(jax.random.key(seed), 9)
    return {
        "rollout": draw_rollout(jax.random.fold_in(key_list[8], 71), 0),
        "w_embed": normal_values(key_list[1], (CH, D), CH ** -0.5, 0.75),
        "w_qkv": draw_w_qkv(jax.random.fold_in(key_list[8], 71), 0),
        "w_out": draw_w_out(jax.random.fold_in(key_list[8], 71), 0),
        "momentum": normal_values(key_list[4], (D // 2, 2, 3, H * HD), 0.5, 3.0, ((0, 4), (1, 2), (3, 4)), jnp.float32),
        "rewards": jnp.clip(jax.random.uniform(key_list[5], (ROLLOUTS,), jnp.float32, 0.0, 1.0), 0.0, 1.0),
        "group_ids": set_ends(jax.random.randint(key_list[6], (ROLLOUTS,), 0, GROUPS), jax.random.fold_in(key_list[6], 1), 0, GROUPS - 1).astype(jnp.int32),
        "timestep": jax.random.randint(key_list[7], (1,), STEPS // 5, 4 * STEPS // 5 + 1).astype(jnp.int32),
    }


SHIFT_FACTOR = 5.0
NOISE_LEVEL = 0.7
MOMENTUM_DECAY = 0.9
LEARNING_RATE = 0.004
LOSS_SCALE = 16384.0
REWARD_FLOOR = 0.1
MASKED = -1e+30

def sigma_at(index, total_steps):
    fraction = index.astype(jnp.float32) / total_steps
    return SHIFT_FACTOR * fraction / (1.0 + (SHIFT_FACTOR - 1.0) * fraction)

def advantage_of(rewards, group_ids):
    members = (group_ids == group_ids[0]).astype(jnp.float32)
    member_total = jnp.sum(members)
    group_mean = jnp.sum(members * rewards) / member_total
    spread = jnp.sqrt(jnp.sum(members * (rewards - group_mean) ** 2) / member_total)
    return (rewards[0] - group_mean) / jnp.maximum(spread, REWARD_FLOOR)

def allowed_keys(seq_index, tok_dev, seq_count):
    tiles_dev = tok_dev // TILE
    query_tile = jnp.arange(tok_dev, dtype=jnp.int32) // TILE
    key_tile = jnp.arange(tok_dev + 2 * TILE, dtype=jnp.int32) // TILE
    in_band = (key_tile[None, :] >= query_tile[:, None]) & (key_tile[None, :] <= query_tile[:, None] + 2)
    global_tile = seq_index * tiles_dev - 1 + key_tile
    inside = (global_tile >= 0) & (global_tile < seq_count * tiles_dev)
    return in_band & inside[None, :]

def rounded(values):
    return lax.optimization_barrier(values.astype(jnp.bfloat16)).astype(jnp.float32)

def reference(rollout, w_embed, w_qkv, w_out, momentum, rewards, group_ids, timestep):
    latent_now = rollout[0]
    latent_next = rollout[1]
    width = H * HD
    extent = TOK_DEV + 2 * TILE
    scale = HD ** (-0.5)
    embedded = jnp.dot(latent_now, w_embed, preferred_element_type=jnp.float32).astype(jnp.bfloat16)
    projected = jnp.einsum('td,dmc->tmc', embedded.astype(jnp.float32), w_qkv.astype(jnp.float32)).astype(jnp.bfloat16)
    padded = jnp.pad(projected[:, 1:3], ((TILE, TILE), (0, 0), (0, 0)))
    advantage = advantage_of(rewards, group_ids)
    sigma_now = sigma_at(timestep[0], STEPS)
    step_size = sigma_at(timestep[0] - 1, STEPS) - sigma_now
    coefficient = advantage * LOSS_SCALE * (1.0 - sigma_now) / (NOISE_LEVEL ** 2 * sigma_now * TOKENS)

    def shard_pass(seq_index):
        first = (seq_index * TOK_DEV).astype(jnp.int32)
        queries = lax.dynamic_slice_in_dim(projected[:, 0], first, TOK_DEV, 0).reshape(TOK_DEV, H, HD).astype(jnp.float32)
        nearby = lax.dynamic_slice_in_dim(padded, first, extent, 0)
        keys_near = nearby[:, 0].reshape(extent, H, HD).astype(jnp.float32)
        values_near = nearby[:, 1].reshape(extent, H, HD).astype(jnp.float32)
        now_block = lax.dynamic_slice_in_dim(latent_now, first, TOK_DEV, 0).astype(jnp.float32)
        next_block = lax.dynamic_slice_in_dim(latent_next, first, TOK_DEV, 0).astype(jnp.float32)
        allowed = allowed_keys(seq_index, TOK_DEV, N_SEQ)
        scores = jnp.einsum('thd,ehd->hte', queries, keys_near) * scale
        scores = jnp.where(allowed[None], scores, MASKED)
        highest = lax.optimization_barrier(jnp.max(scores, axis=2, keepdims=True))
        weights = jnp.exp(scores - highest)
        probs = weights / lax.optimization_barrier(jnp.sum(weights, axis=2, keepdims=True))
        probs_low = rounded(probs)
        attended = jnp.einsum('hte,ehd->thd', probs_low, values_near).astype(jnp.bfloat16).reshape(TOK_DEV, width)
        prediction = jnp.dot(attended, w_out, preferred_element_type=jnp.float32)
        step_mean = now_block + step_size * prediction
        pred_grad = (coefficient * (next_block - step_mean)).astype(jnp.bfloat16)
        attended_grad = rounded(jnp.dot(pred_grad, w_out.T, preferred_element_type=jnp.float32)).reshape(TOK_DEV, H, HD)
        prob_grad = jnp.einsum('thd,ehd->hte', attended_grad, values_near)
        row_dot = lax.optimization_barrier(jnp.sum(probs * prob_grad, axis=2, keepdims=True))
        score_grad = rounded(probs * (prob_grad - row_dot) * scale)
        query_grad = jnp.einsum('hte,ehd->thd', score_grad, keys_near).reshape(TOK_DEV, width)
        key_grad = jnp.einsum('hte,thd->ehd', score_grad, queries).reshape(extent, width)
        value_grad = jnp.einsum('hte,thd->ehd', probs_low, attended_grad).reshape(extent, width)
        return (query_grad, jnp.stack([key_grad, value_grad], axis=1))
    query_grads, near_grads = lax.map(shard_pass, jnp.arange(N_SEQ, dtype=jnp.int32))
    left_rims = rounded(near_grads[:, :TILE])
    right_rims = rounded(near_grads[:, extent - TILE:])
    from_left = jnp.concatenate([jnp.zeros_like(right_rims[:1]), right_rims[:-1]], axis=0)
    from_right = jnp.concatenate([left_rims[1:], jnp.zeros_like(left_rims[:1])], axis=0)
    owned = near_grads[:, TILE:TILE + TOK_DEV]
    owned = owned + jnp.pad(from_left, ((0, 0), (0, TOK_DEV - TILE), (0, 0), (0, 0)))
    owned = owned + jnp.pad(from_right, ((0, 0), (TOK_DEV - TILE, 0), (0, 0), (0, 0)))
    qkv_grad = jnp.concatenate([query_grads[:, :, None], owned], axis=2).astype(jnp.bfloat16)

    def add_term(total, blocks):
        embedded_block, grad_block = blocks
        weight_term = jnp.einsum('tr,tmc->rmc', embedded_block.astype(jnp.float32), grad_block.astype(jnp.float32))
        return (total + rounded(weight_term), None)
    weight_grad = lax.scan(add_term, jnp.zeros((D, 3, width), jnp.float32), (embedded.reshape(N_SEQ, TOK_DEV, D), qkv_grad))[0]
    paired_grad = weight_grad.reshape(D // 2, 2, 3, width)
    new_momentum = MOMENTUM_DECAY * momentum + paired_grad
    new_w_qkv = (w_qkv.astype(jnp.float32) - LEARNING_RATE * new_momentum.reshape(D, 3, width)).astype(jnp.bfloat16)
    return (new_momentum, new_w_qkv)
```

```python
import functools

import jax
import jax.numpy as jnp
from jax import lax
from jax.experimental import pallas as pl
from jax.experimental.pallas import tpu as pltpu
from jax.sharding import PartitionSpec as P

HD = 128
TILE = 192
STEPS = 50
CH = 64
WINDOW = 640
ONE_LANE = 64
BIAS_LANE = 65
LOW_LANE = 66

SHIFT_FACTOR = 5.0
NOISE_LEVEL = 0.7
MOMENTUM_DECAY = 0.9
LEARNING_RATE = 0.004
LOSS_SCALE = 16384.0
REWARD_FLOOR = 0.1
MASKED = -1e30
LOG2E = 1.4426950408889634

F32 = jnp.float32
BF16 = jnp.bfloat16
NT = (((1,), (1,)), ((), ()))
TN = (((0,), (0,)), ((), ()))
NN = (((1,), (0,)), ((), ()))


def dot(a, b, dims=NN):
    return lax.dot_general(a, b, dims, preferred_element_type=F32)


def sigma_at(index, total_steps):
    fraction = index.astype(F32) / total_steps
    return SHIFT_FACTOR * fraction / (1.0 + (SHIFT_FACTOR - 1.0) * fraction)


def advantage_of(rewards, group_ids):
    members = (group_ids == group_ids[0]).astype(F32)
    member_total = jnp.sum(members)
    group_mean = jnp.sum(members * rewards) / member_total
    spread = jnp.sqrt(jnp.sum(members * (rewards - group_mean) ** 2) / member_total)
    return (rewards[0] - group_mean) / jnp.maximum(spread, REWARD_FLOOR)


def swap(x, axis, bit):
    return lax.ppermute(x, axis, [(i, i ^ bit) for i in range(lax.axis_size(axis))])


def butterfly(x, axis):
    bit = 1
    while bit < lax.axis_size(axis):
        x = (x.astype(F32) + swap(x, axis, bit).astype(F32)).astype(x.dtype)
        bit *= 2
    return x


def fold_kernel(e_ref, w_ref, o_ref):
    o_ref[0] = dot(e_ref[...], w_ref[0]).astype(BF16)


def fold(e_rows, w):
    _, rows, width = w.shape
    return pl.pallas_call(
        fold_kernel,
        grid=(3,),
        in_specs=[
            pl.BlockSpec((CH, rows), lambda m: (0, 0)),
            pl.BlockSpec((1, rows, width), lambda m: (m, 0, 0)),
        ],
        out_specs=pl.BlockSpec((1, CH, width), lambda m: (m, 0, 0)),
        out_shape=jax.ShapeDtypeStruct((3, CH, width), BF16),
        name="fold",
    )(e_rows, w)


def forward_kernel(tiles, heads, win_ref, m_ref, wot_ref, e_ref, u_ref, il_ref, pred_ref, mk_ref, att_ref):
    mk_ref[...] = jnp.zeros_like(mk_ref)
    mk_ref[0:CH, :] = m_ref[1]
    lane = lax.broadcasted_iota(jnp.int32, (TILE, HD), 1)
    unit = jnp.where(lane == BIAS_LANE, 1.0, 0.0)
    factor = LOG2E * HD ** (-0.5)
    for j in range(tiles):
        own = win_ref[j, TILE : 2 * TILE, 0:CH]
        queries = dot(own, m_ref[0]).astype(BF16)
        keys = win_ref[j]
        for h in range(heads):
            cols = slice(h * HD, (h + 1) * HD)
            t = dot(queries[:, cols], mk_ref[:, cols], NT) * factor + unit
            s = dot(t.astype(BF16), keys, NT)
            e = jnp.exp2(s - jnp.max(s, axis=1, keepdims=True)).astype(BF16)
            at = slice((j * heads + h) * TILE, (j * heads + h + 1) * TILE)
            e_ref[at, :] = e
            u = dot(e, keys)
            inv = 1.0 / u[:, ONE_LANE : ONE_LANE + 1]
            u = (u * inv).astype(BF16)
            u_ref[at, :] = u
            il_ref[at, :] = jnp.broadcast_to(inv, (TILE, HD))
            att_ref[j * TILE : (j + 1) * TILE, cols] = dot(u[:, 0:CH], m_ref[2, :, cols]).astype(BF16)
    pred_ref[...] = dot(att_ref[...], wot_ref[...], NT).astype(BF16)


def forward(win, m, wot, tiles, heads):
    rows = tiles * heads * TILE
    width = heads * HD
    vm = pl.BlockSpec(memory_space=pltpu.VMEM)
    return pl.pallas_call(
        functools.partial(forward_kernel, tiles, heads),
        in_specs=[vm] * 3,
        out_specs=[vm] * 4,
        out_shape=[
            jax.ShapeDtypeStruct((rows, WINDOW), BF16),
            jax.ShapeDtypeStruct((rows, HD), BF16),
            jax.ShapeDtypeStruct((rows, HD), F32),
            jax.ShapeDtypeStruct((tiles * TILE, CH), BF16),
        ],
        scratch_shapes=[pltpu.VMEM((HD, width), BF16), pltpu.VMEM((tiles * TILE, width), BF16)],
        compiler_params=pltpu.CompilerParams(vmem_limit_bytes=48 * 1024 * 1024),
        name="attend",
    )(win, m, wot)


def backward_kernel(tiles, heads, *refs):
    (sc_ref, win_ref, m_ref, wot_ref, e_ref, u_ref, il_ref, next_ref) = refs[:8]
    pred_refs = refs[8:-3]
    zy_ref, mv_ref, v_ref = refs[-3:]
    width = heads * HD
    mv_ref[...] = jnp.zeros_like(mv_ref)
    mv_ref[0:CH, :] = m_ref[2]
    lane = lax.broadcasted_iota(jnp.int32, (TILE, HD), 1)
    half_lane = lax.broadcasted_iota(jnp.int32, (CH, HD), 1)
    scale = HD ** (-0.5)
    pred = pred_refs[0][...].astype(F32)
    for ref in pred_refs[1:]:
        pred = pred + ref[...].astype(F32)
    pgs = []
    for j in range(tiles):
        at = slice(j * TILE, (j + 1) * TILE)
        now = win_ref[j, TILE : 2 * TILE, 0:CH].astype(F32)
        step_mean = now + sc_ref[1] * pred[at]
        pg = (sc_ref[0] * (next_ref[at, :].astype(F32) - step_mean)).astype(BF16)
        pgs.append(pg)
        ag = dot(pg, wot_ref[...]).astype(BF16)
        keys = win_ref[j]
        for h in range(heads):
            cols = slice(h * HD, (h + 1) * HD)
            rows = slice((j * heads + h) * TILE, (j * heads + h + 1) * TILE)
            w = dot(ag[:, cols], mv_ref[:, cols], NT).astype(BF16).astype(F32)
            u = u_ref[rows, :].astype(F32)
            row_dot = jnp.sum(w * u, axis=1, keepdims=True)
            factor = scale * il_ref[rows, :]
            w = w * factor
            row_dot = row_dot * factor
            high = row_dot.astype(BF16).astype(F32)
            low = row_dot - high
            w = jnp.where(lane == ONE_LANE, -high, jnp.where(lane == LOW_LANE, -low, w))
            x = dot(w.astype(BF16), keys, NT)
            ds = (e_ref[rows, :].astype(F32) * x).astype(BF16)
            v_ref[h, at, :] = dot(ds, keys).astype(BF16)
    pg_all = jnp.concatenate(pgs, axis=0)
    pg_all = jnp.concatenate([jnp.zeros_like(pg_all), pg_all], axis=1)
    own = jnp.concatenate([win_ref[j, TILE : 2 * TILE, 0:CH] for j in range(tiles)], axis=0)
    for h in range(heads):
        z = dot(own, v_ref[h], TN)
        u = jnp.concatenate(
            [u_ref[(j * heads + h) * TILE : (j * heads + h + 1) * TILE, 0:CH] for j in range(tiles)], axis=0
        )
        y = dot(u, pg_all, TN)
        zy_ref[h * CH : (h + 1) * CH, :] = jnp.where(half_lane < CH, z, y).astype(BF16)


def backward(scalars, win, m, wot, e, u, il, latent_next, preds, tiles, heads):
    vm = pl.BlockSpec(memory_space=pltpu.VMEM)
    width = heads * HD
    return pl.pallas_call(
        functools.partial(backward_kernel, tiles, heads),
        in_specs=[pl.BlockSpec(memory_space=pltpu.SMEM)] + [vm] * (7 + len(preds)),
        out_specs=vm,
        out_shape=jax.ShapeDtypeStruct((heads * CH, HD), BF16),
        scratch_shapes=[pltpu.VMEM((HD, width), BF16), pltpu.VMEM((heads, tiles * TILE, HD), BF16)],
        compiler_params=pltpu.CompilerParams(vmem_limit_bytes=48 * 1024 * 1024),
        name="attend_grad",
    )(scalars, win, m, wot, e, u, il, latent_next, *preds)


def update_kernel(heads, steps, pairs, aliased, *refs):
    role_ref, zy_ref, m_ref, wot_ref, et_ref, mom_ref, w_ref = refs[:7]
    recv_refs = refs[7 : 7 + steps]
    onm_ref, ow_ref, g_ref, gs_ref, rs_ref, fs_ref = refs[7 + steps + aliased :]
    width = heads * HD
    lanes = width // HD
    stride = 3 * lanes
    step = pl.program_id(0)
    role = role_ref[0]

    @pl.when(step == 0)
    def _():
        for h in range(heads):
            cols = slice(h * HD, (h + 1) * HD)
            zy = zy_ref[h * CH : (h + 1) * CH, :]
            z = zy[:, 0:CH]
            y = zy[:, CH : 2 * CH]
            g_ref[0, :, cols] = dot(z, m_ref[1, :, cols]).astype(BF16)
            g_ref[1, :, cols] = dot(z, m_ref[0, :, cols], TN).astype(BF16)
            g_ref[2, :, cols] = dot(y, wot_ref[:, cols]).astype(BF16)

    for s in range(steps):

        @pl.when(step == s)
        def _():
            rs_ref[...] = recv_refs[s][...].astype(F32)

    for part in range(3):
        g = dot(et_ref[...], g_ref[part])
        for b in range(lanes):
            cols = slice(b * HD, (b + 1) * HD)
            at = pl.ds(part * lanes + b, pairs, stride=stride)
            gs_ref[...] = g[:, cols]
            own = MOMENTUM_DECAY * mom_ref[at, :] + gs_ref[pl.ds(role, pairs, stride=2), :]
            other = MOMENTUM_DECAY * rs_ref[at, :] + gs_ref[pl.ds(1 - role, pairs, stride=2), :]
            onm_ref[at, :] = own
            fs_ref[pl.ds(role, pairs, stride=2), :] = own
            fs_ref[pl.ds(1 - role, pairs, stride=2), :] = other
            ow_ref[part, :, cols] = (w_ref[part, :, cols].astype(F32) - LEARNING_RATE * fs_ref[...]).astype(BF16)


def update(role, zy, m, wot, et, mom, w, received, first, pairs, before, heads):
    steps = len(received)
    width = heads * HD
    lin = pairs * 3 * heads
    any_space = pl.BlockSpec(memory_space=pl.ANY)
    whole = lambda a: pl.BlockSpec(a.shape, lambda i: (0,) * a.ndim)
    args = [role, zy, m, wot, et, mom, w, *received, *before]
    return pl.pallas_call(
        functools.partial(update_kernel, heads, steps, pairs, len(before)),
        grid=(steps,),
        in_specs=[
            pl.BlockSpec(memory_space=pltpu.SMEM),
            whole(zy),
            whole(m),
            whole(wot),
            pl.BlockSpec((2 * pairs, CH), lambda i: (first + i, 0)),
            pl.BlockSpec((lin, HD), lambda i: (first + i, 0)),
            pl.BlockSpec((3, 2 * pairs, width), lambda i: (0, first + i, 0)),
        ]
        + [whole(a) for a in received]
        + [any_space] * len(before),
        out_specs=[
            pl.BlockSpec((lin, HD), lambda i: (first + i, 0)),
            pl.BlockSpec((3, 2 * pairs, width), lambda i: (0, first + i, 0)),
        ],
        out_shape=[jax.ShapeDtypeStruct(mom.shape, F32), jax.ShapeDtypeStruct(w.shape, BF16)],
        input_output_aliases={7 + steps + k: k for k in range(len(before))},
        scratch_shapes=[
            pltpu.VMEM((3, CH, width), BF16),
            pltpu.VMEM((2 * pairs, HD), F32),
            pltpu.VMEM((lin, HD), F32),
            pltpu.VMEM((2 * pairs, HD), F32),
        ],
        compiler_params=pltpu.CompilerParams(vmem_limit_bytes=48 * 1024 * 1024),
        name="update",
    )(*args)


def body(rollout, w_embed, w_qkv, w_out, momentum, rewards, group_ids, timestep):
    seq_count = lax.axis_size("seq")
    seq_index = lax.axis_index("seq")
    role_index = lax.axis_index("role")
    rows_dev = w_qkv.shape[0]
    width = w_qkv.shape[2]
    heads = width // HD
    tok_dev = rollout.shape[1]
    tiles = tok_dev // TILE
    pair_rows = rows_dev // 2

    mine = rollout[0]
    other = lax.ppermute(mine, "role", [(0, 1), (1, 0)])
    latent_now = jnp.where(role_index == 0, mine, other)
    latent_next = jnp.where(role_index == 0, other, mine)

    mom = momentum.reshape(pair_rows * 3 * heads, HD)
    chunks = 5
    pairs = pair_rows // chunks
    lin = pairs * 3 * heads
    received = []
    for c in range(chunks):
        piece = lax.slice_in_dim(mom, c * lin, (c + 1) * lin, axis=0).astype(BF16)
        received.append(lax.ppermute(piece, "role", [(0, 1), (1, 0)]))

    e_rows = lax.dynamic_slice_in_dim(w_embed, seq_index * rows_dev, rows_dev, axis=1)
    w = w_qkv.transpose(1, 0, 2)
    m = butterfly(fold(e_rows, w), "seq")

    left = lax.ppermute(latent_now[tok_dev - TILE :], "seq", [(i, i + 1) for i in range(seq_count - 1)])
    right = lax.ppermute(latent_now[:TILE], "seq", [(i + 1, i) for i in range(seq_count - 1)])
    near = jnp.concatenate([left, latent_now, right, jnp.zeros((WINDOW - 3 * TILE, CH), BF16)], axis=0)
    key_tile = jnp.arange(near.shape[0], dtype=jnp.int32) // TILE + seq_index * tiles - 1
    inside = (key_tile >= 0) & (key_tile < seq_count * tiles)
    windows = []
    for j in range(tiles):
        seen = inside[j * TILE : j * TILE + WINDOW] & (jnp.arange(WINDOW) < 3 * TILE)
        bias = jnp.where(seen, 0.0, MASKED).astype(BF16)[:, None]
        ones = jnp.ones((WINDOW, 1), BF16)
        rest = jnp.zeros((WINDOW, HD - LOW_LANE - 1), BF16)
        windows.append(jnp.concatenate([near[j * TILE : j * TILE + WINDOW], ones, bias, ones, rest], axis=1))
    win = jnp.stack(windows)

    advantage = advantage_of(rewards, group_ids)
    sigma_now = sigma_at(timestep[0], STEPS)
    step_size = sigma_at(timestep[0] - 1, STEPS) - sigma_now
    tokens_all = tok_dev * seq_count
    coefficient = advantage * LOSS_SCALE * (1.0 - sigma_now) / (NOISE_LEVEL**2 * sigma_now * tokens_all)
    scalars = jnp.stack([coefficient, step_size])

    wot = w_out.T
    e, u, il, partial_pred = forward(win, m, wot, tiles, heads)
    mp_count = lax.axis_size("mp")
    preds = [partial_pred] + [
        lax.ppermute(partial_pred, "mp", [(i, (i + d) % mp_count) for i in range(mp_count)])
        for d in range(1, mp_count)
    ]
    zy = backward(scalars, win, m, wot, e, u, il, latent_next, preds, tiles, heads)
    zy = butterfly(zy, "seq")

    et = e_rows.T
    role = role_index[None]
    first = update(role, zy, m, wot, et, mom, w, received[:-1], 0, pairs, [], heads)
    nm, nw = update(role, zy, m, wot, et, mom, w, received[-1:], chunks - 1, pairs, first, heads)
    return nm.reshape(momentum.shape), nw.transpose(1, 0, 2)


def solution(mesh):
    in_specs = (
        P("role", "seq", None),
        P(),
        P("seq", None, "mp"),
        P("mp", None),
        P("seq", "role", None, "mp"),
        P(),
        P(),
        P(),
    )
    out_specs = (P("seq", "role", None, "mp"), P("seq", None, "mp"))
    return jax.shard_map(body, mesh=mesh, in_specs=in_specs, out_specs=out_specs, check_vma=False)
```

```python
import functools

import jax
import jax.numpy as jnp
from jax import lax
from jax.experimental import pallas as pl
from jax.experimental.pallas import tpu as pltpu
from jax.sharding import PartitionSpec as P

HD = 128
TILE = 192
STEPS = 50
CH = 64
WINDOW = 640
ONE_LANE = 64
BIAS_LANE = 65
LOW_LANE = 66

SHIFT_FACTOR = 5.0
NOISE_LEVEL = 0.7
MOMENTUM_DECAY = 0.9
LEARNING_RATE = 0.004
LOSS_SCALE = 16384.0
REWARD_FLOOR = 0.1
MASKED = -1e30
LOG2E = 1.4426950408889634

F32 = jnp.float32
BF16 = jnp.bfloat16
NT = (((1,), (1,)), ((), ()))
TN = (((0,), (0,)), ((), ()))
NN = (((1,), (0,)), ((), ()))


def dot(a, b, dims=NN):
    return lax.dot_general(a, b, dims, preferred_element_type=F32)


def sigma_at(index, total_steps):
    fraction = index.astype(F32) / total_steps
    return SHIFT_FACTOR * fraction / (1.0 + (SHIFT_FACTOR - 1.0) * fraction)


def advantage_of(rewards, group_ids):
    members = (group_ids == group_ids[:, 0:1]).astype(F32)
    member_total = jnp.sum(members, axis=1, keepdims=True)
    group_mean = jnp.sum(members * rewards, axis=1, keepdims=True) / member_total
    spread = jnp.sqrt(jnp.sum(members * (rewards - group_mean) ** 2, axis=1, keepdims=True) / member_total)
    return (rewards[:, 0:1] - group_mean) / jnp.maximum(spread, REWARD_FLOOR)


def swap(x, axis, bit):
    return lax.ppermute(x, axis, [(i, i ^ bit) for i in range(lax.axis_size(axis))])


def butterfly(x, axis):
    bit = 1
    while bit < lax.axis_size(axis):
        x = (x.astype(F32) + swap(x, axis, bit).astype(F32)).astype(x.dtype)
        bit *= 2
    return x


def fold_kernel(at_ref, e_ref, w_ref, o_ref, et_ref):
    o_ref[0] = dot(e_ref[...], w_ref[0]).astype(BF16)

    @pl.when(pl.program_id(0) == 0)
    def _():
        et_ref[...] = e_ref[...].astype(F32).T.astype(BF16)


def fold(seq, w_embed, w):
    _, rows, width = w.shape
    return pl.pallas_call(
        fold_kernel,
        grid_spec=pltpu.PrefetchScalarGridSpec(
            num_scalar_prefetch=1,
            grid=(3,),
            in_specs=[
                pl.BlockSpec((CH, rows), lambda m, at: (0, at[0])),
                pl.BlockSpec((1, rows, width), lambda m, at: (m, 0, 0)),
            ],
            out_specs=[
                pl.BlockSpec((1, CH, width), lambda m, at: (m, 0, 0)),
                pl.BlockSpec((rows, CH), lambda m, at: (0, 0)),
            ],
        ),
        out_shape=[jax.ShapeDtypeStruct((3, CH, width), BF16), jax.ShapeDtypeStruct((rows, CH), BF16)],
        name="fold",
    )(seq, w_embed, w)


def narrow_kernel(sizes, stride, unit, mom_ref, *out_refs):
    step = pl.program_id(0)
    start = 0
    for size, ref in zip(sizes, out_refs):

        @pl.when((step >= start) & (step < start + size))
        def _():
            for q in range(stride):
                ref[0, q] = (MOMENTUM_DECAY * mom_ref[pl.ds(q, unit, stride=stride), :]).astype(BF16)

        start += size


def narrow(mom, first, sizes, stride, unit):
    starts = [sum(sizes[:k]) for k in range(len(sizes))]
    return pl.pallas_call(
        functools.partial(narrow_kernel, sizes, stride, unit),
        grid=(sum(sizes),),
        in_specs=[pl.BlockSpec((unit * stride, HD), lambda i: (first + i, 0))],
        out_specs=[
            pl.BlockSpec((1, stride, unit, HD), lambda i, a=a, n=n: (jnp.clip(i - a, 0, n - 1), 0, 0, 0))
            for a, n in zip(starts, sizes)
        ],
        out_shape=[jax.ShapeDtypeStruct((n, stride, unit, HD), BF16) for n in sizes],
        name="narrow",
    )(mom)


def forward_kernel(tiles, heads, win_ref, m_ref, wot_ref, e_ref, u_ref, il_ref, pred_ref, mk_ref, att_ref):
    mk_ref[...] = jnp.zeros_like(mk_ref)
    mk_ref[0:CH, :] = m_ref[1]
    lane = lax.broadcasted_iota(jnp.int32, (TILE, HD), 1)
    unit = jnp.where(lane == BIAS_LANE, 1.0, 0.0)
    factor = LOG2E * HD ** (-0.5)
    for j in range(tiles):
        own = win_ref[j, TILE : 2 * TILE, 0:CH]
        queries = dot(own, m_ref[0]).astype(BF16)
        keys = win_ref[j]
        for h in range(heads):
            cols = slice(h * HD, (h + 1) * HD)
            t = dot(queries[:, cols], mk_ref[:, cols], NT) * factor + unit
            s = dot(t.astype(BF16), keys, NT)
            e = jnp.exp2(s - jnp.max(s, axis=1, keepdims=True)).astype(BF16)
            at = slice((j * heads + h) * TILE, (j * heads + h + 1) * TILE)
            e_ref[at, :] = e
            u = dot(e, keys)
            inv = 1.0 / u[:, ONE_LANE : ONE_LANE + 1]
            u = (u * inv).astype(BF16)
            u_ref[at, :] = u
            il_ref[at, :] = jnp.broadcast_to(inv, (TILE, HD))
            att_ref[j * TILE : (j + 1) * TILE, cols] = dot(u[:, 0:CH], m_ref[2, :, cols]).astype(BF16)
    pred_ref[...] = dot(att_ref[...], wot_ref[...], NT).astype(BF16)


def forward(win, m, wot, tiles, heads):
    rows = tiles * heads * TILE
    width = heads * HD
    vm = pl.BlockSpec(memory_space=pltpu.VMEM)
    return pl.pallas_call(
        functools.partial(forward_kernel, tiles, heads),
        in_specs=[vm] * 3,
        out_specs=[vm] * 4,
        out_shape=[
            jax.ShapeDtypeStruct((rows, WINDOW), BF16),
            jax.ShapeDtypeStruct((rows, HD), BF16),
            jax.ShapeDtypeStruct((rows, HD), F32),
            jax.ShapeDtypeStruct((tiles * TILE, CH), BF16),
        ],
        scratch_shapes=[pltpu.VMEM((HD, width), BF16), pltpu.VMEM((tiles * TILE, width), BF16)],
        compiler_params=pltpu.CompilerParams(vmem_limit_bytes=48 * 1024 * 1024),
        name="attend",
    )(win, m, wot)


def backward_kernel(tiles, heads, tokens_all, *refs):
    (time_ref, rewards_ref, groups_ref, win_ref, m_ref, wot_ref, e_ref, u_ref, il_ref, next_ref) = refs[:10]
    pred_refs = refs[10:-3]
    zy_ref, mv_ref, v_ref = refs[-3:]
    width = heads * HD
    mv_ref[...] = jnp.zeros_like(mv_ref)
    mv_ref[0:CH, :] = m_ref[2]
    lane = lax.broadcasted_iota(jnp.int32, (TILE, HD), 1)
    half_lane = lax.broadcasted_iota(jnp.int32, (CH, HD), 1)
    scale = HD ** (-0.5)
    advantage = advantage_of(rewards_ref[...], groups_ref[...])
    index = jnp.full((1, 1), time_ref[0], jnp.int32)
    sigma_now = sigma_at(index, STEPS)
    step_size = sigma_at(index - 1, STEPS) - sigma_now
    coefficient = advantage * LOSS_SCALE * (1.0 - sigma_now) / (NOISE_LEVEL**2 * sigma_now * tokens_all)
    pred = pred_refs[0][...].astype(F32)
    for ref in pred_refs[1:]:
        pred = pred + ref[...].astype(F32)
    pgs = []
    for j in range(tiles):
        at = slice(j * TILE, (j + 1) * TILE)
        now = win_ref[j, TILE : 2 * TILE, 0:CH].astype(F32)
        step_mean = now + step_size * pred[at]
        pg = (coefficient * (next_ref[at, :].astype(F32) - step_mean)).astype(BF16)
        pgs.append(pg)
        ag = dot(pg, wot_ref[...]).astype(BF16)
        keys = win_ref[j]
        for h in range(heads):
            cols = slice(h * HD, (h + 1) * HD)
            rows = slice((j * heads + h) * TILE, (j * heads + h + 1) * TILE)
            w = dot(ag[:, cols], mv_ref[:, cols], NT).astype(BF16).astype(F32)
            u = u_ref[rows, :].astype(F32)
            row_dot = jnp.sum(w * u, axis=1, keepdims=True)
            factor = scale * il_ref[rows, :]
            w = w * factor
            row_dot = row_dot * factor
            high = row_dot.astype(BF16).astype(F32)
            low = row_dot - high
            w = jnp.where(lane == ONE_LANE, -high, jnp.where(lane == LOW_LANE, -low, w))
            x = dot(w.astype(BF16), keys, NT)
            ds = (e_ref[rows, :].astype(F32) * x).astype(BF16)
            v_ref[h, at, :] = dot(ds, keys).astype(BF16)
    pg_all = jnp.concatenate(pgs, axis=0)
    pg_all = jnp.concatenate([jnp.zeros_like(pg_all), pg_all], axis=1)
    own = jnp.concatenate([win_ref[j, TILE : 2 * TILE, 0:CH] for j in range(tiles)], axis=0)
    for h in range(heads):
        z = dot(own, v_ref[h], TN)
        u = jnp.concatenate(
            [u_ref[(j * heads + h) * TILE : (j * heads + h + 1) * TILE, 0:CH] for j in range(tiles)], axis=0
        )
        y = dot(u, pg_all, TN)
        zy_ref[h * CH : (h + 1) * CH, :] = jnp.where(half_lane < CH, z, y).astype(BF16)


def backward(timestep, rewards, group_ids, win, m, wot, e, u, il, latent_next, preds, tiles, heads, tokens_all):
    vm = pl.BlockSpec(memory_space=pltpu.VMEM)
    width = heads * HD
    return pl.pallas_call(
        functools.partial(backward_kernel, tiles, heads, tokens_all),
        in_specs=[pl.BlockSpec(memory_space=pltpu.SMEM)] + [vm] * (9 + len(preds)),
        out_specs=vm,
        out_shape=jax.ShapeDtypeStruct((heads * CH, HD), BF16),
        scratch_shapes=[pltpu.VMEM((HD, width), BF16), pltpu.VMEM((heads, tiles * TILE, HD), BF16)],
        compiler_params=pltpu.CompilerParams(vmem_limit_bytes=48 * 1024 * 1024),
        name="attend_grad",
    )(timestep, rewards, group_ids, win, m, wot, e, u, il, latent_next, *preds)


def update_kernel(heads, sizes, unit, later, *refs):
    role_ref, et_ref, mom_ref, w_ref = refs[:4]
    recv_refs = refs[4 : 4 + len(sizes)]
    rest = refs[4 + len(sizes) :]
    if later:
        g_ref = rest[0]
        onm_ref, ow_ref, gs_ref, fs_ref = rest[3:]
    else:
        zy_ref, m_ref, wot_ref, onm_ref, ow_ref, g_ref, gs_ref, fs_ref = rest
    width = heads * HD
    stride = 3 * heads
    step = pl.program_id(0)
    role = role_ref[0]

    if not later:

        @pl.when(step == 0)
        def _():
            for h in range(heads):
                cols = slice(h * HD, (h + 1) * HD)
                zy = zy_ref[h * CH : (h + 1) * CH, :]
                z = zy[:, 0:CH]
                y = zy[:, CH : 2 * CH]
                g_ref[0, :, cols] = dot(z, m_ref[1, :, cols]).astype(BF16)
                g_ref[1, :, cols] = dot(z, m_ref[0, :, cols], TN).astype(BF16)
                g_ref[2, :, cols] = dot(y, wot_ref[:, cols]).astype(BF16)

    def run(recv_ref):
        for part in range(3):
            g = dot(et_ref[...], g_ref[part])
            for b in range(heads):
                cols = slice(b * HD, (b + 1) * HD)
                at = pl.ds(part * heads + b, unit, stride=stride)
                gs_ref[...] = g[:, cols]
                own = MOMENTUM_DECAY * mom_ref[at, :] + gs_ref[pl.ds(role, unit, stride=2), :]
                other = recv_ref[0, part * heads + b].astype(F32) + gs_ref[pl.ds(1 - role, unit, stride=2), :]
                onm_ref[at, :] = own
                fs_ref[pl.ds(role, unit, stride=2), :] = own
                fs_ref[pl.ds(1 - role, unit, stride=2), :] = other
                ow_ref[part, :, cols] = (w_ref[part, :, cols].astype(F32) - LEARNING_RATE * fs_ref[...]).astype(BF16)

    start = 0
    for size, ref in zip(sizes, recv_refs):

        @pl.when((step >= start) & (step < start + size))
        def _():
            run(ref)

        start += size


def update(role, et, mom, w, received, first, unit, heads, sources=None, before=None):
    sizes = [a.shape[0] for a in received]
    starts = [sum(sizes[:k]) for k in range(len(sizes))]
    width = heads * HD
    stride = 3 * heads
    any_space = pl.BlockSpec(memory_space=pl.ANY)
    whole = lambda a: pl.BlockSpec(a.shape, lambda i: (0,) * a.ndim)
    args = [role, et, mom, w, *received]
    in_specs = [
        pl.BlockSpec(memory_space=pltpu.SMEM),
        pl.BlockSpec((2 * unit, CH), lambda i: (first + i, 0)),
        pl.BlockSpec((unit * stride, HD), lambda i: (first + i, 0)),
        pl.BlockSpec((3, 2 * unit, width), lambda i: (0, first + i, 0)),
    ] + [
        pl.BlockSpec((1, stride, unit, HD), lambda i, a=a, n=n: (jnp.clip(i - a, 0, n - 1), 0, 0, 0))
        for a, n in zip(starts, sizes)
    ]
    out_specs = [
        pl.BlockSpec((unit * stride, HD), lambda i: (first + i, 0)),
        pl.BlockSpec((3, 2 * unit, width), lambda i: (0, first + i, 0)),
    ]
    out_shape = [jax.ShapeDtypeStruct(mom.shape, F32), jax.ShapeDtypeStruct(w.shape, BF16)]
    aliases = {}
    if before is None:
        args += sources
        in_specs += [whole(a) for a in sources]
        g_shape = (3, CH, width)
        out_specs.append(pl.BlockSpec(g_shape, lambda i: (0, 0, 0)))
        out_shape.append(jax.ShapeDtypeStruct(g_shape, BF16))
    else:
        new_mom, new_w, g = before
        aliases = {len(args) + 1: 0, len(args) + 2: 1}
        args += [g, new_mom, new_w]
        in_specs += [whole(g), any_space, any_space]
    return pl.pallas_call(
        functools.partial(update_kernel, heads, sizes, unit, before is not None),
        grid=(sum(sizes),),
        in_specs=in_specs,
        out_specs=out_specs,
        out_shape=out_shape,
        input_output_aliases=aliases,
        scratch_shapes=[pltpu.VMEM((2 * unit, HD), F32), pltpu.VMEM((2 * unit, HD), F32)],
        compiler_params=pltpu.CompilerParams(vmem_limit_bytes=48 * 1024 * 1024),
        name="update",
    )(*args)


def exchange(x):
    return lax.ppermute(x, "role", [(0, 1), (1, 0)])


def body(rollout, w_embed, w_qkv, w_out, momentum, rewards, group_ids, timestep):
    seq_count = lax.axis_size("seq")
    seq_index = lax.axis_index("seq")
    role_index = lax.axis_index("role")
    rows_dev = w_qkv.shape[0]
    width = w_qkv.shape[2]
    heads = width // HD
    tok_dev = rollout.shape[1]
    tiles = tok_dev // TILE
    pair_rows = rows_dev // 2

    mine = rollout[0]
    other = exchange(mine)
    latent_now = jnp.where(role_index == 0, mine, other)
    latent_next = jnp.where(role_index == 0, other, mine)

    stride = 3 * heads
    mom = momentum.reshape(pair_rows * stride, HD)
    unit = pair_rows // 10
    w = w_qkv.transpose(1, 0, 2)
    (piece,) = narrow(mom, 0, (3,), stride, unit)
    w_embed, piece = lax.optimization_barrier((w_embed, piece))
    received = [exchange(piece)]
    if rows_dev % HD == 0:
        m, et = fold(seq_index[None], w_embed, w)
    else:
        m, et = fold(
            jnp.zeros((1,), jnp.int32), lax.dynamic_slice_in_dim(w_embed, seq_index * rows_dev, rows_dev, axis=1), w
        )
    mom_late, m = lax.optimization_barrier((mom, m))
    pieces = narrow(mom_late, 3, (3, 3, 1), stride, unit)
    received += [exchange(p) for p in pieces]
    m = butterfly(m, "seq")

    left = lax.ppermute(latent_now[tok_dev - TILE :], "seq", [(i, i + 1) for i in range(seq_count - 1)])
    right = lax.ppermute(latent_now[:TILE], "seq", [(i + 1, i) for i in range(seq_count - 1)])
    near = jnp.concatenate([left, latent_now, right, jnp.zeros((WINDOW - 3 * TILE, CH), BF16)], axis=0)
    key_tile = jnp.arange(near.shape[0], dtype=jnp.int32) // TILE + seq_index * tiles - 1
    inside = (key_tile >= 0) & (key_tile < seq_count * tiles)
    windows = []
    for j in range(tiles):
        seen = inside[j * TILE : j * TILE + WINDOW] & (jnp.arange(WINDOW) < 3 * TILE)
        bias = jnp.where(seen, 0.0, MASKED).astype(BF16)[:, None]
        ones = jnp.ones((WINDOW, 1), BF16)
        rest = jnp.zeros((WINDOW, HD - LOW_LANE - 1), BF16)
        windows.append(jnp.concatenate([near[j * TILE : j * TILE + WINDOW], ones, bias, ones, rest], axis=1))
    win = jnp.stack(windows)

    wot = w_out.T
    e, u, il, partial_pred = forward(win, m, wot, tiles, heads)
    mp_count = lax.axis_size("mp")
    preds = [partial_pred] + [
        lax.ppermute(partial_pred, "mp", [(i, (i + d) % mp_count) for i in range(mp_count)])
        for d in range(1, mp_count)
    ]
    zy = backward(
        timestep, rewards[None], group_ids[None], win, m, wot, e, u, il, latent_next, preds, tiles, heads, tok_dev * seq_count
    )
    zy = butterfly(zy, "seq")

    role = role_index[None]
    first = update(role, et, mom, w, received[:-1], 0, unit, heads, sources=[zy, m, wot])
    nm, nw = update(role, et, mom, w, received[-1:], 9, unit, heads, before=first)
    return nm.reshape(momentum.shape), nw.transpose(1, 0, 2)


def solution(mesh):
    in_specs = (
        P("role", "seq", None),
        P(),
        P("seq", None, "mp"),
        P("mp", None),
        P("seq", "role", None, "mp"),
        P(),
        P(),
        P(),
    )
    out_specs = (P("seq", "role", None, "mp"), P("seq", None, "mp"))
    return jax.shard_map(body, mesh=mesh, in_specs=in_specs, out_specs=out_specs, check_vma=False)
```

```python
import functools

import jax
import jax.numpy as jnp
from jax import lax
from jax.experimental import pallas as pl
from jax.experimental.pallas import tpu as pltpu
from jax.sharding import PartitionSpec as P

HD = 128
TILE = 192
STEPS = 50
CH = 64
WINDOW = 640
ONE_LANE = 64
BIAS_LANE = 65
LOW_LANE = 66

SHIFT_FACTOR = 5.0
NOISE_LEVEL = 0.7
MOMENTUM_DECAY = 0.9
LEARNING_RATE = 0.004
LOSS_SCALE = 16384.0
REWARD_FLOOR = 0.1
MASKED = -1e30
LOG2E = 1.4426950408889634

F32 = jnp.float32
BF16 = jnp.bfloat16
NT = (((1,), (1,)), ((), ()))
TN = (((0,), (0,)), ((), ()))
NN = (((1,), (0,)), ((), ()))


VMEM = pl.BlockSpec(memory_space=pltpu.VMEM)
SMEM = pl.BlockSpec(memory_space=pltpu.SMEM)
HBM = pl.BlockSpec(memory_space=pltpu.HBM)
MIB = 1024 * 1024


def in_hbm(x):
    return pltpu.with_memory_space_constraint(x, pltpu.HBM)


def in_vmem(x):
    return pltpu.with_memory_space_constraint(x, pltpu.VMEM)


def params(mib):
    return pltpu.CompilerParams(vmem_limit_bytes=mib * MIB)


def dot(a, b, dims=NN):
    return lax.dot_general(a, b, dims, preferred_element_type=F32)


def sigma_at(index, total_steps):
    fraction = index.astype(F32) / total_steps
    return SHIFT_FACTOR * fraction / (1.0 + (SHIFT_FACTOR - 1.0) * fraction)


def advantage_of(rewards, group_ids):
    members = (group_ids == group_ids[:, 0:1]).astype(F32)
    member_total = jnp.sum(members, axis=1, keepdims=True)
    group_mean = jnp.sum(members * rewards, axis=1, keepdims=True) / member_total
    spread = jnp.sqrt(jnp.sum(members * (rewards - group_mean) ** 2, axis=1, keepdims=True) / member_total)
    return (rewards[:, 0:1] - group_mean) / jnp.maximum(spread, REWARD_FLOOR)


def swap(x, axis, bit):
    return lax.ppermute(x, axis, [(i, i ^ bit) for i in range(lax.axis_size(axis))])


def add_kernel(a_ref, b_ref, o_ref):
    o_ref[...] = (a_ref[...].astype(F32) + b_ref[...].astype(F32)).astype(BF16)


def add(a, b):
    return pl.pallas_call(
        add_kernel,
        in_specs=[VMEM, VMEM],
        out_specs=VMEM,
        out_shape=pltpu.VMEM(a.shape, BF16),
        compiler_params=params(4),
        name="add",
    )(a, b)


def butterfly(x, axis):
    bit = 1
    while 2 * bit < lax.axis_size(axis):
        x = add(x, swap(x, axis, bit))
        bit *= 2
    return x, swap(x, axis, bit)


def pick_kernel(place_ref, mine_ref, other_ref, now_ref, next_ref, head_ref, tail_ref):
    mine = mine_ref[...]
    other = other_ref[...]
    sampler = place_ref[1] == 0
    now = jnp.where(sampler, mine.astype(F32), other.astype(F32)).astype(BF16)
    now_ref[...] = now
    next_ref[...] = jnp.where(sampler, other.astype(F32), mine.astype(F32)).astype(BF16)
    spare = head_ref.shape[1]
    head_ref[...] = now[:, :spare]
    tail_ref[...] = now[:, now.shape[1] - spare :]


def pick(place, mine, other, spare):
    shape = pltpu.VMEM(mine.shape, BF16)
    edge = pltpu.VMEM((mine.shape[0], spare), BF16)
    return pl.pallas_call(
        pick_kernel,
        in_specs=[SMEM, VMEM, VMEM],
        out_specs=[VMEM] * 4,
        out_shape=[shape, shape, edge, edge],
        compiler_params=params(4),
        name="pick",
    )(place, mine, other)


def lead_kernel(stride, unit, mom_ref, o_ref):
    for q in range(stride):
        o_ref[0, q] = (MOMENTUM_DECAY * mom_ref[pl.ds(q, unit, stride=stride), :]).astype(BF16)


def lead(mom, stride, unit):
    return pl.pallas_call(
        functools.partial(lead_kernel, stride, unit),
        grid=(1,),
        in_specs=[pl.BlockSpec((unit * stride, HD), lambda i: (0, 0))],
        out_specs=pl.BlockSpec((1, stride, unit, HD), lambda i: (0, 0, 0, 0)),
        out_shape=jax.ShapeDtypeStruct((1, stride, unit, HD), BF16),
        name="lead",
    )(mom)


def prepare_kernel(sizes, stride, unit, sliced, at_ref, e_hbm, mom_hbm, w_hbm, m_ref, et_ref, w_ref, mom_ref, *rest):
    pieces = rest[: len(sizes)]
    e_ref, e_sem, w_sem, mom_sem = rest[len(sizes) :]
    rows = w_ref.shape[1]
    half = rows // 2
    count = mom_ref.shape[0] // 5
    if sliced:
        e_src = e_hbm
    else:
        e_src = e_hbm.at[:, pl.ds(pl.multiple_of(at_ref[0] * rows, HD), rows)]
    e_copy = pltpu.make_async_copy(e_src, e_ref, e_sem)
    e_copy.start()
    w_copies = []
    for m in range(3):
        for k in range(2):
            at = pl.ds(k * half, half)
            w_copies.append(pltpu.make_async_copy(w_hbm.at[m, at], w_ref.at[m, at], w_sem.at[2 * m + k]))
    mom_copies = [
        pltpu.make_async_copy(mom_hbm.at[pl.ds(k * count, count)], mom_ref.at[pl.ds(k * count, count)], mom_sem.at[k])
        for k in range(5)
    ]
    for copy in w_copies[:2] + mom_copies[:2] + w_copies[2:4] + mom_copies[2:4] + w_copies[4:] + mom_copies[4:]:
        copy.start()
    e_copy.wait()
    et_ref[...] = e_ref[...].astype(F32).T.astype(BF16)
    waited = 0
    done = 0
    for m in range(3):
        w_copies[2 * m].wait()
        w_copies[2 * m + 1].wait()
        m_ref[m] = dot(e_ref[...], w_ref[m]).astype(BF16)
        target = 2 * m + 2 if m < 2 else 5
        while waited < target:
            mom_copies[waited].wait()
            waited += 1
        for u in range(done, 2 * target):
            if u > 0:
                k, first = 0, 1
                while u >= first + sizes[k]:
                    first += sizes[k]
                    k += 1
                for q in range(stride):
                    part = mom_ref[pl.ds(u * unit * stride + q, unit, stride=stride), :]
                    pieces[k][u - first, q] = (MOMENTUM_DECAY * part).astype(BF16)
        done = 2 * target


def prepare(place, w_embed, mom, w, sizes, stride, unit):
    _, rows, width = w.shape
    sliced = rows % HD != 0
    if sliced:
        w_embed = lax.dynamic_slice_in_dim(w_embed, place[0] * rows, rows, axis=1)
    return pl.pallas_call(
        functools.partial(prepare_kernel, sizes, stride, unit, sliced),
        in_specs=[SMEM, HBM, HBM, HBM],
        out_specs=[VMEM] * (4 + len(sizes)),
        out_shape=[
            pltpu.VMEM((3, CH, width), BF16),
            pltpu.VMEM((rows, CH), BF16),
            pltpu.VMEM(w.shape, BF16),
            pltpu.VMEM(mom.shape, F32),
        ]
        + [pltpu.VMEM((n, stride, unit, HD), BF16) for n in sizes],
        scratch_shapes=[
            pltpu.VMEM((CH, rows), BF16),
            pltpu.SemaphoreType.DMA(()),
            pltpu.SemaphoreType.DMA((6,)),
            pltpu.SemaphoreType.DMA((5,)),
        ],
        compiler_params=params(4),
        name="prepare",
    )(place, in_hbm(w_embed), in_hbm(mom), in_hbm(w))


def forward_kernel(tiles, heads, ends, *refs):
    place_ref, left_ref, now_ref, right_ref, ma_ref, mb_ref, wot_ref = refs[:7]
    m_ref, win_ref, e_ref, u_ref, il_ref, pred_ref, mk_ref, att_ref = refs[7:]
    tok = tiles * TILE
    m_ref[...] = (ma_ref[...].astype(F32) + mb_ref[...].astype(F32)).astype(BF16)
    mk_ref[...] = jnp.zeros_like(mk_ref)
    mk_ref[0:CH, :] = m_ref[1]

    spare = left_ref.shape[1]
    left = left_ref[...].astype(F32).T[spare - TILE :]
    now = now_ref[...].astype(F32).T
    right = right_ref[...].astype(F32).T[:TILE]
    blocks = [left] + [now[j * TILE : (j + 1) * TILE] for j in range(tiles)] + [right]
    lane = lax.broadcasted_iota(jnp.int32, (TILE, CH), 1) + CH
    flags = jnp.where((lane == ONE_LANE) | (lane == LOW_LANE), 1.0, 0.0)
    seq = place_ref[0]
    for j in range(tiles):
        for k in range(3):
            extra = flags
            if j + k == 0:
                extra = jnp.where(lane == BIAS_LANE, jnp.where(seq == 0, MASKED, 0.0), flags)
            if j + k == tiles + 1:
                extra = jnp.where(lane == BIAS_LANE, jnp.where(seq == ends, MASKED, 0.0), flags)
            win_ref[j, k * TILE : (k + 1) * TILE, :] = jnp.concatenate([blocks[j + k], extra], axis=1).astype(BF16)
        pad_lane = lax.broadcasted_iota(jnp.int32, (WINDOW - 3 * TILE, HD), 1)
        win_ref[j, 3 * TILE :, :] = jnp.where(pad_lane == BIAS_LANE, MASKED, 0.0).astype(BF16)

    lane = lax.broadcasted_iota(jnp.int32, (TILE, HD), 1)
    unit = jnp.where(lane == BIAS_LANE, 1.0, 0.0)
    factor = LOG2E * HD ** (-0.5)
    for j in range(tiles):
        own = win_ref[j, TILE : 2 * TILE, 0:CH]
        queries = dot(own, m_ref[0]).astype(BF16)
        keys = win_ref[j]
        for h in range(heads):
            cols = slice(h * HD, (h + 1) * HD)
            t = dot(queries[:, cols], mk_ref[:, cols], NT) * factor + unit
            s = dot(t.astype(BF16), keys, NT)
            e = jnp.exp2(s - jnp.max(s, axis=1, keepdims=True)).astype(BF16)
            at = slice(h * tok + j * TILE, h * tok + (j + 1) * TILE)
            e_ref[at, :] = e
            u = dot(e, keys)
            inv = 1.0 / u[:, ONE_LANE : ONE_LANE + 1]
            u = (u * inv).astype(BF16)
            u_ref[at, :] = u
            il_ref[at, :] = jnp.broadcast_to(inv, (TILE, HD))
            att_ref[j * TILE : (j + 1) * TILE, cols] = dot(u[:, 0:CH], m_ref[2, :, cols]).astype(BF16)
    pred_ref[...] = dot(wot_ref[...], att_ref[...], NT).astype(BF16)


def forward(place, left, now, right, ma, mb, wot, tiles, heads, seq_count):
    tok = tiles * TILE
    rows = heads * tok
    width = heads * HD
    return pl.pallas_call(
        functools.partial(forward_kernel, tiles, heads, seq_count - 1),
        in_specs=[SMEM] + [VMEM] * 6,
        out_specs=[VMEM] * 6,
        out_shape=[
            pltpu.VMEM((3, CH, width), BF16),
            pltpu.VMEM((tiles, WINDOW, HD), BF16),
            pltpu.VMEM((rows, WINDOW), BF16),
            pltpu.VMEM((rows, HD), BF16),
            pltpu.VMEM((rows, HD), F32),
            pltpu.VMEM((CH, tok), BF16),
        ],
        scratch_shapes=[pltpu.VMEM((HD, width), BF16), pltpu.VMEM((tok, width), BF16)],
        compiler_params=params(8),
        name="attend",
    )(place, left, now, right, ma, mb, wot)


def backward_kernel(tiles, heads, tokens_all, *refs):
    (time_ref, rewards_ref, groups_ref, win_ref, m_ref, wot_ref, e_ref, u_ref, il_ref, now_ref, next_ref) = refs[:11]
    pred_refs = refs[11:-3]
    zy_ref, mv_ref, v_ref = refs[-3:]
    tok = tiles * TILE
    mv_ref[...] = jnp.zeros_like(mv_ref)
    mv_ref[0:CH, :] = m_ref[2]
    lane = lax.broadcasted_iota(jnp.int32, (TILE, HD), 1)
    scale = HD ** (-0.5)
    advantage = advantage_of(rewards_ref[...], groups_ref[...])
    index = jnp.full((1, 1), time_ref[0], jnp.int32)
    sigma_now = sigma_at(index, STEPS)
    step_size = sigma_at(index - 1, STEPS) - sigma_now
    coefficient = advantage * LOSS_SCALE * (1.0 - sigma_now) / (NOISE_LEVEL**2 * sigma_now * tokens_all)
    pred = pred_refs[0][...].astype(F32)
    for ref in pred_refs[1:]:
        pred = pred + ref[...].astype(F32)
    step_mean = now_ref[...].astype(F32) + step_size * pred
    pg_flat = coefficient * (next_ref[...].astype(F32) - step_mean)
    pg = pg_flat.T.astype(BF16)
    pg_flat = pg_flat.astype(BF16)
    ag_all = dot(pg, wot_ref[...]).astype(BF16)
    for j in range(tiles):
        at = slice(j * TILE, (j + 1) * TILE)
        ag = ag_all[at]
        keys = win_ref[j]
        for h in range(heads):
            cols = slice(h * HD, (h + 1) * HD)
            rows = slice(h * tok + j * TILE, h * tok + (j + 1) * TILE)
            w = dot(ag[:, cols], mv_ref[:, cols], NT).astype(BF16).astype(F32)
            u = u_ref[rows, :].astype(F32)
            row_dot = jnp.sum(w * u, axis=1, keepdims=True)
            factor = scale * il_ref[rows, :]
            w = w * factor
            row_dot = row_dot * factor
            high = row_dot.astype(BF16).astype(F32)
            low = row_dot - high
            w = jnp.where(lane == ONE_LANE, -high, jnp.where(lane == LOW_LANE, -low, w))
            x = dot(w.astype(BF16), keys, NT)
            ds = (e_ref[rows, :].astype(F32) * x).astype(BF16)
            v_ref[rows, :] = dot(ds, keys).astype(BF16)
    now = now_ref[...]
    for h in range(heads):
        rows = slice(h * tok, (h + 1) * tok)
        z = dot(now, v_ref[rows, :])
        y = dot(pg_flat, u_ref[rows, :])
        zy_ref[h * CH : (h + 1) * CH, :] = jnp.concatenate([z[:, 0:CH], y[:, 0:CH]], axis=1).astype(BF16)


def backward(timestep, rewards, group_ids, win, m, wot, e, u, il, now, later, preds, tiles, heads, tokens_all):
    width = heads * HD
    return pl.pallas_call(
        functools.partial(backward_kernel, tiles, heads, tokens_all),
        in_specs=[SMEM] + [VMEM] * (10 + len(preds)),
        out_specs=VMEM,
        out_shape=pltpu.VMEM((heads * CH, HD), BF16),
        scratch_shapes=[pltpu.VMEM((HD, width), BF16), pltpu.VMEM((heads * tiles * TILE, HD), BF16)],
        compiler_params=params(8),
        name="attend_grad",
    )(timestep, rewards, group_ids, win, m, wot, e, u, il, now, later, *preds)


def update_kernel(heads, sizes, first, unit, later, *refs):
    place_ref, et_ref, mom_ref, w_ref = refs[:4]
    recv_refs = refs[4 : 4 + len(sizes)]
    rest = refs[4 + len(sizes) :]
    if later:
        g_ref = rest[0]
        onm_hbm, ow_hbm, gs_ref, fs_ref, onm_ref, ow_ref, sems = rest[3:]
    else:
        za_ref, zb_ref, m_ref, wot_ref, onm_hbm, ow_hbm, g_ref, gs_ref, fs_ref, onm_ref, ow_ref, sems = rest
    stride = 3 * heads
    lin = unit * stride
    role = place_ref[1]
    slots = onm_ref.shape[0]

    if not later:
        for h in range(heads):
            cols = slice(h * HD, (h + 1) * HD)
            rows = slice(h * CH, (h + 1) * CH)
            zy = (za_ref[rows, :].astype(F32) + zb_ref[rows, :].astype(F32)).astype(BF16)
            z = zy[:, 0:CH]
            y = zy[:, CH : 2 * CH]
            g_ref[0, :, cols] = dot(z, m_ref[1, :, cols]).astype(BF16)
            g_ref[1, :, cols] = dot(z, m_ref[0, :, cols], TN).astype(BF16)
            g_ref[2, :, cols] = dot(y, wot_ref[:, cols], TN).astype(BF16)

    def copies(u, slot):
        rows = pl.ds(u * 2 * unit, 2 * unit)
        return [
            pltpu.make_async_copy(onm_ref.at[slot], onm_hbm.at[pl.ds(u * lin, lin)], sems.at[0, slot]),
            pltpu.make_async_copy(ow_ref.at[slot], ow_hbm.at[:, rows], sems.at[1, slot]),
        ]

    order = [(k, i) for k, size in enumerate(sizes) for i in range(size)]
    for step, (k, i) in enumerate(order):
        u = first + step
        slot = step % slots
        if step >= slots:
            for copy in copies(u - slots, slot):
                copy.wait()
        natural = slice(u * 2 * unit, (u + 1) * 2 * unit)
        for part in range(3):
            g = dot(et_ref[natural, :], g_ref[part])
            for b in range(heads):
                q = part * heads + b
                cols = slice(b * HD, (b + 1) * HD)
                gs_ref[q] = g[:, cols]
                own = MOMENTUM_DECAY * mom_ref[pl.ds(u * lin + q, unit, stride=stride), :]
                own = own + gs_ref[q, pl.ds(role, unit, stride=2), :]
                other = recv_refs[k][i, q].astype(F32) + gs_ref[q, pl.ds(1 - role, unit, stride=2), :]
                onm_ref[slot, pl.ds(q, unit, stride=stride), :] = own
                fs_ref[q, pl.ds(role, unit, stride=2), :] = own
                fs_ref[q, pl.ds(1 - role, unit, stride=2), :] = other
                new = w_ref[part, natural, cols].astype(F32) - LEARNING_RATE * fs_ref[q]
                ow_ref[slot, part, :, cols] = new.astype(BF16)
        for copy in copies(u, slot):
            copy.start()
    steps = len(order)
    for step in range(max(steps - slots, 0), steps):
        for copy in copies(first + step, step % slots):
            copy.wait()


def update(place, et, mom, w, received, first, unit, heads, sources=None, before=None):
    sizes = [a.shape[0] for a in received]
    width = heads * HD
    stride = 3 * heads
    slots = min(sum(sizes), 4)
    args = [place, et, in_vmem(mom), in_vmem(w), *received]
    in_specs = [SMEM] + [VMEM] * (3 + len(received))
    out_specs = [HBM, HBM]
    out_shape = [jax.ShapeDtypeStruct(mom.shape, F32), jax.ShapeDtypeStruct(w.shape, BF16)]
    aliases = {}
    if before is None:
        args += sources
        in_specs += [VMEM] * len(sources)
        out_specs.append(VMEM)
        out_shape.append(pltpu.VMEM((3, CH, width), BF16))
    else:
        new_mom, new_w, g = before
        aliases = {len(args) + 1: 0, len(args) + 2: 1}
        args += [g, new_mom, new_w]
        in_specs += [VMEM, HBM, HBM]
    return pl.pallas_call(
        functools.partial(update_kernel, heads, sizes, first, unit, before is not None),
        in_specs=in_specs,
        out_specs=out_specs,
        out_shape=out_shape,
        input_output_aliases=aliases,
        scratch_shapes=[
            pltpu.VMEM((stride, 2 * unit, HD), F32),
            pltpu.VMEM((stride, 2 * unit, HD), F32),
            pltpu.VMEM((slots, unit * stride, HD), F32),
            pltpu.VMEM((slots, 3, 2 * unit, width), BF16),
            pltpu.SemaphoreType.DMA((2, slots)),
        ],
        compiler_params=params(10),
        name="update",
    )(*args)


def exchange(x):
    return lax.ppermute(x, "role", [(0, 1), (1, 0)])


def body(rollout, w_embed, w_qkv, w_out, momentum, rewards, group_ids, timestep):
    seq_count = lax.axis_size("seq")
    seq_index = lax.axis_index("seq")
    role_index = lax.axis_index("role")
    rows_dev = w_qkv.shape[0]
    width = w_qkv.shape[2]
    heads = width // HD
    tok_dev = rollout.shape[1]
    tiles = tok_dev // TILE
    pair_rows = rows_dev // 2

    stride = 3 * heads
    unit = pair_rows // 10
    sizes = (4, 4, 1)
    mom = momentum.reshape(pair_rows * stride, HD)
    w = w_qkv.transpose(1, 0, 2)
    wot = w_out.T
    place = jnp.stack([seq_index, role_index])

    piece = lead(mom, stride, unit)
    received = [exchange(piece)]
    mine = rollout[0].T
    other = exchange(mine)
    mom, piece = lax.optimization_barrier((mom, piece))
    m, et, w, mom, *pieces = prepare(place, w_embed, mom, w, sizes, stride, unit)
    m, received[0], other, pieces = lax.optimization_barrier((m, received[0], other, pieces))
    received += [exchange(p) for p in pieces]
    ma, mb = butterfly(m, "seq")

    latent_now, latent_next, head, tail = pick(place, mine, other, min(2 * HD, tok_dev))
    left = lax.ppermute(tail, "seq", [(i, i + 1) for i in range(seq_count - 1)])
    right = lax.ppermute(head, "seq", [(i + 1, i) for i in range(seq_count - 1)])

    m, win, e, u, il, partial_pred = forward(place, left, latent_now, right, ma, mb, wot, tiles, heads, seq_count)
    mp_count = lax.axis_size("mp")
    preds = [partial_pred] + [
        lax.ppermute(partial_pred, "mp", [(i, (i + d) % mp_count) for i in range(mp_count)])
        for d in range(1, mp_count)
    ]
    za, zb = butterfly(
        backward(
            timestep,
            rewards[None],
            group_ids[None],
            win,
            m,
            wot,
            e,
            u,
            il,
            latent_now,
            latent_next,
            preds,
            tiles,
            heads,
            tok_dev * seq_count,
        ),
        "seq",
    )

    first = update(place, et, mom, w, received[:-1], 0, unit, heads, sources=[za, zb, m, wot])
    nm, nw = update(place, et, mom, w, received[-1:], 10 - sizes[-1], unit, heads, before=first)
    return nm.reshape(momentum.shape), nw.transpose(1, 0, 2)


def solution(mesh):
    in_specs = (
        P("role", "seq", None),
        P(),
        P("seq", None, "mp"),
        P("mp", None),
        P("seq", "role", None, "mp"),
        P(),
        P(),
        P(),
    )
    out_specs = (P("seq", "role", None, "mp"), P("seq", None, "mp"))
    return jax.shard_map(body, mesh=mesh, in_specs=in_specs, out_specs=out_specs, check_vma=False)
```

```python
import functools

import jax
import jax.numpy as jnp
from jax import lax
from jax.experimental import pallas as pl
from jax.experimental.pallas import tpu as pltpu
from jax.sharding import PartitionSpec as P

HD = 128
TILE = 192
STEPS = 50
CH = 64
WINDOW = 640
ONE_LANE = 64
BIAS_LANE = 65
LOW_LANE = 66

SHIFT_FACTOR = 5.0
NOISE_LEVEL = 0.7
MOMENTUM_DECAY = 0.9
LEARNING_RATE = 0.004
LOSS_SCALE = 16384.0
REWARD_FLOOR = 0.1
MASKED = -1e30
LOG2E = 1.4426950408889634

F32 = jnp.float32
BF16 = jnp.bfloat16
NT = (((1,), (1,)), ((), ()))
TN = (((0,), (0,)), ((), ()))
NN = (((1,), (0,)), ((), ()))


VMEM = pl.BlockSpec(memory_space=pltpu.VMEM)
SMEM = pl.BlockSpec(memory_space=pltpu.SMEM)
HBM = pl.BlockSpec(memory_space=pltpu.HBM)
MIB = 1024 * 1024


def in_hbm(x):
    return pltpu.with_memory_space_constraint(x, pltpu.HBM)


def in_vmem(x):
    return pltpu.with_memory_space_constraint(x, pltpu.VMEM)


def params(mib):
    return pltpu.CompilerParams(vmem_limit_bytes=mib * MIB)


def cost(flops, nbytes, exps=0):
    return pl.CostEstimate(flops=flops, bytes_accessed=nbytes, transcendentals=exps)


def dot(a, b, dims=NN):
    return lax.dot_general(a, b, dims, preferred_element_type=F32)


def sigma_at(index, total_steps):
    fraction = index.astype(F32) / total_steps
    return SHIFT_FACTOR * fraction / (1.0 + (SHIFT_FACTOR - 1.0) * fraction)


def advantage_of(rewards, group_ids):
    members = (group_ids == group_ids[:, 0:1]).astype(F32)
    member_total = jnp.sum(members, axis=1, keepdims=True)
    group_mean = jnp.sum(members * rewards, axis=1, keepdims=True) / member_total
    spread = jnp.sqrt(jnp.sum(members * (rewards - group_mean) ** 2, axis=1, keepdims=True) / member_total)
    return (rewards[:, 0:1] - group_mean) / jnp.maximum(spread, REWARD_FLOOR)


def swap(x, axis, bit):
    return lax.ppermute(x, axis, [(i, i ^ bit) for i in range(lax.axis_size(axis))])


def add_kernel(a_ref, b_ref, o_ref):
    o_ref[...] = (a_ref[...].astype(F32) + b_ref[...].astype(F32)).astype(BF16)


def add(a, b):
    return pl.pallas_call(
        add_kernel,
        in_specs=[VMEM, VMEM],
        out_specs=VMEM,
        out_shape=pltpu.VMEM(a.shape, BF16),
        compiler_params=params(4),
        cost_estimate=cost(a.size, 6 * a.size),
        name="add",
    )(a, b)


def butterfly(x, axis):
    bit = 1
    while 2 * bit < lax.axis_size(axis):
        x = add(x, swap(x, axis, bit))
        bit *= 2
    return x, swap(x, axis, bit)


def pick_kernel(place_ref, mine_ref, other_ref, now_ref, next_ref, head_ref, tail_ref):
    mine = mine_ref[...]
    other = other_ref[...]
    sampler = place_ref[1] == 0
    now = jnp.where(sampler, mine.astype(F32), other.astype(F32)).astype(BF16)
    now_ref[...] = now
    next_ref[...] = jnp.where(sampler, other.astype(F32), mine.astype(F32)).astype(BF16)
    spare = head_ref.shape[1]
    head_ref[...] = now[:, :spare]
    tail_ref[...] = now[:, now.shape[1] - spare :]


def pick(place, mine, other, spare):
    shape = pltpu.VMEM(mine.shape, BF16)
    edge = pltpu.VMEM((mine.shape[0], spare), BF16)
    return pl.pallas_call(
        pick_kernel,
        in_specs=[SMEM, VMEM, VMEM],
        out_specs=[VMEM] * 4,
        out_shape=[shape, shape, edge, edge],
        compiler_params=params(4),
        cost_estimate=cost(mine.size, 10 * mine.size),
        name="pick",
    )(place, mine, other)


def narrow(mom_ref, o_ref, stride, first, count, at=0):
    for q in range(stride):
        part = mom_ref[pl.ds(first * stride + q, count, stride=stride), :]
        o_ref[q, pl.ds(at, count), :] = (MOMENTUM_DECAY * part).astype(BF16)


def lead_kernel(stride, count, steps, mom_hbm, o_ref, mom_ref, sems):
    copies = []
    for k in range(steps):
        rows = pl.ds(k * count * stride, count * stride)
        copies.append(pltpu.make_async_copy(mom_hbm.at[rows], mom_ref.at[rows], sems.at[k]))
        copies[-1].start()
    for k in range(steps):
        copies[k].wait()
        narrow(mom_ref, o_ref, stride, k * count, count, k * count)


def lead(mom, stride, count, steps):
    pairs = count * steps
    return pl.pallas_call(
        functools.partial(lead_kernel, stride, count, steps),
        in_specs=[HBM],
        out_specs=VMEM,
        out_shape=pltpu.VMEM((stride, pairs, HD), BF16),
        scratch_shapes=[pltpu.VMEM((pairs * stride, HD), F32), pltpu.SemaphoreType.DMA((steps,))],
        compiler_params=params(4),
        cost_estimate=cost(pairs * stride * HD, 6 * pairs * stride * HD),
        name="lead",
    )(in_hbm(mom))


def prepare_kernel(sizes, stride, skip, sliced, place_ref, e_hbm, mom_hbm, w_hbm, m_ref, et_ref, w_ref, mom_ref, *rest):
    pieces = rest[: len(sizes)]
    e_ref, e_sem, w_sem, mom_sem = rest[len(sizes) :]
    rows = w_ref.shape[1]
    half = rows // 2
    if sliced:
        e_src = e_hbm
    else:
        e_src = e_hbm.at[:, pl.ds(pl.multiple_of(place_ref[0] * rows, HD), rows)]
    e_copy = pltpu.make_async_copy(e_src, e_ref, e_sem)
    e_copy.start()
    w_copies = []
    for m in range(3):
        for k in range(2):
            at = pl.ds(k * half, half)
            w_copies.append(pltpu.make_async_copy(w_hbm.at[m, at], w_ref.at[m, at], w_sem.at[2 * m + k]))
    cuts = [(0, skip, -1, 0)]
    first = skip
    for k, size in enumerate(sizes):
        cuts += [(first + at, skip, k, at) for at in range(0, size, skip)]
        first += size
    mom_copies = []
    for k, (first, count, _, _) in enumerate(cuts):
        rows = pl.ds(first * stride, count * stride)
        mom_copies.append(pltpu.make_async_copy(mom_hbm.at[rows], mom_ref.at[rows], mom_sem.at[k]))
    for copy in w_copies + mom_copies:
        copy.start()
    e_copy.wait()
    et_ref[...] = e_ref[...].astype(F32).T.astype(BF16)
    for m in range(3):
        w_copies[2 * m].wait()
        w_copies[2 * m + 1].wait()
        m_ref[m] = dot(e_ref[...], w_ref[m]).astype(BF16)
    for (first, count, k, at), copy in zip(cuts, mom_copies):
        copy.wait()
        if k >= 0:
            narrow(mom_ref, pieces[k], stride, first, count, at)


def prepare(place, w_embed, mom, w, sizes, stride, skip):
    _, rows, width = w.shape
    sliced = rows % HD != 0
    if sliced:
        w_embed = lax.dynamic_slice_in_dim(w_embed, place[0] * rows, rows, axis=1)
    return pl.pallas_call(
        functools.partial(prepare_kernel, sizes, stride, skip, sliced),
        in_specs=[SMEM, HBM, HBM, HBM],
        out_specs=[VMEM] * (4 + len(sizes)),
        out_shape=[
            pltpu.VMEM((3, CH, width), BF16),
            pltpu.VMEM((rows, CH), BF16),
            pltpu.VMEM(w.shape, BF16),
            pltpu.VMEM(mom.shape, F32),
        ]
        + [pltpu.VMEM((stride, n, HD), BF16) for n in sizes],
        scratch_shapes=[
            pltpu.VMEM((CH, rows), BF16),
            pltpu.SemaphoreType.DMA(()),
            pltpu.SemaphoreType.DMA((6,)),
            pltpu.SemaphoreType.DMA((1 + sum(sizes) // skip,)),
        ],
        compiler_params=params(4),
        cost_estimate=cost(2 * CH * w.size, 4 * w.size + 10 * mom.size),
        name="prepare",
    )(place, in_hbm(w_embed), in_hbm(mom), in_hbm(w))


def forward_kernel(tiles, heads, ends, *refs):
    place_ref, left_ref, now_ref, right_ref, ma_ref, mb_ref, wot_ref = refs[:7]
    m_ref, win_ref, e_ref, u_ref, il_ref, pred_ref, mk_ref, att_ref, t_ref, s_ref = refs[7:]
    tok = tiles * TILE
    m_ref[...] = (ma_ref[...].astype(F32) + mb_ref[...].astype(F32)).astype(BF16)
    mk_ref[...] = jnp.zeros_like(mk_ref)
    mk_ref[0:CH, :] = m_ref[1]

    spare = left_ref.shape[1]
    left = left_ref[...].astype(F32).T[spare - TILE :]
    now = now_ref[...].astype(F32).T
    right = right_ref[...].astype(F32).T[:TILE]
    blocks = [left] + [now[j * TILE : (j + 1) * TILE] for j in range(tiles)] + [right]
    lane = lax.broadcasted_iota(jnp.int32, (TILE, CH), 1) + CH
    flags = jnp.where((lane == ONE_LANE) | (lane == LOW_LANE), 1.0, 0.0)
    seq = place_ref[0]
    for j in range(tiles):
        for k in range(3):
            extra = flags
            if j + k == 0:
                extra = jnp.where(lane == BIAS_LANE, jnp.where(seq == 0, MASKED, 0.0), flags)
            if j + k == tiles + 1:
                extra = jnp.where(lane == BIAS_LANE, jnp.where(seq == ends, MASKED, 0.0), flags)
            win_ref[j, k * TILE : (k + 1) * TILE, :] = jnp.concatenate([blocks[j + k], extra], axis=1).astype(BF16)
        pad_lane = lax.broadcasted_iota(jnp.int32, (WINDOW - 3 * TILE, HD), 1)
        win_ref[j, 3 * TILE :, :] = jnp.where(pad_lane == BIAS_LANE, MASKED, 0.0).astype(BF16)

    lane = lax.broadcasted_iota(jnp.int32, (tok, HD), 1)
    unit = jnp.where(lane == BIAS_LANE, 1.0, 0.0)
    factor = LOG2E * HD ** (-0.5)
    queries = dot(now.astype(BF16), m_ref[0]).astype(BF16)
    for h in range(heads):
        cols = slice(h * HD, (h + 1) * HD)
        t = (dot(queries[:, cols], mk_ref[:, cols], NT) * factor + unit).astype(BF16)
        for j in range(tiles):
            t_ref[j, h * TILE : (h + 1) * TILE, :] = t[j * TILE : (j + 1) * TILE]
    for j in range(tiles):
        keys = win_ref[j]
        s_ref[...] = dot(t_ref[j], keys, NT)
        for h in range(heads):
            rows = slice(h * TILE, (h + 1) * TILE)
            s = s_ref[rows, :]
            e_ref[j, rows, :] = jnp.exp2(s - jnp.max(s, axis=1, keepdims=True)).astype(BF16)
        u = dot(e_ref[j], keys)
        inv = 1.0 / u[:, ONE_LANE : ONE_LANE + 1]
        u = (u * inv).astype(BF16)
        inv = jnp.broadcast_to(inv, u.shape)
        for h in range(heads):
            rows = slice(h * TILE, (h + 1) * TILE)
            at = slice(h * tok + j * TILE, h * tok + (j + 1) * TILE)
            u_ref[at, :] = u[rows]
            il_ref[at, :] = inv[rows]
    for h in range(heads):
        cols = slice(h * HD, (h + 1) * HD)
        att_ref[:, cols] = dot(u_ref[h * tok : (h + 1) * tok, 0:CH], m_ref[2, :, cols]).astype(BF16)
    pred_ref[...] = dot(wot_ref[...], att_ref[...], NT).astype(BF16)


def forward(place, left, now, right, ma, mb, wot, tiles, heads, seq_count):
    tok = tiles * TILE
    rows = heads * tok
    width = heads * HD
    return pl.pallas_call(
        functools.partial(forward_kernel, tiles, heads, seq_count - 1),
        in_specs=[SMEM] + [VMEM] * 6,
        out_specs=[VMEM] * 6,
        out_shape=[
            pltpu.VMEM((3, CH, width), BF16),
            pltpu.VMEM((tiles, WINDOW, HD), BF16),
            pltpu.VMEM((tiles, heads * TILE, WINDOW), BF16),
            pltpu.VMEM((rows, HD), BF16),
            pltpu.VMEM((rows, HD), F32),
            pltpu.VMEM((CH, tok), BF16),
        ],
        scratch_shapes=[
            pltpu.VMEM((HD, width), BF16),
            pltpu.VMEM((tok, width), BF16),
            pltpu.VMEM((tiles, heads * TILE, HD), BF16),
            pltpu.VMEM((heads * TILE, WINDOW), F32),
        ],
        compiler_params=params(12),
        cost_estimate=cost(rows * (WINDOW + CH) * 4 * HD, 20 * rows * WINDOW, rows * WINDOW),
        name="attend",
    )(place, left, now, right, ma, mb, wot)


def backward_kernel(tiles, heads, tokens_all, *refs):
    (time_ref, rewards_ref, groups_ref, win_ref, m_ref, wot_ref, e_ref, u_ref, il_ref, now_ref, next_ref) = refs[:11]
    pred_refs = refs[11:-6]
    zy_ref, mv_ref, v_ref, t_ref, s_ref, d_ref = refs[-6:]
    tok = tiles * TILE
    mv_ref[...] = jnp.zeros_like(mv_ref)
    mv_ref[0:CH, :] = m_ref[2]
    lane = lax.broadcasted_iota(jnp.int32, (tok, HD), 1)
    scale = HD ** (-0.5)
    advantage = advantage_of(rewards_ref[...], groups_ref[...])
    index = jnp.full((1, 1), time_ref[0], jnp.int32)
    sigma_now = sigma_at(index, STEPS)
    step_size = sigma_at(index - 1, STEPS) - sigma_now
    coefficient = advantage * LOSS_SCALE * (1.0 - sigma_now) / (NOISE_LEVEL**2 * sigma_now * tokens_all)
    pred = pred_refs[0][...].astype(F32)
    for ref in pred_refs[1:]:
        pred = pred + ref[...].astype(F32)
    step_mean = now_ref[...].astype(F32) + step_size * pred
    pg_flat = coefficient * (next_ref[...].astype(F32) - step_mean)
    pg = pg_flat.T.astype(BF16)
    pg_flat = pg_flat.astype(BF16)
    ag_all = dot(pg, wot_ref[...]).astype(BF16)
    for h in range(heads):
        cols = slice(h * HD, (h + 1) * HD)
        rows = slice(h * tok, (h + 1) * tok)
        w = dot(ag_all[:, cols], mv_ref[:, cols], NT).astype(BF16).astype(F32)
        row_dot = jnp.sum(w * u_ref[rows, :].astype(F32), axis=1, keepdims=True)
        factor = scale * il_ref[rows, :]
        w = w * factor
        row_dot = row_dot * factor
        high = row_dot.astype(BF16).astype(F32)
        low = row_dot - high
        w = jnp.where(lane == ONE_LANE, -high, jnp.where(lane == LOW_LANE, -low, w)).astype(BF16)
        for j in range(tiles):
            t_ref[j, h * TILE : (h + 1) * TILE, :] = w[j * TILE : (j + 1) * TILE]
    for j in range(tiles):
        keys = win_ref[j]
        s_ref[...] = dot(t_ref[j], keys, NT)
        for h in range(heads):
            rows = slice(h * TILE, (h + 1) * TILE)
            d_ref[rows, :] = (e_ref[j, rows, :].astype(F32) * s_ref[rows, :]).astype(BF16)
        v = dot(d_ref[...], keys).astype(BF16)
        for h in range(heads):
            v_ref[h * tok + j * TILE : h * tok + (j + 1) * TILE, :] = v[h * TILE : (h + 1) * TILE]
    now = now_ref[...]
    for h in range(heads):
        rows = slice(h * tok, (h + 1) * tok)
        z = dot(now, v_ref[rows, :])
        y = dot(pg_flat, u_ref[rows, :])
        zy_ref[h * CH : (h + 1) * CH, :] = jnp.concatenate([z[:, 0:CH], y[:, 0:CH]], axis=1).astype(BF16)


def backward(timestep, rewards, group_ids, win, m, wot, e, u, il, now, later, preds, tiles, heads, tokens_all):
    width = heads * HD
    return pl.pallas_call(
        functools.partial(backward_kernel, tiles, heads, tokens_all),
        in_specs=[SMEM] + [VMEM] * (10 + len(preds)),
        out_specs=VMEM,
        out_shape=pltpu.VMEM((heads * CH, HD), BF16),
        scratch_shapes=[
            pltpu.VMEM((HD, width), BF16),
            pltpu.VMEM((heads * tiles * TILE, HD), BF16),
            pltpu.VMEM((tiles, heads * TILE, HD), BF16),
            pltpu.VMEM((heads * TILE, WINDOW), F32),
            pltpu.VMEM((heads * TILE, WINDOW), BF16),
        ],
        compiler_params=params(12),
        cost_estimate=cost(width * tiles * TILE * (WINDOW + CH) * 4, 20 * heads * tiles * TILE * WINDOW),
        name="attend_grad",
    )(timestep, rewards, group_ids, win, m, wot, e, u, il, now, later, *preds)


def update_kernel(heads, unit, sizes, first, later, *refs):
    place_ref, et_ref, mom_ref, w_ref = refs[:4]
    recv_refs = refs[4 : 4 + len(sizes)]
    rest = refs[4 + len(sizes) :]
    if later:
        g_ref = rest[0]
        onm_hbm, ow_hbm, gs_ref, fs_ref, onm_ref, ow_ref, sems = rest[3:]
    else:
        za_ref, zb_ref, m_ref, wot_ref, onm_hbm, ow_hbm, g_ref, gs_ref, fs_ref, onm_ref, ow_ref, sems = rest
    stride = 3 * heads
    role = place_ref[1]
    slots = onm_ref.shape[0]

    if not later:
        for h in range(heads):
            cols = slice(h * HD, (h + 1) * HD)
            rows = slice(h * CH, (h + 1) * CH)
            zy = (za_ref[rows, :].astype(F32) + zb_ref[rows, :].astype(F32)).astype(BF16)
            z = zy[:, 0:CH]
            y = zy[:, CH : 2 * CH]
            g_ref[0, :, cols] = dot(z, m_ref[1, :, cols]).astype(BF16)
            g_ref[1, :, cols] = dot(z, m_ref[0, :, cols], TN).astype(BF16)
            g_ref[2, :, cols] = dot(y, wot_ref[:, cols], TN).astype(BF16)

    total = sum(sizes)
    for part in range(3):
        g = dot(et_ref[2 * first : 2 * (first + total), :], g_ref[part])
        for b in range(heads):
            gs_ref[part * heads + b] = g[:, b * HD : (b + 1) * HD]

    def copies(pair, count, slot):
        lin = pl.ds(pair * stride, count * stride)
        rows = pl.ds(2 * pair, 2 * count)
        return [
            pltpu.make_async_copy(onm_ref.at[slot, pl.ds(0, count * stride)], onm_hbm.at[lin], sems.at[0, slot]),
            pltpu.make_async_copy(ow_ref.at[slot, :, pl.ds(0, 2 * count)], ow_hbm.at[:, rows], sems.at[1, slot]),
        ]

    order = []
    pair = first
    for k, size in enumerate(sizes):
        count = 2 * unit if size % (2 * unit) == 0 else unit
        for i in range(size // count):
            order.append((k, i * count, pair, count))
            pair += count
    for step, (k, at, pair, count) in enumerate(order):
        slot = step % slots
        if step >= slots:
            for copy in copies(*order[step - slots][2:], slot):
                copy.wait()
        natural = slice(2 * pair, 2 * (pair + count))
        local = 2 * (pair - first)
        mine = pl.ds(role, count, stride=2)
        theirs = pl.ds(1 - role, count, stride=2)
        for q in range(stride):
            part, b = divmod(q, heads)
            cols = slice(b * HD, (b + 1) * HD)
            own = MOMENTUM_DECAY * mom_ref[pl.ds(pair * stride + q, count, stride=stride), :]
            own = own + gs_ref[q, pl.ds(local + role, count, stride=2), :]
            other = recv_refs[k][q, at : at + count, :].astype(F32)
            other = other + gs_ref[q, pl.ds(local + 1 - role, count, stride=2), :]
            onm_ref[slot, pl.ds(q, count, stride=stride), :] = own
            fs_ref[q, mine, :] = own
            fs_ref[q, theirs, :] = other
            new = w_ref[part, natural, cols].astype(F32) - LEARNING_RATE * fs_ref[q, 0 : 2 * count, :]
            ow_ref[slot, part, 0 : 2 * count, cols] = new.astype(BF16)
        for copy in copies(pair, count, slot):
            copy.start()
    for step in range(max(len(order) - slots, 0), len(order)):
        for copy in copies(*order[step][2:], step % slots):
            copy.wait()


def update(place, et, mom, w, received, first, unit, heads, sources=None, before=None):
    sizes = [a.shape[1] for a in received]
    _, rows, width = w.shape
    stride = 3 * heads
    slots = min(sum(sizes) // unit, 4)
    most = max(2 * unit if n % (2 * unit) == 0 else unit for n in sizes)
    args = [place, et, in_vmem(mom), in_vmem(w), *received]
    in_specs = [SMEM] + [VMEM] * (3 + len(received))
    out_specs = [HBM, HBM]
    out_shape = [jax.ShapeDtypeStruct((rows // 2 * stride, HD), F32), jax.ShapeDtypeStruct(w.shape, BF16)]
    aliases = {}
    if before is None:
        args += sources
        in_specs += [VMEM] * len(sources)
        out_specs.append(VMEM)
        out_shape.append(pltpu.VMEM((3, CH, width), BF16))
    else:
        new_mom, new_w, g = before
        aliases = {len(args) + 1: 0, len(args) + 2: 1}
        args += [g, new_mom, new_w]
        in_specs += [VMEM, HBM, HBM]
    return pl.pallas_call(
        functools.partial(update_kernel, heads, unit, sizes, first, before is not None),
        in_specs=in_specs,
        out_specs=out_specs,
        out_shape=out_shape,
        input_output_aliases=aliases,
        scratch_shapes=[
            pltpu.VMEM((stride, 2 * sum(sizes), HD), F32),
            pltpu.VMEM((stride, 2 * most, HD), F32),
            pltpu.VMEM((slots, most * stride, HD), F32),
            pltpu.VMEM((slots, 3, 2 * most, width), BF16),
            pltpu.SemaphoreType.DMA((2, slots)),
        ],
        compiler_params=params(14),
        cost_estimate=cost(2 * sum(sizes) * stride * HD * 2 * CH, 22 * sum(sizes) * stride * HD),
        name="update",
    )(*args)


def exchange(x):
    return lax.ppermute(x, "role", [(0, 1), (1, 0)])


def body(rollout, w_embed, w_qkv, w_out, momentum, rewards, group_ids, timestep):
    seq_count = lax.axis_size("seq")
    seq_index = lax.axis_index("seq")
    role_index = lax.axis_index("role")
    rows_dev = w_qkv.shape[0]
    width = w_qkv.shape[2]
    heads = width // HD
    tok_dev = rollout.shape[1]
    tiles = tok_dev // TILE
    pair_rows = rows_dev // 2

    stride = 3 * heads
    unit = pair_rows // 20
    sizes = (2 * unit, 10 * unit, 6 * unit, 2 * unit)
    mom = momentum.reshape(pair_rows * stride, HD)
    w = w_qkv.transpose(1, 0, 2)
    wot = w_out.T
    place = jnp.stack([seq_index, role_index])

    mine = rollout[0].T
    other = exchange(mine)
    piece = lead(mom, stride, unit, 2)
    received = [exchange(piece)]
    mom, piece = lax.optimization_barrier((mom, piece))
    m, et, w, mom, *pieces = prepare(place, w_embed, mom, w, sizes[1:], stride, sizes[0])
    other, pieces = lax.optimization_barrier((other, pieces))
    received += [exchange(p) for p in pieces[:-1]]
    m, received[0] = lax.optimization_barrier((m, received[0]))
    ma, mb = butterfly(m, "seq")

    latent_now, latent_next, head, tail = pick(place, mine, other, min(2 * HD, tok_dev))
    left = lax.ppermute(tail, "seq", [(i, i + 1) for i in range(seq_count - 1)])
    right = lax.ppermute(head, "seq", [(i + 1, i) for i in range(seq_count - 1)])

    m, win, e, u, il, partial_pred = forward(place, left, latent_now, right, ma, mb, wot, tiles, heads, seq_count)
    mp_count = lax.axis_size("mp")
    preds = [partial_pred] + [
        lax.ppermute(partial_pred, "mp", [(i, (i + d) % mp_count) for i in range(mp_count)])
        for d in range(1, mp_count)
    ]
    za, zb = butterfly(
        backward(
            timestep,
            rewards[None],
            group_ids[None],
            win,
            m,
            wot,
            e,
            u,
            il,
            latent_now,
            latent_next,
            preds,
            tiles,
            heads,
            tok_dev * seq_count,
        ),
        "seq",
    )

    zb, last = lax.optimization_barrier((zb, pieces[-1]))
    received.append(exchange(last))
    done = update(place, et, mom, w, received[:2], 0, unit, heads, sources=[za, zb, m, wot])
    g = done[2]
    first = sizes[0] + sizes[1]
    done = update(place, et, mom, w, received[2:3], first, unit, heads, before=[*done[:2], g])
    nm, nw = update(place, et, mom, w, received[3:], first + sizes[2], unit, heads, before=[*done, g])
    return nm.reshape(momentum.shape), nw.transpose(1, 0, 2)


def solution(mesh):
    in_specs = (
        P("role", "seq", None),
        P(),
        P("seq", None, "mp"),
        P("mp", None),
        P("seq", "role", None, "mp"),
        P(),
        P(),
        P(),
    )
    out_specs = (P("seq", "role", None, "mp"), P("seq", None, "mp"))
    return jax.shard_map(body, mesh=mesh, in_specs=in_specs, out_specs=out_specs, check_vma=False)
```

```python
import functools

import jax
import jax.numpy as jnp
from jax import lax
from jax.experimental import pallas as pl
from jax.experimental.pallas import tpu as pltpu
from jax.sharding import PartitionSpec as P

HD = 128
TILE = 192
STEPS = 50
CH = 64
WINDOW = 640
ONE_LANE = 64
BIAS_LANE = 65
LOW_LANE = 66

SHIFT_FACTOR = 5.0
NOISE_LEVEL = 0.7
MOMENTUM_DECAY = 0.9
LEARNING_RATE = 0.004
LOSS_SCALE = 16384.0
REWARD_FLOOR = 0.1
MASKED = -1e30
LOG2E = 1.4426950408889634

F32 = jnp.float32
BF16 = jnp.bfloat16
NT = (((1,), (1,)), ((), ()))
TN = (((0,), (0,)), ((), ()))
NN = (((1,), (0,)), ((), ()))


VMEM = pl.BlockSpec(memory_space=pltpu.VMEM)
SMEM = pl.BlockSpec(memory_space=pltpu.SMEM)
HBM = pl.BlockSpec(memory_space=pltpu.HBM)
MIB = 1024 * 1024


def in_hbm(x):
    return pltpu.with_memory_space_constraint(x, pltpu.HBM)


def in_vmem(x):
    return pltpu.with_memory_space_constraint(x, pltpu.VMEM)


def params(mib):
    return pltpu.CompilerParams(vmem_limit_bytes=mib * MIB)


def cost(flops, nbytes, exps=0):
    return pl.CostEstimate(flops=flops, bytes_accessed=nbytes, transcendentals=exps)


def dot(a, b, dims=NN):
    return lax.dot_general(a, b, dims, preferred_element_type=F32)


def sigma_at(index, total_steps):
    fraction = index.astype(F32) / total_steps
    return SHIFT_FACTOR * fraction / (1.0 + (SHIFT_FACTOR - 1.0) * fraction)


def advantage_of(rewards, group_ids):
    members = (group_ids == group_ids[:, 0:1]).astype(F32)
    member_total = jnp.sum(members, axis=1, keepdims=True)
    group_mean = jnp.sum(members * rewards, axis=1, keepdims=True) / member_total
    spread = jnp.sqrt(jnp.sum(members * (rewards - group_mean) ** 2, axis=1, keepdims=True) / member_total)
    return (rewards[:, 0:1] - group_mean) / jnp.maximum(spread, REWARD_FLOOR)


def swap(x, axis, bit):
    return lax.ppermute(x, axis, [(i, i ^ bit) for i in range(lax.axis_size(axis))])


def add_kernel(a_ref, b_ref, o_ref):
    o_ref[...] = (a_ref[...].astype(F32) + b_ref[...].astype(F32)).astype(BF16)


def add(a, b):
    return pl.pallas_call(
        add_kernel,
        in_specs=[VMEM, VMEM],
        out_specs=VMEM,
        out_shape=pltpu.VMEM(a.shape, BF16),
        compiler_params=params(4),
        cost_estimate=cost(a.size, 6 * a.size),
        name="add",
    )(a, b)


def butterfly(x, axis):
    bit = 1
    while 2 * bit < lax.axis_size(axis):
        x = add(x, swap(x, axis, bit))
        bit *= 2
    return x, swap(x, axis, bit)


def pick_kernel(place_ref, mine_ref, other_ref, now_ref, next_ref, head_ref, tail_ref):
    mine = mine_ref[...]
    other = other_ref[...]
    sampler = place_ref[1] == 0
    now = jnp.where(sampler, mine.astype(F32), other.astype(F32)).astype(BF16)
    now_ref[...] = now
    next_ref[...] = jnp.where(sampler, other.astype(F32), mine.astype(F32)).astype(BF16)
    spare = head_ref.shape[1]
    head_ref[...] = now[:, :spare]
    tail_ref[...] = now[:, now.shape[1] - spare :]


def pick(place, mine, other, spare):
    shape = pltpu.VMEM(mine.shape, BF16)
    edge = pltpu.VMEM((mine.shape[0], spare), BF16)
    return pl.pallas_call(
        pick_kernel,
        in_specs=[SMEM, VMEM, VMEM],
        out_specs=[VMEM] * 4,
        out_shape=[shape, shape, edge, edge],
        compiler_params=params(4),
        cost_estimate=cost(mine.size, 10 * mine.size),
        name="pick",
    )(place, mine, other)


def chunk_of(size, unit):
    return 2 * unit if size % (2 * unit) == 0 else unit


def narrow(mom_ref, o_ref, stride, first, count, at=0):
    for q in range(stride):
        part = mom_ref[pl.ds(first * stride + q, count, stride=stride), :]
        o_ref[q, pl.ds(at, count), :] = (MOMENTUM_DECAY * part).astype(BF16)


def lead_kernel(stride, count, steps, mom_hbm, o_ref, mom_ref, sems):
    copies = []
    for k in range(steps):
        rows = pl.ds(k * count * stride, count * stride)
        copies.append(pltpu.make_async_copy(mom_hbm.at[rows], mom_ref.at[rows], sems.at[k]))
        copies[-1].start()
    for k in range(steps):
        copies[k].wait()
        narrow(mom_ref, o_ref, stride, k * count, count, k * count)


def lead(mom, stride, count, steps):
    pairs = count * steps
    return pl.pallas_call(
        functools.partial(lead_kernel, stride, count, steps),
        in_specs=[HBM],
        out_specs=VMEM,
        out_shape=pltpu.VMEM((stride, pairs, HD), BF16),
        scratch_shapes=[pltpu.VMEM((pairs * stride, HD), F32), pltpu.SemaphoreType.DMA((steps,))],
        compiler_params=params(4),
        cost_estimate=cost(pairs * stride * HD, 6 * pairs * stride * HD),
        name="lead",
    )(in_hbm(mom))


def prepare_kernel(sizes, stride, skip, unit, sliced, place_ref, e_hbm, mom_hbm, w_hbm, m_ref, et_ref, w_ref, mom_ref, *rest):
    pieces = rest[: len(sizes)]
    e_ref, e_sem, w_sem, mom_sem = rest[len(sizes) :]
    rows = w_ref.shape[1]
    half = rows // 2
    if sliced:
        e_src = e_hbm
    else:
        e_src = e_hbm.at[:, pl.ds(pl.multiple_of(place_ref[0] * rows, HD), rows)]
    e_copy = pltpu.make_async_copy(e_src, e_ref, e_sem)
    e_copy.start()
    w_copies = []
    for m in range(3):
        for k in range(2):
            at = pl.ds(k * half, half)
            w_copies.append(pltpu.make_async_copy(w_hbm.at[m, at], w_ref.at[m, at], w_sem.at[2 * m + k]))
    cuts = [(0, skip, -1, 0)]
    first = skip
    for k, size in enumerate(sizes):
        step = chunk_of(size, unit)
        cuts += [(first + at, step, k, at) for at in range(0, size, step)]
        first += size
    mom_copies = []
    for k, (first, count, _, _) in enumerate(cuts):
        rows = pl.ds(first * stride, count * stride)
        mom_copies.append(pltpu.make_async_copy(mom_hbm.at[rows], mom_ref.at[rows], mom_sem.at[k]))
    for copy in w_copies + mom_copies:
        copy.start()
    e_copy.wait()
    et_ref[...] = e_ref[...].astype(F32).T.astype(BF16)
    for m in range(3):
        w_copies[2 * m].wait()
        w_copies[2 * m + 1].wait()
        m_ref[m] = dot(e_ref[...], w_ref[m]).astype(BF16)
    for (first, count, k, at), copy in zip(cuts, mom_copies):
        copy.wait()
        if k >= 0:
            narrow(mom_ref, pieces[k], stride, first, count, at)


def prepare(place, w_embed, mom, w, sizes, stride, skip, unit):
    _, rows, width = w.shape
    sliced = rows % HD != 0
    if sliced:
        w_embed = lax.dynamic_slice_in_dim(w_embed, place[0] * rows, rows, axis=1)
    return pl.pallas_call(
        functools.partial(prepare_kernel, sizes, stride, skip, unit, sliced),
        in_specs=[SMEM, HBM, HBM, HBM],
        out_specs=[VMEM] * (4 + len(sizes)),
        out_shape=[
            pltpu.VMEM((3, CH, width), BF16),
            pltpu.VMEM((rows, CH), BF16),
            pltpu.VMEM(w.shape, BF16),
            pltpu.VMEM(mom.shape, F32),
        ]
        + [pltpu.VMEM((stride, n, HD), BF16) for n in sizes],
        scratch_shapes=[
            pltpu.VMEM((CH, rows), BF16),
            pltpu.SemaphoreType.DMA(()),
            pltpu.SemaphoreType.DMA((6,)),
            pltpu.SemaphoreType.DMA((1 + sum(sizes) // unit,)),
        ],
        compiler_params=params(4),
        cost_estimate=cost(2 * CH * w.size, 4 * w.size + 10 * mom.size),
        name="prepare",
    )(place, in_hbm(w_embed), in_hbm(mom), in_hbm(w))


def forward_kernel(tiles, heads, ends, *refs):
    place_ref, left_ref, now_ref, right_ref, ma_ref, mb_ref, wot_ref = refs[:7]
    m_ref, win_ref, e_ref, u_ref, il_ref, pred_ref, mk_ref, att_ref, t_ref, s_ref = refs[7:]
    tok = tiles * TILE
    m_ref[...] = (ma_ref[...].astype(F32) + mb_ref[...].astype(F32)).astype(BF16)
    mk_ref[...] = jnp.zeros_like(mk_ref)
    mk_ref[0:CH, :] = m_ref[1]

    spare = left_ref.shape[1]
    left = left_ref[...].astype(F32).T[spare - TILE :]
    now = now_ref[...].astype(F32).T
    right = right_ref[...].astype(F32).T[:TILE]
    blocks = [left] + [now[j * TILE : (j + 1) * TILE] for j in range(tiles)] + [right]
    lane = lax.broadcasted_iota(jnp.int32, (TILE, CH), 1) + CH
    flags = jnp.where((lane == ONE_LANE) | (lane == LOW_LANE), 1.0, 0.0)
    seq = place_ref[0]
    for j in range(tiles):
        for k in range(3):
            extra = flags
            if j + k == 0:
                extra = jnp.where(lane == BIAS_LANE, jnp.where(seq == 0, MASKED, 0.0), flags)
            if j + k == tiles + 1:
                extra = jnp.where(lane == BIAS_LANE, jnp.where(seq == ends, MASKED, 0.0), flags)
            win_ref[j, k * TILE : (k + 1) * TILE, :] = jnp.concatenate([blocks[j + k], extra], axis=1).astype(BF16)
        pad_lane = lax.broadcasted_iota(jnp.int32, (WINDOW - 3 * TILE, HD), 1)
        win_ref[j, 3 * TILE :, :] = jnp.where(pad_lane == BIAS_LANE, MASKED, 0.0).astype(BF16)

    lane = lax.broadcasted_iota(jnp.int32, (tok, HD), 1)
    unit = jnp.where(lane == BIAS_LANE, 1.0, 0.0)
    factor = LOG2E * HD ** (-0.5)
    queries = dot(now.astype(BF16), m_ref[0]).astype(BF16)
    for h in range(heads):
        cols = slice(h * HD, (h + 1) * HD)
        t = (dot(queries[:, cols], mk_ref[:, cols], NT) * factor + unit).astype(BF16)
        for j in range(tiles):
            t_ref[j, h * TILE : (h + 1) * TILE, :] = t[j * TILE : (j + 1) * TILE]
    for j in range(tiles):
        keys = win_ref[j]
        s_ref[...] = dot(t_ref[j], keys, NT)
        for h in range(heads):
            rows = slice(h * TILE, (h + 1) * TILE)
            s = s_ref[rows, :]
            e_ref[j, rows, :] = jnp.exp2(s - jnp.max(s, axis=1, keepdims=True)).astype(BF16)
        u = dot(e_ref[j], keys)
        inv = 1.0 / u[:, ONE_LANE : ONE_LANE + 1]
        u = (u * inv).astype(BF16)
        inv = jnp.broadcast_to(inv, u.shape)
        for h in range(heads):
            rows = slice(h * TILE, (h + 1) * TILE)
            at = slice(h * tok + j * TILE, h * tok + (j + 1) * TILE)
            u_ref[at, :] = u[rows]
            il_ref[at, :] = inv[rows]
    for h in range(heads):
        cols = slice(h * HD, (h + 1) * HD)
        att_ref[:, cols] = dot(u_ref[h * tok : (h + 1) * tok, 0:CH], m_ref[2, :, cols]).astype(BF16)
    pred_ref[...] = dot(wot_ref[...], att_ref[...], NT).astype(BF16)


def forward(place, left, now, right, ma, mb, wot, tiles, heads, seq_count):
    tok = tiles * TILE
    rows = heads * tok
    width = heads * HD
    return pl.pallas_call(
        functools.partial(forward_kernel, tiles, heads, seq_count - 1),
        in_specs=[SMEM] + [VMEM] * 6,
        out_specs=[VMEM] * 6,
        out_shape=[
            pltpu.VMEM((3, CH, width), BF16),
            pltpu.VMEM((tiles, WINDOW, HD), BF16),
            pltpu.VMEM((tiles, heads * TILE, WINDOW), BF16),
            pltpu.VMEM((rows, HD), BF16),
            pltpu.VMEM((rows, HD), F32),
            pltpu.VMEM((CH, tok), BF16),
        ],
        scratch_shapes=[
            pltpu.VMEM((HD, width), BF16),
            pltpu.VMEM((tok, width), BF16),
            pltpu.VMEM((tiles, heads * TILE, HD), BF16),
            pltpu.VMEM((heads * TILE, WINDOW), F32),
        ],
        compiler_params=params(12),
        cost_estimate=cost(rows * (WINDOW + CH) * 4 * HD, 20 * rows * WINDOW, rows * WINDOW),
        name="attend",
    )(place, left, now, right, ma, mb, wot)


def backward_kernel(tiles, heads, tokens_all, *refs):
    (time_ref, rewards_ref, groups_ref, win_ref, m_ref, wot_ref, e_ref, u_ref, il_ref, now_ref, next_ref) = refs[:11]
    pred_refs = refs[11:-6]
    zy_ref, mv_ref, v_ref, t_ref, s_ref, d_ref = refs[-6:]
    tok = tiles * TILE
    mv_ref[...] = jnp.zeros_like(mv_ref)
    mv_ref[0:CH, :] = m_ref[2]
    lane = lax.broadcasted_iota(jnp.int32, (tok, HD), 1)
    scale = HD ** (-0.5)
    advantage = advantage_of(rewards_ref[...], groups_ref[...])
    index = jnp.full((1, 1), time_ref[0], jnp.int32)
    sigma_now = sigma_at(index, STEPS)
    step_size = sigma_at(index - 1, STEPS) - sigma_now
    coefficient = advantage * LOSS_SCALE * (1.0 - sigma_now) / (NOISE_LEVEL**2 * sigma_now * tokens_all)
    pred = pred_refs[0][...].astype(F32)
    for ref in pred_refs[1:]:
        pred = pred + ref[...].astype(F32)
    step_mean = now_ref[...].astype(F32) + step_size * pred
    pg_flat = coefficient * (next_ref[...].astype(F32) - step_mean)
    pg = pg_flat.T.astype(BF16)
    pg_flat = pg_flat.astype(BF16)
    ag_all = dot(pg, wot_ref[...]).astype(BF16)
    for h in range(heads):
        cols = slice(h * HD, (h + 1) * HD)
        rows = slice(h * tok, (h + 1) * tok)
        w = dot(ag_all[:, cols], mv_ref[:, cols], NT).astype(BF16).astype(F32)
        row_dot = jnp.sum(w * u_ref[rows, :].astype(F32), axis=1, keepdims=True)
        factor = scale * il_ref[rows, :]
        w = w * factor
        row_dot = row_dot * factor
        high = row_dot.astype(BF16).astype(F32)
        low = row_dot - high
        w = jnp.where(lane == ONE_LANE, -high, jnp.where(lane == LOW_LANE, -low, w)).astype(BF16)
        for j in range(tiles):
            t_ref[j, h * TILE : (h + 1) * TILE, :] = w[j * TILE : (j + 1) * TILE]
    for j in range(tiles):
        keys = win_ref[j]
        s_ref[...] = dot(t_ref[j], keys, NT)
        for h in range(heads):
            rows = slice(h * TILE, (h + 1) * TILE)
            d_ref[rows, :] = (e_ref[j, rows, :].astype(F32) * s_ref[rows, :]).astype(BF16)
        v = dot(d_ref[...], keys).astype(BF16)
        for h in range(heads):
            v_ref[h * tok + j * TILE : h * tok + (j + 1) * TILE, :] = v[h * TILE : (h + 1) * TILE]
    now = now_ref[...]
    for h in range(heads):
        rows = slice(h * tok, (h + 1) * tok)
        z = dot(now, v_ref[rows, :])
        y = dot(pg_flat, u_ref[rows, :])
        zy_ref[h * CH : (h + 1) * CH, :] = jnp.concatenate([z[:, 0:CH], y[:, 0:CH]], axis=1).astype(BF16)


def backward(timestep, rewards, group_ids, win, m, wot, e, u, il, now, later, preds, tiles, heads, tokens_all):
    width = heads * HD
    return pl.pallas_call(
        functools.partial(backward_kernel, tiles, heads, tokens_all),
        in_specs=[SMEM] + [VMEM] * (10 + len(preds)),
        out_specs=VMEM,
        out_shape=pltpu.VMEM((heads * CH, HD), BF16),
        scratch_shapes=[
            pltpu.VMEM((HD, width), BF16),
            pltpu.VMEM((heads * tiles * TILE, HD), BF16),
            pltpu.VMEM((tiles, heads * TILE, HD), BF16),
            pltpu.VMEM((heads * TILE, WINDOW), F32),
            pltpu.VMEM((heads * TILE, WINDOW), BF16),
        ],
        compiler_params=params(12),
        cost_estimate=cost(width * tiles * TILE * (WINDOW + CH) * 4, 20 * heads * tiles * TILE * WINDOW),
        name="attend_grad",
    )(timestep, rewards, group_ids, win, m, wot, e, u, il, now, later, *preds)


def update_kernel(heads, unit, sizes, *refs):
    place_ref, et_ref, mom_ref, w_ref, za_ref, zb_ref, m_ref, wot_ref = refs[:8]
    here = len(sizes) - 1
    recv_refs = refs[8 : 8 + here]
    onm_hbm, ow_hbm, base_ref, g_ref, gs_ref, fs_ref, onm_ref, ow_ref, sems = refs[8 + here :]
    stride = 3 * heads
    role = place_ref[1]
    slots = onm_ref.shape[0]
    for h in range(heads):
        cols = slice(h * HD, (h + 1) * HD)
        rows = slice(h * CH, (h + 1) * CH)
        zy = (za_ref[rows, :].astype(F32) + zb_ref[rows, :].astype(F32)).astype(BF16)
        z = zy[:, 0:CH]
        y = zy[:, CH : 2 * CH]
        g_ref[0, :, cols] = dot(z, m_ref[1, :, cols]).astype(BF16)
        g_ref[1, :, cols] = dot(z, m_ref[0, :, cols], TN).astype(BF16)
        g_ref[2, :, cols] = dot(y, wot_ref[:, cols], TN).astype(BF16)

    arrived = sum(sizes[:here])
    order = []
    pair = 0
    for k, size in enumerate(sizes):
        count = chunk_of(size, unit)
        for i in range(size // count):
            order.append((k, i * count, pair, count))
            pair += count

    def copies(k, at, pair, count, slot):
        lin = pl.ds(pair * stride, count * stride)
        rows = pl.ds(2 * pair, 2 * count)
        out = [pltpu.make_async_copy(onm_ref.at[slot, pl.ds(0, count * stride)], onm_hbm.at[lin], sems.at[0, slot])]
        if k < here:
            out.append(
                pltpu.make_async_copy(ow_ref.at[slot, :, pl.ds(0, 2 * count)], ow_hbm.at[:, rows], sems.at[1, slot])
            )
        return out

    group = -1
    for step, (k, at, pair, count) in enumerate(order):
        if group != (k == here):
            group = k == here
            origin = arrived if group else 0
            span = sizes[here] if group else arrived
            for part in range(3):
                g = dot(et_ref[2 * origin : 2 * (origin + span), :], g_ref[part])
                for b in range(heads):
                    gs_ref[part * heads + b, 0 : 2 * span, :] = g[:, b * HD : (b + 1) * HD]
        slot = step % slots
        if step >= slots:
            for copy in copies(*order[step - slots], slot):
                copy.wait()
        natural = slice(2 * pair, 2 * (pair + count))
        local = 2 * (pair - origin)
        mine = pl.ds(role, count, stride=2)
        theirs = pl.ds(1 - role, count, stride=2)
        for q in range(stride):
            part, b = divmod(q, heads)
            cols = slice(b * HD, (b + 1) * HD)
            own = MOMENTUM_DECAY * mom_ref[pl.ds(pair * stride + q, count, stride=stride), :]
            own = own + gs_ref[q, pl.ds(local + role, count, stride=2), :]
            other = gs_ref[q, pl.ds(local + 1 - role, count, stride=2), :]
            if k < here:
                other = other + recv_refs[k][q, at : at + count, :].astype(F32)
            onm_ref[slot, pl.ds(q, count, stride=stride), :] = own
            fs_ref[q, mine, :] = own
            fs_ref[q, theirs, :] = other
            new = w_ref[part, natural, cols].astype(F32) - LEARNING_RATE * fs_ref[q, 0 : 2 * count, :]
            if k < here:
                ow_ref[slot, part, 0 : 2 * count, cols] = new.astype(BF16)
            else:
                base_ref[q, local : local + 2 * count, :] = new
        for copy in copies(k, at, pair, count, slot):
            copy.start()
    for step in range(max(len(order) - slots, 0), len(order)):
        for copy in copies(*order[step], step % slots):
            copy.wait()


def update(place, et, mom, w, received, rest, unit, heads, sources):
    sizes = [a.shape[1] for a in received] + [rest]
    _, rows, width = w.shape
    stride = 3 * heads
    slots = 4
    return pl.pallas_call(
        functools.partial(update_kernel, heads, unit, sizes),
        in_specs=[SMEM] + [VMEM] * (7 + len(received)),
        out_specs=[HBM, HBM, VMEM],
        out_shape=[
            jax.ShapeDtypeStruct(mom.shape, F32),
            jax.ShapeDtypeStruct(w.shape, BF16),
            pltpu.VMEM((stride, 2 * rest, HD), F32),
        ],
        scratch_shapes=[
            pltpu.VMEM((3, CH, width), BF16),
            pltpu.VMEM((stride, 2 * max(sum(sizes) - rest, rest), HD), F32),
            pltpu.VMEM((stride, 4 * unit, HD), F32),
            pltpu.VMEM((slots, 2 * unit * stride, HD), F32),
            pltpu.VMEM((slots, 3, 4 * unit, width), BF16),
            pltpu.SemaphoreType.DMA((2, slots)),
        ],
        compiler_params=params(16),
        cost_estimate=cost(4 * CH * w.size, 22 * mom.size),
        name="update",
    )(place, et, in_vmem(mom), in_vmem(w), *sources, *received)


def finish_kernel(heads, unit, first, local, place_ref, base_ref, recv_ref, old_hbm, ow_hbm, fs_ref, ow_ref, sems):
    del old_hbm
    stride, size, _ = recv_ref.shape
    role = place_ref[1]
    count = chunk_of(size, unit)
    fs_ref[...] = jnp.zeros_like(fs_ref)
    copies = []
    for step in range(size // count):
        at = 2 * step * count
        for q in range(stride):
            part, b = divmod(q, heads)
            fs_ref[q, pl.ds(1 - role, count, stride=2), :] = recv_ref[q, at // 2 : at // 2 + count, :].astype(F32)
            new = base_ref[q, 2 * local + at : 2 * local + at + 2 * count, :] - LEARNING_RATE * fs_ref[q]
            ow_ref[part, at : at + 2 * count, b * HD : (b + 1) * HD] = new.astype(BF16)
        source = ow_ref.at[:, pl.ds(at, 2 * count)]
        target = ow_hbm.at[:, pl.ds(2 * first + at, 2 * count)]
        copies.append(pltpu.make_async_copy(source, target, sems.at[step]))
        copies[-1].start()
    for copy in copies:
        copy.wait()


def finish(place, base, recv, old, first, local, unit, heads):
    stride, size, _ = recv.shape
    count = chunk_of(size, unit)
    return pl.pallas_call(
        functools.partial(finish_kernel, heads, unit, first, local),
        in_specs=[SMEM, VMEM, VMEM, HBM],
        out_specs=HBM,
        out_shape=jax.ShapeDtypeStruct(old.shape, BF16),
        input_output_aliases={3: 0},
        scratch_shapes=[
            pltpu.VMEM((stride, 2 * count, HD), F32),
            pltpu.VMEM((3, 2 * size, heads * HD), BF16),
            pltpu.SemaphoreType.DMA((size // count,)),
        ],
        compiler_params=params(4),
        cost_estimate=cost(2 * recv.size, 14 * recv.size),
        name="finish",
    )(place, in_vmem(base), recv, old)


def exchange(x):
    return lax.ppermute(x, "role", [(0, 1), (1, 0)])


def body(rollout, w_embed, w_qkv, w_out, momentum, rewards, group_ids, timestep):
    seq_count = lax.axis_size("seq")
    seq_index = lax.axis_index("seq")
    role_index = lax.axis_index("role")
    rows_dev = w_qkv.shape[0]
    width = w_qkv.shape[2]
    heads = width // HD
    tok_dev = rollout.shape[1]
    tiles = tok_dev // TILE
    pair_rows = rows_dev // 2

    stride = 3 * heads
    unit = pair_rows // 20
    sizes = (3 * unit, 10 * unit, 6 * unit, unit)
    mom = momentum.reshape(pair_rows * stride, HD)
    w = w_qkv.transpose(1, 0, 2)
    wot = w_out.T
    place = jnp.stack([seq_index, role_index])

    piece = lead(mom, stride, unit, 3)
    mine, piece = lax.optimization_barrier((rollout[0].T, piece))
    other = exchange(mine)
    received = [exchange(piece)]
    mom, other = lax.optimization_barrier((mom, other))
    m, et, w, mom, *pieces = prepare(place, w_embed, mom, w, sizes[1:], stride, sizes[0], unit)
    received += [exchange(p) for p in pieces[:-1]]
    m, received[0] = lax.optimization_barrier((m, received[0]))
    ma, mb = butterfly(m, "seq")

    latent_now, latent_next, head, tail = pick(place, mine, other, min(2 * HD, tok_dev))
    left = lax.ppermute(tail, "seq", [(i, i + 1) for i in range(seq_count - 1)])
    right = lax.ppermute(head, "seq", [(i + 1, i) for i in range(seq_count - 1)])

    m, win, e, u, il, partial_pred = forward(place, left, latent_now, right, ma, mb, wot, tiles, heads, seq_count)
    mp_count = lax.axis_size("mp")
    preds = [partial_pred] + [
        lax.ppermute(partial_pred, "mp", [(i, (i + d) % mp_count) for i in range(mp_count)])
        for d in range(1, mp_count)
    ]
    za, zb = butterfly(
        backward(
            timestep,
            rewards[None],
            group_ids[None],
            win,
            m,
            wot,
            e,
            u,
            il,
            latent_now,
            latent_next,
            preds,
            tiles,
            heads,
            tok_dev * seq_count,
        ),
        "seq",
    )

    zb, last = lax.optimization_barrier((zb, pieces[-1]))
    received.append(exchange(last))
    rest = sizes[2] + sizes[3]
    nm, nw, base = update(place, et, mom, w, received[:2], rest, unit, heads, [za, zb, m, wot])
    first = sizes[0] + sizes[1]
    nw = finish(place, base, received[2], nw, first, 0, unit, heads)
    nw = finish(place, base, received[3], nw, first + sizes[2], sizes[2], unit, heads)
    return nm.reshape(momentum.shape), nw.transpose(1, 0, 2)


def solution(mesh):
    in_specs = (
        P("role", "seq", None),
        P(),
        P("seq", None, "mp"),
        P("mp", None),
        P("seq", "role", None, "mp"),
        P(),
        P(),
        P(),
    )
    out_specs = (P("seq", "role", None, "mp"), P("seq", None, "mp"))
    return jax.shard_map(body, mesh=mesh, in_specs=in_specs, out_specs=out_specs, check_vma=False)
```

```python
import functools

import jax
import jax.numpy as jnp
from jax import lax
from jax.experimental import pallas as pl
from jax.experimental.pallas import tpu as pltpu
from jax.sharding import PartitionSpec as P

HD = 128
TILE = 192
STEPS = 50
CH = 64
WINDOW = 640
ONE_LANE = 64
BIAS_LANE = 65
LOW_LANE = 66

SHIFT_FACTOR = 5.0
NOISE_LEVEL = 0.7
MOMENTUM_DECAY = 0.9
LEARNING_RATE = 0.004
LOSS_SCALE = 16384.0
REWARD_FLOOR = 0.1
MASKED = -1e30
LOG2E = 1.4426950408889634

F32 = jnp.float32
BF16 = jnp.bfloat16
NT = (((1,), (1,)), ((), ()))
TN = (((0,), (0,)), ((), ()))
NN = (((1,), (0,)), ((), ()))


VMEM = pl.BlockSpec(memory_space=pltpu.VMEM)
SMEM = pl.BlockSpec(memory_space=pltpu.SMEM)
HBM = pl.BlockSpec(memory_space=pltpu.HBM)
MIB = 1024 * 1024


def in_hbm(x):
    return pltpu.with_memory_space_constraint(x, pltpu.HBM)


def in_vmem(x):
    return pltpu.with_memory_space_constraint(x, pltpu.VMEM)


def params(mib):
    return pltpu.CompilerParams(vmem_limit_bytes=mib * MIB)


def cost(flops, nbytes, exps=0):
    return pl.CostEstimate(flops=flops, bytes_accessed=nbytes, transcendentals=exps)


def dot(a, b, dims=NN):
    return lax.dot_general(a, b, dims, preferred_element_type=F32)


def sigma_at(index, total_steps):
    fraction = index.astype(F32) / total_steps
    return SHIFT_FACTOR * fraction / (1.0 + (SHIFT_FACTOR - 1.0) * fraction)


def advantage_of(rewards, group_ids):
    members = (group_ids == group_ids[:, 0:1]).astype(F32)
    member_total = jnp.sum(members, axis=1, keepdims=True)
    group_mean = jnp.sum(members * rewards, axis=1, keepdims=True) / member_total
    spread = jnp.sqrt(jnp.sum(members * (rewards - group_mean) ** 2, axis=1, keepdims=True) / member_total)
    return (rewards[:, 0:1] - group_mean) / jnp.maximum(spread, REWARD_FLOOR)


def swap(x, axis, bit):
    return lax.ppermute(x, axis, [(i, i ^ bit) for i in range(lax.axis_size(axis))])


def add_kernel(a_ref, b_ref, o_ref):
    o_ref[...] = (a_ref[...].astype(F32) + b_ref[...].astype(F32)).astype(BF16)


def add(a, b):
    return pl.pallas_call(
        add_kernel,
        in_specs=[VMEM, VMEM],
        out_specs=VMEM,
        out_shape=pltpu.VMEM(a.shape, BF16),
        compiler_params=params(4),
        cost_estimate=cost(a.size, 6 * a.size),
        name="add",
    )(a, b)


def butterfly(x, axis):
    bit = 1
    while 2 * bit < lax.axis_size(axis):
        x = add(x, swap(x, axis, bit))
        bit *= 2
    return x, swap(x, axis, bit)


def pick_kernel(place_ref, mine_ref, other_ref, now_ref, next_ref, head_ref, tail_ref):
    mine = mine_ref[...]
    other = other_ref[...]
    sampler = place_ref[1] == 0
    now = jnp.where(sampler, mine.astype(F32), other.astype(F32)).astype(BF16)
    now_ref[...] = now
    next_ref[...] = jnp.where(sampler, other.astype(F32), mine.astype(F32)).astype(BF16)
    spare = head_ref.shape[1]
    head_ref[...] = now[:, :spare]
    tail_ref[...] = now[:, now.shape[1] - spare :]


def pick(place, mine, other, spare):
    shape = pltpu.VMEM(mine.shape, BF16)
    edge = pltpu.VMEM((mine.shape[0], spare), BF16)
    return pl.pallas_call(
        pick_kernel,
        in_specs=[SMEM, VMEM, VMEM],
        out_specs=[VMEM] * 4,
        out_shape=[shape, shape, edge, edge],
        compiler_params=params(4),
        cost_estimate=cost(mine.size, 10 * mine.size),
        name="pick",
    )(place, mine, other)


def chunk_of(size, unit):
    return 2 * unit if size % (2 * unit) == 0 else unit


def narrow(mom_ref, o_ref, stride, first, count, at=0):
    for q in range(stride):
        part = mom_ref[pl.ds(first * stride + q, count, stride=stride), :]
        o_ref[q, pl.ds(at, count), :] = (MOMENTUM_DECAY * part).astype(BF16)


def lead_kernel(stride, count, steps, mom_hbm, o_ref, mom_ref, sems):
    copies = []
    for k in range(steps):
        rows = pl.ds(k * count * stride, count * stride)
        copies.append(pltpu.make_async_copy(mom_hbm.at[rows], mom_ref.at[rows], sems.at[k]))
        copies[-1].start()
    for k in range(steps):
        copies[k].wait()
        narrow(mom_ref, o_ref, stride, k * count, count, k * count)


def lead(mom, stride, count, steps):
    pairs = count * steps
    return pl.pallas_call(
        functools.partial(lead_kernel, stride, count, steps),
        in_specs=[HBM],
        out_specs=VMEM,
        out_shape=pltpu.VMEM((stride, pairs, HD), BF16),
        scratch_shapes=[pltpu.VMEM((pairs * stride, HD), F32), pltpu.SemaphoreType.DMA((steps,))],
        compiler_params=params(4),
        cost_estimate=cost(pairs * stride * HD, 6 * pairs * stride * HD),
        name="lead",
    )(in_hbm(mom))


def prepare_kernel(sizes, stride, skip, unit, sliced, place_ref, e_hbm, mom_hbm, w_hbm, m_ref, et_ref, w_ref, mom_ref, *rest):
    pieces = rest[: len(sizes)]
    e_ref, e_sem, w_sem, mom_sem = rest[len(sizes) :]
    rows = w_ref.shape[1]
    half = rows // 2
    if sliced:
        e_src = e_hbm
    else:
        e_src = e_hbm.at[:, pl.ds(pl.multiple_of(place_ref[0] * rows, HD), rows)]
    e_copy = pltpu.make_async_copy(e_src, e_ref, e_sem)
    e_copy.start()
    w_copies = []
    for m in range(3):
        for k in range(2):
            at = pl.ds(k * half, half)
            w_copies.append(pltpu.make_async_copy(w_hbm.at[m, at], w_ref.at[m, at], w_sem.at[2 * m + k]))
    cuts = [(0, skip, -1, 0)]
    first = skip
    for k, size in enumerate(sizes):
        step = chunk_of(size, unit)
        cuts += [(first + at, step, k, at) for at in range(0, size, step)]
        first += size
    mom_copies = []
    for k, (first, count, _, _) in enumerate(cuts):
        rows = pl.ds(first * stride, count * stride)
        mom_copies.append(pltpu.make_async_copy(mom_hbm.at[rows], mom_ref.at[rows], mom_sem.at[k]))
    for copy in w_copies + mom_copies:
        copy.start()
    e_copy.wait()
    et_ref[...] = e_ref[...].astype(F32).T.astype(BF16)
    for m in range(3):
        w_copies[2 * m].wait()
        w_copies[2 * m + 1].wait()
        m_ref[m] = dot(e_ref[...], w_ref[m]).astype(BF16)
    for (first, count, k, at), copy in zip(cuts, mom_copies):
        copy.wait()
        if k >= 0:
            narrow(mom_ref, pieces[k], stride, first, count, at)


def prepare(place, w_embed, mom, w, sizes, stride, skip, unit):
    _, rows, width = w.shape
    sliced = rows % HD != 0
    if sliced:
        w_embed = lax.dynamic_slice_in_dim(w_embed, place[0] * rows, rows, axis=1)
    return pl.pallas_call(
        functools.partial(prepare_kernel, sizes, stride, skip, unit, sliced),
        in_specs=[SMEM, HBM, HBM, HBM],
        out_specs=[VMEM] * (4 + len(sizes)),
        out_shape=[
            pltpu.VMEM((3, CH, width), BF16),
            pltpu.VMEM((rows, CH), BF16),
            pltpu.VMEM(w.shape, BF16),
            pltpu.VMEM(mom.shape, F32),
        ]
        + [pltpu.VMEM((stride, n, HD), BF16) for n in sizes],
        scratch_shapes=[
            pltpu.VMEM((CH, rows), BF16),
            pltpu.SemaphoreType.DMA(()),
            pltpu.SemaphoreType.DMA((6,)),
            pltpu.SemaphoreType.DMA((1 + sum(sizes) // unit,)),
        ],
        compiler_params=params(4),
        cost_estimate=cost(2 * CH * w.size, 4 * w.size + 10 * mom.size),
        name="prepare",
    )(place, in_hbm(w_embed), in_hbm(mom), in_hbm(w))


def forward_kernel(tiles, heads, ends, *refs):
    place_ref, left_ref, now_ref, right_ref, ma_ref, mb_ref, wot_ref = refs[:7]
    m_ref, win_ref, e_ref, u_ref, il_ref, pred_ref, mk_ref, att_ref, t_ref, s_ref = refs[7:]
    tok = tiles * TILE
    m_ref[...] = (ma_ref[...].astype(F32) + mb_ref[...].astype(F32)).astype(BF16)
    mk_ref[...] = jnp.zeros_like(mk_ref)
    mk_ref[0:CH, :] = m_ref[1]

    spare = left_ref.shape[1]
    left = left_ref[...].astype(F32).T[spare - TILE :]
    now = now_ref[...].astype(F32).T
    right = right_ref[...].astype(F32).T[:TILE]
    blocks = [left] + [now[j * TILE : (j + 1) * TILE] for j in range(tiles)] + [right]
    lane = lax.broadcasted_iota(jnp.int32, (TILE, CH), 1) + CH
    flags = jnp.where((lane == ONE_LANE) | (lane == LOW_LANE), 1.0, 0.0)
    seq = place_ref[0]
    for j in range(tiles):
        for k in range(3):
            extra = flags
            if j + k == 0:
                extra = jnp.where(lane == BIAS_LANE, jnp.where(seq == 0, MASKED, 0.0), flags)
            if j + k == tiles + 1:
                extra = jnp.where(lane == BIAS_LANE, jnp.where(seq == ends, MASKED, 0.0), flags)
            win_ref[j, k * TILE : (k + 1) * TILE, :] = jnp.concatenate([blocks[j + k], extra], axis=1).astype(BF16)
        pad_lane = lax.broadcasted_iota(jnp.int32, (WINDOW - 3 * TILE, HD), 1)
        win_ref[j, 3 * TILE :, :] = jnp.where(pad_lane == BIAS_LANE, MASKED, 0.0).astype(BF16)

    lane = lax.broadcasted_iota(jnp.int32, (tok, HD), 1)
    unit = jnp.where(lane == BIAS_LANE, 1.0, 0.0)
    factor = LOG2E * HD ** (-0.5)
    queries = dot(now.astype(BF16), m_ref[0]).astype(BF16)
    for h in range(heads):
        cols = slice(h * HD, (h + 1) * HD)
        t = (dot(queries[:, cols], mk_ref[:, cols], NT) * factor + unit).astype(BF16)
        for j in range(tiles):
            t_ref[j, h * TILE : (h + 1) * TILE, :] = t[j * TILE : (j + 1) * TILE]
    for j in range(tiles):
        keys = win_ref[j]
        s_ref[...] = dot(t_ref[j], keys, NT)
        for h in range(heads):
            rows = slice(h * TILE, (h + 1) * TILE)
            s = s_ref[rows, :]
            e_ref[j, rows, :] = jnp.exp2(s - jnp.max(s, axis=1, keepdims=True)).astype(BF16)
        u = dot(e_ref[j], keys)
        inv = 1.0 / u[:, ONE_LANE : ONE_LANE + 1]
        u = (u * inv).astype(BF16)
        inv = jnp.broadcast_to(inv, u.shape)
        for h in range(heads):
            rows = slice(h * TILE, (h + 1) * TILE)
            at = slice(h * tok + j * TILE, h * tok + (j + 1) * TILE)
            u_ref[at, :] = u[rows]
            il_ref[at, :] = inv[rows]
    for h in range(heads):
        cols = slice(h * HD, (h + 1) * HD)
        att_ref[:, cols] = dot(u_ref[h * tok : (h + 1) * tok, 0:CH], m_ref[2, :, cols]).astype(BF16)
    pred_ref[...] = dot(wot_ref[...], att_ref[...], NT).astype(BF16)


def forward(place, left, now, right, ma, mb, wot, tiles, heads, seq_count):
    tok = tiles * TILE
    rows = heads * tok
    width = heads * HD
    return pl.pallas_call(
        functools.partial(forward_kernel, tiles, heads, seq_count - 1),
        in_specs=[SMEM] + [VMEM] * 6,
        out_specs=[VMEM] * 6,
        out_shape=[
            pltpu.VMEM((3, CH, width), BF16),
            pltpu.VMEM((tiles, WINDOW, HD), BF16),
            pltpu.VMEM((tiles, heads * TILE, WINDOW), BF16),
            pltpu.VMEM((rows, HD), BF16),
            pltpu.VMEM((rows, HD), F32),
            pltpu.VMEM((CH, tok), BF16),
        ],
        scratch_shapes=[
            pltpu.VMEM((HD, width), BF16),
            pltpu.VMEM((tok, width), BF16),
            pltpu.VMEM((tiles, heads * TILE, HD), BF16),
            pltpu.VMEM((heads * TILE, WINDOW), F32),
        ],
        compiler_params=params(12),
        cost_estimate=cost(rows * (WINDOW + CH) * 4 * HD, 20 * rows * WINDOW, rows * WINDOW),
        name="attend",
    )(place, left, now, right, ma, mb, wot)


def backward_kernel(tiles, heads, tokens_all, *refs):
    (time_ref, rewards_ref, groups_ref, win_ref, m_ref, wot_ref, e_ref, u_ref, il_ref, now_ref, next_ref) = refs[:11]
    pred_refs = refs[11:-6]
    zy_ref, mv_ref, v_ref, t_ref, s_ref, d_ref = refs[-6:]
    tok = tiles * TILE
    mv_ref[...] = jnp.zeros_like(mv_ref)
    mv_ref[0:CH, :] = m_ref[2]
    lane = lax.broadcasted_iota(jnp.int32, (tok, HD), 1)
    scale = HD ** (-0.5)
    advantage = advantage_of(rewards_ref[...], groups_ref[...])
    index = jnp.full((1, 1), time_ref[0], jnp.int32)
    sigma_now = sigma_at(index, STEPS)
    step_size = sigma_at(index - 1, STEPS) - sigma_now
    coefficient = advantage * LOSS_SCALE * (1.0 - sigma_now) / (NOISE_LEVEL**2 * sigma_now * tokens_all)
    pred = pred_refs[0][...].astype(F32)
    for ref in pred_refs[1:]:
        pred = pred + ref[...].astype(F32)
    step_mean = now_ref[...].astype(F32) + step_size * pred
    pg_flat = coefficient * (next_ref[...].astype(F32) - step_mean)
    pg = pg_flat.T.astype(BF16)
    pg_flat = pg_flat.astype(BF16)
    ag_all = dot(pg, wot_ref[...]).astype(BF16)
    for h in range(heads):
        cols = slice(h * HD, (h + 1) * HD)
        rows = slice(h * tok, (h + 1) * tok)
        w = dot(ag_all[:, cols], mv_ref[:, cols], NT).astype(BF16).astype(F32)
        row_dot = jnp.sum(w * u_ref[rows, :].astype(F32), axis=1, keepdims=True)
        factor = scale * il_ref[rows, :]
        w = w * factor
        row_dot = row_dot * factor
        high = row_dot.astype(BF16).astype(F32)
        low = row_dot - high
        w = jnp.where(lane == ONE_LANE, -high, jnp.where(lane == LOW_LANE, -low, w)).astype(BF16)
        for j in range(tiles):
            t_ref[j, h * TILE : (h + 1) * TILE, :] = w[j * TILE : (j + 1) * TILE]
    for j in range(tiles):
        keys = win_ref[j]
        s_ref[...] = dot(t_ref[j], keys, NT)
        for h in range(heads):
            rows = slice(h * TILE, (h + 1) * TILE)
            d_ref[rows, :] = (e_ref[j, rows, :].astype(F32) * s_ref[rows, :]).astype(BF16)
        v = dot(d_ref[...], keys).astype(BF16)
        for h in range(heads):
            v_ref[h * tok + j * TILE : h * tok + (j + 1) * TILE, :] = v[h * TILE : (h + 1) * TILE]
    now = now_ref[...]
    for h in range(heads):
        rows = slice(h * tok, (h + 1) * tok)
        z = dot(now, v_ref[rows, :])
        y = dot(pg_flat, u_ref[rows, :])
        zy_ref[h * CH : (h + 1) * CH, :] = jnp.concatenate([z[:, 0:CH], y[:, 0:CH]], axis=1).astype(BF16)


def backward(timestep, rewards, group_ids, win, m, wot, e, u, il, now, later, preds, tiles, heads, tokens_all):
    width = heads * HD
    return pl.pallas_call(
        functools.partial(backward_kernel, tiles, heads, tokens_all),
        in_specs=[SMEM] + [VMEM] * (10 + len(preds)),
        out_specs=VMEM,
        out_shape=pltpu.VMEM((heads * CH, HD), BF16),
        scratch_shapes=[
            pltpu.VMEM((HD, width), BF16),
            pltpu.VMEM((heads * tiles * TILE, HD), BF16),
            pltpu.VMEM((tiles, heads * TILE, HD), BF16),
            pltpu.VMEM((heads * TILE, WINDOW), F32),
            pltpu.VMEM((heads * TILE, WINDOW), BF16),
        ],
        compiler_params=params(12),
        cost_estimate=cost(width * tiles * TILE * (WINDOW + CH) * 4, 20 * heads * tiles * TILE * WINDOW),
        name="attend_grad",
    )(timestep, rewards, group_ids, win, m, wot, e, u, il, now, later, *preds)


def update_kernel(heads, unit, sizes, *refs):
    place_ref, et_ref, mom_ref, w_ref, za_ref, zb_ref, m_ref, wot_ref = refs[:8]
    here = len(sizes) - 1
    recv_refs = refs[8 : 8 + here]
    onm_hbm, ow_hbm, base_ref, g_ref, gs_ref, fs_ref, onm_ref, ow_ref, sems = refs[8 + here :]
    stride = 3 * heads
    role = place_ref[1]
    slots = onm_ref.shape[0]
    for h in range(heads):
        cols = slice(h * HD, (h + 1) * HD)
        rows = slice(h * CH, (h + 1) * CH)
        zy = (za_ref[rows, :].astype(F32) + zb_ref[rows, :].astype(F32)).astype(BF16)
        z = zy[:, 0:CH]
        y = zy[:, CH : 2 * CH]
        g_ref[0, :, cols] = dot(z, m_ref[1, :, cols]).astype(BF16)
        g_ref[1, :, cols] = dot(z, m_ref[0, :, cols], TN).astype(BF16)
        g_ref[2, :, cols] = dot(y, wot_ref[:, cols], TN).astype(BF16)

    arrived = sum(sizes[:here])
    order = []
    pair = 0
    for k, size in enumerate(sizes):
        count = chunk_of(size, unit)
        for i in range(size // count):
            order.append((k, i * count, pair, count))
            pair += count

    def copies(k, at, pair, count, slot):
        lin = pl.ds(pair * stride, count * stride)
        rows = pl.ds(2 * pair, 2 * count)
        out = [pltpu.make_async_copy(onm_ref.at[slot, pl.ds(0, count * stride)], onm_hbm.at[lin], sems.at[0, slot])]
        if k < here:
            out.append(
                pltpu.make_async_copy(ow_ref.at[slot, :, pl.ds(0, 2 * count)], ow_hbm.at[:, rows], sems.at[1, slot])
            )
        return out

    group = -1
    for step, (k, at, pair, count) in enumerate(order):
        if group != (k == here):
            group = k == here
            origin = arrived if group else 0
            span = sizes[here] if group else arrived
            for part in range(3):
                g = dot(et_ref[2 * origin : 2 * (origin + span), :], g_ref[part])
                for b in range(heads):
                    gs_ref[part * heads + b, 0 : 2 * span, :] = g[:, b * HD : (b + 1) * HD]
        slot = step % slots
        if step >= slots:
            for copy in copies(*order[step - slots], slot):
                copy.wait()
        natural = slice(2 * pair, 2 * (pair + count))
        local = 2 * (pair - origin)
        mine = pl.ds(role, count, stride=2)
        theirs = pl.ds(1 - role, count, stride=2)
        for q in range(stride):
            part, b = divmod(q, heads)
            cols = slice(b * HD, (b + 1) * HD)
            own = MOMENTUM_DECAY * mom_ref[pl.ds(pair * stride + q, count, stride=stride), :]
            own = own + gs_ref[q, pl.ds(local + role, count, stride=2), :]
            other = gs_ref[q, pl.ds(local + 1 - role, count, stride=2), :]
            if k < here:
                other = other + recv_refs[k][q, at : at + count, :].astype(F32)
            onm_ref[slot, pl.ds(q, count, stride=stride), :] = own
            fs_ref[q, mine, :] = own
            fs_ref[q, theirs, :] = other
            new = w_ref[part, natural, cols].astype(F32) - LEARNING_RATE * fs_ref[q, 0 : 2 * count, :]
            if k < here:
                ow_ref[slot, part, 0 : 2 * count, cols] = new.astype(BF16)
            else:
                base_ref[q, local : local + 2 * count, :] = new
        for copy in copies(k, at, pair, count, slot):
            copy.start()
    for step in range(max(len(order) - slots, 0), len(order)):
        for copy in copies(*order[step], step % slots):
            copy.wait()


def update(place, et, mom, w, received, rest, unit, heads, sources):
    sizes = [a.shape[1] for a in received] + [rest]
    _, rows, width = w.shape
    stride = 3 * heads
    slots = 4
    return pl.pallas_call(
        functools.partial(update_kernel, heads, unit, sizes),
        in_specs=[SMEM] + [VMEM] * (7 + len(received)),
        out_specs=[HBM, HBM, VMEM],
        out_shape=[
            jax.ShapeDtypeStruct(mom.shape, F32),
            jax.ShapeDtypeStruct(w.shape, BF16),
            pltpu.VMEM((stride, 2 * rest, HD), F32),
        ],
        scratch_shapes=[
            pltpu.VMEM((3, CH, width), BF16),
            pltpu.VMEM((stride, 2 * max(sum(sizes) - rest, rest), HD), F32),
            pltpu.VMEM((stride, 4 * unit, HD), F32),
            pltpu.VMEM((slots, 2 * unit * stride, HD), F32),
            pltpu.VMEM((slots, 3, 4 * unit, width), BF16),
            pltpu.SemaphoreType.DMA((2, slots)),
        ],
        compiler_params=params(16),
        cost_estimate=cost(4 * CH * w.size, 22 * mom.size),
        name="update",
    )(place, et, in_vmem(mom), in_vmem(w), *sources, *received)


def finish_kernel(heads, unit, first, local, place_ref, base_ref, recv_ref, old_hbm, ow_hbm, fs_ref, ow_ref, sems):
    del old_hbm
    stride, size, _ = recv_ref.shape
    role = place_ref[1]
    count = chunk_of(size, unit)
    fs_ref[...] = jnp.zeros_like(fs_ref)
    copies = []
    for step in range(size // count):
        at = 2 * step * count
        for q in range(stride):
            part, b = divmod(q, heads)
            fs_ref[q, pl.ds(1 - role, count, stride=2), :] = recv_ref[q, at // 2 : at // 2 + count, :].astype(F32)
            new = base_ref[q, 2 * local + at : 2 * local + at + 2 * count, :] - LEARNING_RATE * fs_ref[q]
            ow_ref[part, at : at + 2 * count, b * HD : (b + 1) * HD] = new.astype(BF16)
        source = ow_ref.at[:, pl.ds(at, 2 * count)]
        target = ow_hbm.at[:, pl.ds(2 * first + at, 2 * count)]
        copies.append(pltpu.make_async_copy(source, target, sems.at[step]))
        copies[-1].start()
    for copy in copies:
        copy.wait()


def finish(place, base, recv, old, first, local, unit, heads):
    stride, size, _ = recv.shape
    count = chunk_of(size, unit)
    return pl.pallas_call(
        functools.partial(finish_kernel, heads, unit, first, local),
        in_specs=[SMEM, VMEM, VMEM, HBM],
        out_specs=HBM,
        out_shape=jax.ShapeDtypeStruct(old.shape, BF16),
        input_output_aliases={3: 0},
        scratch_shapes=[
            pltpu.VMEM((stride, 2 * count, HD), F32),
            pltpu.VMEM((3, 2 * size, heads * HD), BF16),
            pltpu.SemaphoreType.DMA((size // count,)),
        ],
        compiler_params=params(4),
        cost_estimate=cost(2 * recv.size, 14 * recv.size),
        name="finish",
    )(place, in_vmem(base), recv, old)


def exchange(x):
    return lax.ppermute(x, "role", [(0, 1), (1, 0)])


def body(rollout, w_embed, w_qkv, w_out, momentum, rewards, group_ids, timestep):
    seq_count = lax.axis_size("seq")
    seq_index = lax.axis_index("seq")
    role_index = lax.axis_index("role")
    rows_dev = w_qkv.shape[0]
    width = w_qkv.shape[2]
    heads = width // HD
    tok_dev = rollout.shape[1]
    tiles = tok_dev // TILE
    pair_rows = rows_dev // 2

    stride = 3 * heads
    unit = pair_rows // 20
    sizes = (3 * unit, 10 * unit, 6 * unit, unit)
    mom = momentum.reshape(pair_rows * stride, HD)
    w = w_qkv.transpose(1, 0, 2)
    wot = w_out.T
    place = jnp.stack([seq_index, role_index])

    mine = rollout[0].T
    other = exchange(mine)
    piece = lead(mom, stride, unit, 3)
    received = [exchange(piece)]
    mom, piece = lax.optimization_barrier((mom, piece))
    m, et, w, mom, *pieces = prepare(place, w_embed, mom, w, sizes[1:], stride, sizes[0], unit)
    other, pieces = lax.optimization_barrier((other, pieces))
    received += [exchange(p) for p in pieces[:-1]]
    m, received[0] = lax.optimization_barrier((m, received[0]))
    ma, mb = butterfly(m, "seq")

    latent_now, latent_next, head, tail = pick(place, mine, other, min(2 * HD, tok_dev))
    left = lax.ppermute(tail, "seq", [(i, i + 1) for i in range(seq_count - 1)])
    right = lax.ppermute(head, "seq", [(i + 1, i) for i in range(seq_count - 1)])

    m, win, e, u, il, partial_pred = forward(place, left, latent_now, right, ma, mb, wot, tiles, heads, seq_count)
    mp_count = lax.axis_size("mp")
    preds = [partial_pred] + [
        lax.ppermute(partial_pred, "mp", [(i, (i + d) % mp_count) for i in range(mp_count)])
        for d in range(1, mp_count)
    ]
    za, zb = butterfly(
        backward(
            timestep,
            rewards[None],
            group_ids[None],
            win,
            m,
            wot,
            e,
            u,
            il,
            latent_now,
            latent_next,
            preds,
            tiles,
            heads,
            tok_dev * seq_count,
        ),
        "seq",
    )

    zb, last = lax.optimization_barrier((zb, pieces[-1]))
    received.append(exchange(last))
    rest = sizes[2] + sizes[3]
    nm, nw, base = update(place, et, mom, w, received[:2], rest, unit, heads, [za, zb, m, wot])
    first = sizes[0] + sizes[1]
    nw = finish(place, base, received[2], nw, first, 0, unit, heads)
    nw = finish(place, base, received[3], nw, first + sizes[2], sizes[2], unit, heads)
    return nm.reshape(momentum.shape), nw.transpose(1, 0, 2)


def solution(mesh):
    in_specs = (
        P("role", "seq", None),
        P(),
        P("seq", None, "mp"),
        P("mp", None),
        P("seq", "role", None, "mp"),
        P(),
        P(),
        P(),
    )
    out_specs = (P("seq", "role", None, "mp"), P("seq", None, "mp"))
    return jax.shard_map(body, mesh=mesh, in_specs=in_specs, out_specs=out_specs, check_vma=False)
```

```python
import functools

import jax
import jax.numpy as jnp
from jax import lax
from jax.experimental import pallas as pl
from jax.experimental.pallas import tpu as pltpu
from jax.sharding import PartitionSpec as P

HD = 128
TILE = 192
STEPS = 50
CH = 64
WINDOW = 640
ONE_LANE = 64
BIAS_LANE = 65
LOW_LANE = 66

SHIFT_FACTOR = 5.0
NOISE_LEVEL = 0.7
MOMENTUM_DECAY = 0.9
LEARNING_RATE = 0.004
LOSS_SCALE = 16384.0
REWARD_FLOOR = 0.1
MASKED = -1e30
LOG2E = 1.4426950408889634

F32 = jnp.float32
BF16 = jnp.bfloat16
NT = (((1,), (1,)), ((), ()))
TN = (((0,), (0,)), ((), ()))
NN = (((1,), (0,)), ((), ()))


VMEM = pl.BlockSpec(memory_space=pltpu.VMEM)
SMEM = pl.BlockSpec(memory_space=pltpu.SMEM)
HBM = pl.BlockSpec(memory_space=pltpu.HBM)
MIB = 1024 * 1024


def in_hbm(x):
    return pltpu.with_memory_space_constraint(x, pltpu.HBM)


def in_vmem(x):
    return pltpu.with_memory_space_constraint(x, pltpu.VMEM)


def params(mib):
    return pltpu.CompilerParams(vmem_limit_bytes=mib * MIB)


def cost(flops, nbytes, exps=0):
    return pl.CostEstimate(flops=flops, bytes_accessed=nbytes, transcendentals=exps)


def dot(a, b, dims=NN):
    return lax.dot_general(a, b, dims, preferred_element_type=F32)


def sigma_at(index, total_steps):
    fraction = index.astype(F32) / total_steps
    return SHIFT_FACTOR * fraction / (1.0 + (SHIFT_FACTOR - 1.0) * fraction)


def advantage_of(rewards, group_ids):
    members = (group_ids == group_ids[:, 0:1]).astype(F32)
    member_total = jnp.sum(members, axis=1, keepdims=True)
    group_mean = jnp.sum(members * rewards, axis=1, keepdims=True) / member_total
    spread = jnp.sqrt(jnp.sum(members * (rewards - group_mean) ** 2, axis=1, keepdims=True) / member_total)
    return (rewards[:, 0:1] - group_mean) / jnp.maximum(spread, REWARD_FLOOR)


def swap(x, axis, bit):
    return lax.ppermute(x, axis, [(i, i ^ bit) for i in range(lax.axis_size(axis))])


def add_kernel(a_ref, b_ref, o_ref):
    o_ref[...] = (a_ref[...].astype(F32) + b_ref[...].astype(F32)).astype(BF16)


def add(a, b):
    return pl.pallas_call(
        add_kernel,
        in_specs=[VMEM, VMEM],
        out_specs=VMEM,
        out_shape=pltpu.VMEM(a.shape, BF16),
        compiler_params=params(4),
        cost_estimate=cost(a.size, 6 * a.size),
        name="add",
    )(a, b)


def butterfly(x, axis):
    bit = 1
    while 2 * bit < lax.axis_size(axis):
        x = add(x, swap(x, axis, bit))
        bit *= 2
    return x, swap(x, axis, bit)


def pick_kernel(place_ref, mine_ref, piece_ref, now_ref, next_ref, head_ref, tail_ref):
    mine = mine_ref[...]
    tok = mine.shape[1]
    start = piece_ref.shape[0] - mine.size // HD
    sampler = place_ref[1] == 0
    spare = head_ref.shape[1]
    for k in range(tok // HD):
        cols = slice(k * HD, (k + 1) * HD)
        own = mine_ref[:, cols].astype(F32)
        other = piece_ref[start + k * CH : start + (k + 1) * CH, :].astype(F32)
        now_ref[:, cols] = jnp.where(sampler, own, other).astype(BF16)
        next_ref[:, cols] = jnp.where(sampler, other, own).astype(BF16)
    head_ref[...] = now_ref[:, :spare]
    tail_ref[...] = now_ref[:, tok - spare :]


def pick(place, mine, piece, spare):
    shape = pltpu.VMEM(mine.shape, BF16)
    edge = pltpu.VMEM((mine.shape[0], spare), BF16)
    return pl.pallas_call(
        pick_kernel,
        in_specs=[SMEM, VMEM, VMEM],
        out_specs=[VMEM] * 4,
        out_shape=[shape, shape, edge, edge],
        compiler_params=params(4),
        cost_estimate=cost(mine.size, 10 * mine.size),
        name="pick",
    )(place, mine, piece)


def chunk_of(size, unit):
    return 2 * unit if size % (2 * unit) == 0 else unit


def narrow(mom_ref, o_ref, stride, first, count, at, size):
    for q in range(stride):
        part = mom_ref[pl.ds(first * stride + q, count, stride=stride), :]
        o_ref[pl.ds(q * size + at, count), :] = (MOMENTUM_DECAY * part).astype(BF16)


def lead_kernel(stride, count, steps, mom_hbm, mine_hbm, o_ref, mom_ref, mine_ref, mine_sem, sems):
    mine_copy = pltpu.make_async_copy(mine_hbm, mine_ref, mine_sem)
    mine_copy.start()
    copies = []
    for k in range(steps):
        rows = pl.ds(k * count * stride, count * stride)
        copies.append(pltpu.make_async_copy(mom_hbm.at[rows], mom_ref.at[rows], sems.at[k]))
        copies[-1].start()
    start = stride * count * steps
    mine_copy.wait()
    for k in range(mine_ref.shape[1] // HD):
        o_ref[start + k * CH : start + (k + 1) * CH, :] = mine_ref[:, k * HD : (k + 1) * HD]
    for k in range(steps):
        copies[k].wait()
        narrow(mom_ref, o_ref, stride, k * count, count, k * count, count * steps)


def lead(mom, mine, stride, count, steps):
    pairs = count * steps
    return pl.pallas_call(
        functools.partial(lead_kernel, stride, count, steps),
        in_specs=[HBM, HBM],
        out_specs=VMEM,
        out_shape=pltpu.VMEM((stride * pairs + mine.size // HD, HD), BF16),
        scratch_shapes=[
            pltpu.VMEM((pairs * stride, HD), F32),
            pltpu.VMEM(mine.shape, BF16),
            pltpu.SemaphoreType.DMA(()),
            pltpu.SemaphoreType.DMA((steps,)),
        ],
        compiler_params=params(4),
        cost_estimate=cost(pairs * stride * HD, 6 * pairs * stride * HD),
        name="lead",
    )(in_hbm(mom), in_hbm(mine))


def prepare_kernel(sizes, stride, skip, unit, sliced, place_ref, e_hbm, mom_hbm, w_hbm, m_ref, et_ref, w_ref, mom_ref, *rest):
    pieces = rest[: len(sizes)]
    e_ref, e_sem, w_sem, mom_sem = rest[len(sizes) :]
    rows = w_ref.shape[1]
    half = rows // 2
    if sliced:
        e_src = e_hbm
    else:
        e_src = e_hbm.at[:, pl.ds(pl.multiple_of(place_ref[0] * rows, HD), rows)]
    e_copy = pltpu.make_async_copy(e_src, e_ref, e_sem)
    e_copy.start()
    w_copies = []
    for m in range(3):
        for k in range(2):
            at = pl.ds(k * half, half)
            w_copies.append(pltpu.make_async_copy(w_hbm.at[m, at], w_ref.at[m, at], w_sem.at[2 * m + k]))
    cuts = [(0, skip, -1, 0)]
    first = skip
    for k, size in enumerate(sizes):
        step = chunk_of(size, unit)
        cuts += [(first + at, step, k, at) for at in range(0, size, step)]
        first += size
    mom_copies = []
    for k, (first, count, _, _) in enumerate(cuts):
        rows = pl.ds(first * stride, count * stride)
        mom_copies.append(pltpu.make_async_copy(mom_hbm.at[rows], mom_ref.at[rows], mom_sem.at[k]))
    for copy in w_copies + mom_copies:
        copy.start()
    e_copy.wait()
    et_ref[...] = e_ref[...].astype(F32).T.astype(BF16)
    for m in range(3):
        w_copies[2 * m].wait()
        w_copies[2 * m + 1].wait()
        m_ref[m] = dot(e_ref[...], w_ref[m]).astype(BF16)
    for (first, count, k, at), copy in zip(cuts, mom_copies):
        copy.wait()
        if k >= 0:
            narrow(mom_ref, pieces[k], stride, first, count, at, sizes[k])


def prepare(place, w_embed, mom, w, sizes, stride, skip, unit):
    _, rows, width = w.shape
    sliced = rows % HD != 0
    if sliced:
        w_embed = lax.dynamic_slice_in_dim(w_embed, place[0] * rows, rows, axis=1)
    return pl.pallas_call(
        functools.partial(prepare_kernel, sizes, stride, skip, unit, sliced),
        in_specs=[SMEM, HBM, HBM, HBM],
        out_specs=[VMEM] * (4 + len(sizes)),
        out_shape=[
            pltpu.VMEM((3, CH, width), BF16),
            pltpu.VMEM((rows, CH), BF16),
            pltpu.VMEM(w.shape, BF16),
            pltpu.VMEM(mom.shape, F32),
        ]
        + [pltpu.VMEM((stride * n, HD), BF16) for n in sizes],
        scratch_shapes=[
            pltpu.VMEM((CH, rows), BF16),
            pltpu.SemaphoreType.DMA(()),
            pltpu.SemaphoreType.DMA((6,)),
            pltpu.SemaphoreType.DMA((1 + sum(sizes) // unit,)),
        ],
        compiler_params=params(4),
        cost_estimate=cost(2 * CH * w.size, 4 * w.size + 10 * mom.size),
        name="prepare",
    )(place, in_hbm(w_embed), in_hbm(mom), in_hbm(w))


def forward_kernel(tiles, heads, ends, *refs):
    place_ref, left_ref, now_ref, right_ref, ma_ref, mb_ref, wot_ref = refs[:7]
    m_ref, win_ref, e_ref, u_ref, il_ref, pred_ref, mk_ref, att_ref, t_ref, s_ref = refs[7:]
    tok = tiles * TILE
    m_ref[...] = (ma_ref[...].astype(F32) + mb_ref[...].astype(F32)).astype(BF16)
    mk_ref[...] = jnp.zeros_like(mk_ref)
    mk_ref[0:CH, :] = m_ref[1]

    spare = left_ref.shape[1]
    left = left_ref[...].astype(F32).T[spare - TILE :]
    now = now_ref[...].astype(F32).T
    right = right_ref[...].astype(F32).T[:TILE]
    blocks = [left] + [now[j * TILE : (j + 1) * TILE] for j in range(tiles)] + [right]
    lane = lax.broadcasted_iota(jnp.int32, (TILE, CH), 1) + CH
    flags = jnp.where((lane == ONE_LANE) | (lane == LOW_LANE), 1.0, 0.0)
    seq = place_ref[0]
    for j in range(tiles):
        for k in range(3):
            extra = flags
            if j + k == 0:
                extra = jnp.where(lane == BIAS_LANE, jnp.where(seq == 0, MASKED, 0.0), flags)
            if j + k == tiles + 1:
                extra = jnp.where(lane == BIAS_LANE, jnp.where(seq == ends, MASKED, 0.0), flags)
            win_ref[j, k * TILE : (k + 1) * TILE, :] = jnp.concatenate([blocks[j + k], extra], axis=1).astype(BF16)
        pad_lane = lax.broadcasted_iota(jnp.int32, (WINDOW - 3 * TILE, HD), 1)
        win_ref[j, 3 * TILE :, :] = jnp.where(pad_lane == BIAS_LANE, MASKED, 0.0).astype(BF16)

    lane = lax.broadcasted_iota(jnp.int32, (tok, HD), 1)
    unit = jnp.where(lane == BIAS_LANE, 1.0, 0.0)
    factor = LOG2E * HD ** (-0.5)
    queries = dot(now.astype(BF16), m_ref[0]).astype(BF16)
    for h in range(heads):
        cols = slice(h * HD, (h + 1) * HD)
        t = (dot(queries[:, cols], mk_ref[:, cols], NT) * factor + unit).astype(BF16)
        for j in range(tiles):
            t_ref[j, h * TILE : (h + 1) * TILE, :] = t[j * TILE : (j + 1) * TILE]
    for j in range(tiles):
        keys = win_ref[j]
        s_ref[...] = dot(t_ref[j], keys, NT)
        for h in range(heads):
            rows = slice(h * TILE, (h + 1) * TILE)
            s = s_ref[rows, :]
            e_ref[j, rows, :] = jnp.exp2(s - jnp.max(s, axis=1, keepdims=True)).astype(BF16)
        u = dot(e_ref[j], keys)
        inv = 1.0 / u[:, ONE_LANE : ONE_LANE + 1]
        u = (u * inv).astype(BF16)
        inv = jnp.broadcast_to(inv, u.shape)
        for h in range(heads):
            rows = slice(h * TILE, (h + 1) * TILE)
            at = slice(h * tok + j * TILE, h * tok + (j + 1) * TILE)
            u_ref[at, :] = u[rows]
            il_ref[at, :] = inv[rows]
    for h in range(heads):
        cols = slice(h * HD, (h + 1) * HD)
        att_ref[:, cols] = dot(u_ref[h * tok : (h + 1) * tok, 0:CH], m_ref[2, :, cols]).astype(BF16)
    pred_ref[...] = dot(wot_ref[...], att_ref[...], NT).astype(BF16)


def forward(place, left, now, right, ma, mb, wot, tiles, heads, seq_count):
    tok = tiles * TILE
    rows = heads * tok
    width = heads * HD
    return pl.pallas_call(
        functools.partial(forward_kernel, tiles, heads, seq_count - 1),
        in_specs=[SMEM] + [VMEM] * 6,
        out_specs=[VMEM] * 6,
        out_shape=[
            pltpu.VMEM((3, CH, width), BF16),
            pltpu.VMEM((tiles, WINDOW, HD), BF16),
            pltpu.VMEM((tiles, heads * TILE, WINDOW), BF16),
            pltpu.VMEM((rows, HD), BF16),
            pltpu.VMEM((rows, HD), F32),
            pltpu.VMEM((CH, tok), BF16),
        ],
        scratch_shapes=[
            pltpu.VMEM((HD, width), BF16),
            pltpu.VMEM((tok, width), BF16),
            pltpu.VMEM((tiles, heads * TILE, HD), BF16),
            pltpu.VMEM((heads * TILE, WINDOW), F32),
        ],
        compiler_params=params(12),
        cost_estimate=cost(rows * (WINDOW + CH) * 4 * HD, 20 * rows * WINDOW, rows * WINDOW),
        name="attend",
    )(place, left, now, right, ma, mb, wot)


def backward_kernel(tiles, heads, tokens_all, *refs):
    (time_ref, rewards_ref, groups_ref, win_ref, m_ref, wot_ref, e_ref, u_ref, il_ref, now_ref, next_ref) = refs[:11]
    pred_refs = refs[11:-6]
    zy_ref, mv_ref, v_ref, t_ref, s_ref, d_ref = refs[-6:]
    tok = tiles * TILE
    mv_ref[...] = jnp.zeros_like(mv_ref)
    mv_ref[0:CH, :] = m_ref[2]
    lane = lax.broadcasted_iota(jnp.int32, (tok, HD), 1)
    scale = HD ** (-0.5)
    advantage = advantage_of(rewards_ref[...], groups_ref[...])
    index = jnp.full((1, 1), time_ref[0], jnp.int32)
    sigma_now = sigma_at(index, STEPS)
    step_size = sigma_at(index - 1, STEPS) - sigma_now
    coefficient = advantage * LOSS_SCALE * (1.0 - sigma_now) / (NOISE_LEVEL**2 * sigma_now * tokens_all)
    pred = pred_refs[0][...].astype(F32)
    for ref in pred_refs[1:]:
        pred = pred + ref[...].astype(F32)
    step_mean = now_ref[...].astype(F32) + step_size * pred
    pg_flat = coefficient * (next_ref[...].astype(F32) - step_mean)
    pg = pg_flat.T.astype(BF16)
    pg_flat = pg_flat.astype(BF16)
    ag_all = dot(pg, wot_ref[...]).astype(BF16)
    for h in range(heads):
        cols = slice(h * HD, (h + 1) * HD)
        rows = slice(h * tok, (h + 1) * tok)
        w = dot(ag_all[:, cols], mv_ref[:, cols], NT).astype(BF16).astype(F32)
        row_dot = jnp.sum(w * u_ref[rows, :].astype(F32), axis=1, keepdims=True)
        factor = scale * il_ref[rows, :]
        w = w * factor
        row_dot = row_dot * factor
        high = row_dot.astype(BF16).astype(F32)
        low = row_dot - high
        w = jnp.where(lane == ONE_LANE, -high, jnp.where(lane == LOW_LANE, -low, w)).astype(BF16)
        for j in range(tiles):
            t_ref[j, h * TILE : (h + 1) * TILE, :] = w[j * TILE : (j + 1) * TILE]
    for j in range(tiles):
        keys = win_ref[j]
        s_ref[...] = dot(t_ref[j], keys, NT)
        for h in range(heads):
            rows = slice(h * TILE, (h + 1) * TILE)
            d_ref[rows, :] = (e_ref[j, rows, :].astype(F32) * s_ref[rows, :]).astype(BF16)
        v = dot(d_ref[...], keys).astype(BF16)
        for h in range(heads):
            v_ref[h * tok + j * TILE : h * tok + (j + 1) * TILE, :] = v[h * TILE : (h + 1) * TILE]
    now = now_ref[...]
    for h in range(heads):
        rows = slice(h * tok, (h + 1) * tok)
        z = dot(now, v_ref[rows, :])
        y = dot(pg_flat, u_ref[rows, :])
        zy_ref[h * CH : (h + 1) * CH, :] = jnp.concatenate([z[:, 0:CH], y[:, 0:CH]], axis=1).astype(BF16)


def backward(timestep, rewards, group_ids, win, m, wot, e, u, il, now, later, preds, tiles, heads, tokens_all):
    width = heads * HD
    return pl.pallas_call(
        functools.partial(backward_kernel, tiles, heads, tokens_all),
        in_specs=[SMEM] + [VMEM] * (10 + len(preds)),
        out_specs=VMEM,
        out_shape=pltpu.VMEM((heads * CH, HD), BF16),
        scratch_shapes=[
            pltpu.VMEM((HD, width), BF16),
            pltpu.VMEM((heads * tiles * TILE, HD), BF16),
            pltpu.VMEM((tiles, heads * TILE, HD), BF16),
            pltpu.VMEM((heads * TILE, WINDOW), F32),
            pltpu.VMEM((heads * TILE, WINDOW), BF16),
        ],
        compiler_params=params(12),
        cost_estimate=cost(width * tiles * TILE * (WINDOW + CH) * 4, 20 * heads * tiles * TILE * WINDOW),
        name="attend_grad",
    )(timestep, rewards, group_ids, win, m, wot, e, u, il, now, later, *preds)


def update_kernel(heads, unit, sizes, *refs):
    place_ref, et_ref, mom_ref, w_ref, za_ref, zb_ref, m_ref, wot_ref = refs[:8]
    here = len(sizes) - 1
    recv_refs = refs[8 : 8 + here]
    onm_hbm, ow_hbm, base_ref, g_ref, gs_ref, fs_ref, onm_ref, ow_ref, sems = refs[8 + here :]
    stride = 3 * heads
    role = place_ref[1]
    slots = onm_ref.shape[0]
    for h in range(heads):
        cols = slice(h * HD, (h + 1) * HD)
        rows = slice(h * CH, (h + 1) * CH)
        zy = (za_ref[rows, :].astype(F32) + zb_ref[rows, :].astype(F32)).astype(BF16)
        z = zy[:, 0:CH]
        y = zy[:, CH : 2 * CH]
        g_ref[0, :, cols] = dot(z, m_ref[1, :, cols]).astype(BF16)
        g_ref[1, :, cols] = dot(z, m_ref[0, :, cols], TN).astype(BF16)
        g_ref[2, :, cols] = dot(y, wot_ref[:, cols], TN).astype(BF16)

    arrived = sum(sizes[:here])
    order = []
    pair = 0
    for k, size in enumerate(sizes):
        count = chunk_of(size, unit)
        for i in range(size // count):
            order.append((k, i * count, pair, count))
            pair += count

    def copies(k, at, pair, count, slot):
        lin = pl.ds(pair * stride, count * stride)
        rows = pl.ds(2 * pair, 2 * count)
        out = [pltpu.make_async_copy(onm_ref.at[slot, pl.ds(0, count * stride)], onm_hbm.at[lin], sems.at[0, slot])]
        if k < here:
            out.append(
                pltpu.make_async_copy(ow_ref.at[slot, :, pl.ds(0, 2 * count)], ow_hbm.at[:, rows], sems.at[1, slot])
            )
        return out

    group = -1
    for step, (k, at, pair, count) in enumerate(order):
        if group != (k == here):
            group = k == here
            origin = arrived if group else 0
            span = sizes[here] if group else arrived
            for part in range(3):
                g = dot(et_ref[2 * origin : 2 * (origin + span), :], g_ref[part])
                for b in range(heads):
                    gs_ref[part * heads + b, 0 : 2 * span, :] = g[:, b * HD : (b + 1) * HD]
        slot = step % slots
        if step >= slots:
            for copy in copies(*order[step - slots], slot):
                copy.wait()
        natural = slice(2 * pair, 2 * (pair + count))
        local = 2 * (pair - origin)
        mine = pl.ds(role, count, stride=2)
        theirs = pl.ds(1 - role, count, stride=2)
        for q in range(stride):
            part, b = divmod(q, heads)
            cols = slice(b * HD, (b + 1) * HD)
            own = MOMENTUM_DECAY * mom_ref[pl.ds(pair * stride + q, count, stride=stride), :]
            own = own + gs_ref[q, pl.ds(local + role, count, stride=2), :]
            other = gs_ref[q, pl.ds(local + 1 - role, count, stride=2), :]
            if k < here:
                row = q * sizes[k] + at
                other = other + recv_refs[k][row : row + count, :].astype(F32)
            onm_ref[slot, pl.ds(q, count, stride=stride), :] = own
            fs_ref[q, mine, :] = own
            fs_ref[q, theirs, :] = other
            new = w_ref[part, natural, cols].astype(F32) - LEARNING_RATE * fs_ref[q, 0 : 2 * count, :]
            if k < here:
                ow_ref[slot, part, 0 : 2 * count, cols] = new.astype(BF16)
            else:
                base_ref[q, local : local + 2 * count, :] = new
        for copy in copies(k, at, pair, count, slot):
            copy.start()
    for step in range(max(len(order) - slots, 0), len(order)):
        for copy in copies(*order[step], step % slots):
            copy.wait()


def update(place, et, mom, w, received, sizes, rest, unit, heads, sources):
    sizes = [*sizes, rest]
    _, rows, width = w.shape
    stride = 3 * heads
    slots = 4
    return pl.pallas_call(
        functools.partial(update_kernel, heads, unit, sizes),
        in_specs=[SMEM] + [VMEM] * (7 + len(received)),
        out_specs=[HBM, HBM, VMEM],
        out_shape=[
            jax.ShapeDtypeStruct(mom.shape, F32),
            jax.ShapeDtypeStruct(w.shape, BF16),
            pltpu.VMEM((stride, 2 * rest, HD), F32),
        ],
        scratch_shapes=[
            pltpu.VMEM((3, CH, width), BF16),
            pltpu.VMEM((stride, 2 * max(sum(sizes) - rest, rest), HD), F32),
            pltpu.VMEM((stride, 4 * unit, HD), F32),
            pltpu.VMEM((slots, 2 * unit * stride, HD), F32),
            pltpu.VMEM((slots, 3, 4 * unit, width), BF16),
            pltpu.SemaphoreType.DMA((2, slots)),
        ],
        compiler_params=params(16),
        cost_estimate=cost(4 * CH * w.size, 22 * mom.size),
        name="update",
    )(place, et, in_vmem(mom), in_vmem(w), *sources, *received)


def finish_kernel(heads, unit, first, local, place_ref, base_ref, recv_ref, old_hbm, ow_hbm, fs_ref, ow_ref, sems):
    del old_hbm
    stride = base_ref.shape[0]
    size = recv_ref.shape[0] // stride
    role = place_ref[1]
    count = chunk_of(size, unit)
    fs_ref[...] = jnp.zeros_like(fs_ref)
    copies = []
    for step in range(size // count):
        at = 2 * step * count
        for q in range(stride):
            part, b = divmod(q, heads)
            row = q * size + at // 2
            fs_ref[q, pl.ds(1 - role, count, stride=2), :] = recv_ref[row : row + count, :].astype(F32)
            new = base_ref[q, 2 * local + at : 2 * local + at + 2 * count, :] - LEARNING_RATE * fs_ref[q]
            ow_ref[part, at : at + 2 * count, b * HD : (b + 1) * HD] = new.astype(BF16)
        source = ow_ref.at[:, pl.ds(at, 2 * count)]
        target = ow_hbm.at[:, pl.ds(2 * first + at, 2 * count)]
        copies.append(pltpu.make_async_copy(source, target, sems.at[step]))
        copies[-1].start()
    for copy in copies:
        copy.wait()


def finish(place, base, recv, old, first, local, unit, heads):
    stride = base.shape[0]
    size = recv.shape[0] // stride
    count = chunk_of(size, unit)
    return pl.pallas_call(
        functools.partial(finish_kernel, heads, unit, first, local),
        in_specs=[SMEM, VMEM, VMEM, HBM],
        out_specs=HBM,
        out_shape=jax.ShapeDtypeStruct(old.shape, BF16),
        input_output_aliases={3: 0},
        scratch_shapes=[
            pltpu.VMEM((stride, 2 * count, HD), F32),
            pltpu.VMEM((3, 2 * size, heads * HD), BF16),
            pltpu.SemaphoreType.DMA((size // count,)),
        ],
        compiler_params=params(4),
        cost_estimate=cost(2 * recv.size, 14 * recv.size),
        name="finish",
    )(place, in_vmem(base), recv, old)


def exchange(x):
    return lax.ppermute(x, "role", [(0, 1), (1, 0)])


def body(rollout, w_embed, w_qkv, w_out, momentum, rewards, group_ids, timestep):
    seq_count = lax.axis_size("seq")
    seq_index = lax.axis_index("seq")
    role_index = lax.axis_index("role")
    rows_dev = w_qkv.shape[0]
    width = w_qkv.shape[2]
    heads = width // HD
    tok_dev = rollout.shape[1]
    tiles = tok_dev // TILE
    pair_rows = rows_dev // 2

    stride = 3 * heads
    unit = pair_rows // 20
    sizes = (3 * unit, 8 * unit, 6 * unit, 3 * unit)
    mom = momentum.reshape(pair_rows * stride, HD)
    w = w_qkv.transpose(1, 0, 2)
    wot = w_out.T
    place = jnp.stack([seq_index, role_index])

    mine = rollout[0].T
    piece = lead(mom, mine, stride, unit, sizes[0] // unit)
    received = [exchange(piece)]
    mom, piece = lax.optimization_barrier((mom, piece))
    m, et, w, mom, *pieces = prepare(place, w_embed, mom, w, sizes[1:], stride, sizes[0], unit)
    received += [exchange(p) for p in pieces]
    m, received[0] = lax.optimization_barrier((m, received[0]))
    ma, mb = butterfly(m, "seq")

    latent_now, latent_next, head, tail = pick(place, mine, received[0], min(2 * HD, tok_dev))
    left = lax.ppermute(tail, "seq", [(i, i + 1) for i in range(seq_count - 1)])
    right = lax.ppermute(head, "seq", [(i + 1, i) for i in range(seq_count - 1)])

    m, win, e, u, il, partial_pred = forward(place, left, latent_now, right, ma, mb, wot, tiles, heads, seq_count)
    preds = list(butterfly(partial_pred, "mp"))
    preds, received[1] = lax.optimization_barrier((preds, received[1]))
    za, zb = butterfly(
        backward(
            timestep,
            rewards[None],
            group_ids[None],
            win,
            m,
            wot,
            e,
            u,
            il,
            latent_now,
            latent_next,
            preds,
            tiles,
            heads,
            tok_dev * seq_count,
        ),
        "seq",
    )

    rest = sizes[-1]
    nm, nw, base = update(place, et, mom, w, received[:-1], sizes[:-1], rest, unit, heads, [za, zb, m, wot])
    first = sum(sizes) - rest
    nw = finish(place, base, received[-1], nw, first, 0, unit, heads)
    return nm.reshape(momentum.shape), nw.transpose(1, 0, 2)


def solution(mesh):
    in_specs = (
        P("role", "seq", None),
        P(),
        P("seq", None, "mp"),
        P("mp", None),
        P("seq", "role", None, "mp"),
        P(),
        P(),
        P(),
    )
    out_specs = (P("seq", "role", None, "mp"), P("seq", None, "mp"))
    return jax.shard_map(body, mesh=mesh, in_specs=in_specs, out_specs=out_specs, check_vma=False)
```

```python
import functools

import jax
import jax.numpy as jnp
from jax import lax
from jax.experimental import pallas as pl
from jax.experimental.pallas import tpu as pltpu
from jax.sharding import PartitionSpec as P

HD = 128
TILE = 192
STEPS = 50
CH = 64
WINDOW = 640
ONE_LANE = 64
BIAS_LANE = 65
LOW_LANE = 66

SHIFT_FACTOR = 5.0
NOISE_LEVEL = 0.7
MOMENTUM_DECAY = 0.9
LEARNING_RATE = 0.004
LOSS_SCALE = 16384.0
REWARD_FLOOR = 0.1
MASKED = -1e30
LOG2E = 1.4426950408889634

F32 = jnp.float32
BF16 = jnp.bfloat16
NT = (((1,), (1,)), ((), ()))
TN = (((0,), (0,)), ((), ()))
NN = (((1,), (0,)), ((), ()))


VMEM = pl.BlockSpec(memory_space=pltpu.VMEM)
SMEM = pl.BlockSpec(memory_space=pltpu.SMEM)
HBM = pl.BlockSpec(memory_space=pltpu.HBM)
MIB = 1024 * 1024


def in_hbm(x):
    return pltpu.with_memory_space_constraint(x, pltpu.HBM)


def in_vmem(x):
    return pltpu.with_memory_space_constraint(x, pltpu.VMEM)


def params(mib):
    return pltpu.CompilerParams(vmem_limit_bytes=mib * MIB)


def cost(flops, nbytes, exps=0):
    return pl.CostEstimate(flops=flops, bytes_accessed=nbytes, transcendentals=exps)


def dot(a, b, dims=NN):
    return lax.dot_general(a, b, dims, preferred_element_type=F32)


def sigma_at(index, total_steps):
    fraction = index.astype(F32) / total_steps
    return SHIFT_FACTOR * fraction / (1.0 + (SHIFT_FACTOR - 1.0) * fraction)


def advantage_of(rewards, group_ids):
    members = (group_ids == group_ids[:, 0:1]).astype(F32)
    member_total = jnp.sum(members, axis=1, keepdims=True)
    group_mean = jnp.sum(members * rewards, axis=1, keepdims=True) / member_total
    spread = jnp.sqrt(jnp.sum(members * (rewards - group_mean) ** 2, axis=1, keepdims=True) / member_total)
    return (rewards[:, 0:1] - group_mean) / jnp.maximum(spread, REWARD_FLOOR)


def swap(x, axis, bit):
    return lax.ppermute(x, axis, [(i, i ^ bit) for i in range(lax.axis_size(axis))])


def add_kernel(a_ref, b_ref, o_ref):
    o_ref[...] = (a_ref[...].astype(F32) + b_ref[...].astype(F32)).astype(BF16)


def add(a, b):
    return pl.pallas_call(
        add_kernel,
        in_specs=[VMEM, VMEM],
        out_specs=VMEM,
        out_shape=pltpu.VMEM(a.shape, BF16),
        compiler_params=params(4),
        cost_estimate=cost(a.size, 6 * a.size),
        name="add",
    )(a, b)


def butterfly(x, axis):
    bit = 1
    while 2 * bit < lax.axis_size(axis):
        x = add(x, swap(x, axis, bit))
        bit *= 2
    return x, swap(x, axis, bit)


def pick_kernel(place_ref, mine_ref, piece_ref, now_ref, next_ref, head_ref, tail_ref):
    mine = mine_ref[...]
    tok = mine.shape[1]
    start = piece_ref.shape[0] - mine.size // HD
    sampler = place_ref[1] == 0
    spare = head_ref.shape[1]
    for k in range(tok // HD):
        cols = slice(k * HD, (k + 1) * HD)
        own = mine_ref[:, cols].astype(F32)
        other = piece_ref[start + k * CH : start + (k + 1) * CH, :].astype(F32)
        now_ref[:, cols] = jnp.where(sampler, own, other).astype(BF16)
        next_ref[:, cols] = jnp.where(sampler, other, own).astype(BF16)
    head_ref[...] = now_ref[:, :spare]
    tail_ref[...] = now_ref[:, tok - spare :]


def pick(place, mine, piece, spare):
    shape = pltpu.VMEM(mine.shape, BF16)
    edge = pltpu.VMEM((mine.shape[0], spare), BF16)
    return pl.pallas_call(
        pick_kernel,
        in_specs=[SMEM, VMEM, VMEM],
        out_specs=[VMEM] * 4,
        out_shape=[shape, shape, edge, edge],
        compiler_params=params(4),
        cost_estimate=cost(mine.size, 10 * mine.size),
        name="pick",
    )(place, mine, piece)


def chunk_of(size, unit):
    return 2 * unit if size % (2 * unit) == 0 else unit


def narrow(mom_ref, o_ref, stride, first, count, at, size):
    for q in range(stride):
        part = mom_ref[pl.ds(first * stride + q, count, stride=stride), :]
        o_ref[pl.ds(q * size + at, count), :] = (MOMENTUM_DECAY * part).astype(BF16)


def lead_kernel(stride, count, steps, mom_hbm, mine_hbm, o_ref, mom_ref, mine_ref, mine_sem, sems):
    mine_copy = pltpu.make_async_copy(mine_hbm, mine_ref, mine_sem)
    mine_copy.start()
    copies = []
    for k in range(steps):
        rows = pl.ds(k * count * stride, count * stride)
        copies.append(pltpu.make_async_copy(mom_hbm.at[rows], mom_ref.at[rows], sems.at[k]))
        copies[-1].start()
    start = stride * count * steps
    mine_copy.wait()
    for k in range(mine_ref.shape[1] // HD):
        o_ref[start + k * CH : start + (k + 1) * CH, :] = mine_ref[:, k * HD : (k + 1) * HD]
    for k in range(steps):
        copies[k].wait()
        narrow(mom_ref, o_ref, stride, k * count, count, k * count, count * steps)


def lead(mom, mine, stride, count, steps):
    pairs = count * steps
    return pl.pallas_call(
        functools.partial(lead_kernel, stride, count, steps),
        in_specs=[HBM, HBM],
        out_specs=VMEM,
        out_shape=pltpu.VMEM((stride * pairs + mine.size // HD, HD), BF16),
        scratch_shapes=[
            pltpu.VMEM((pairs * stride, HD), F32),
            pltpu.VMEM(mine.shape, BF16),
            pltpu.SemaphoreType.DMA(()),
            pltpu.SemaphoreType.DMA((steps,)),
        ],
        compiler_params=params(4),
        cost_estimate=cost(pairs * stride * HD, 6 * pairs * stride * HD),
        name="lead",
    )(in_hbm(mom), in_hbm(mine))


def prepare_kernel(sizes, stride, skip, unit, sliced, place_ref, e_hbm, mom_hbm, w_hbm, m_ref, et_ref, w_ref, mom_ref, *rest):
    pieces = rest[: len(sizes)]
    e_ref, e_sem, w_sem, mom_sem = rest[len(sizes) :]
    rows = w_ref.shape[1]
    half = rows // 2
    if sliced:
        e_src = e_hbm
    else:
        e_src = e_hbm.at[:, pl.ds(pl.multiple_of(place_ref[0] * rows, HD), rows)]
    e_copy = pltpu.make_async_copy(e_src, e_ref, e_sem)
    e_copy.start()
    w_copies = []
    for m in range(3):
        for k in range(2):
            at = pl.ds(k * half, half)
            w_copies.append(pltpu.make_async_copy(w_hbm.at[m, at], w_ref.at[m, at], w_sem.at[2 * m + k]))
    cuts = [(0, skip, -1, 0)]
    first = skip
    for k, size in enumerate(sizes):
        step = chunk_of(size, unit)
        cuts += [(first + at, step, k, at) for at in range(0, size, step)]
        first += size
    mom_copies = []
    for k, (first, count, _, _) in enumerate(cuts):
        rows = pl.ds(first * stride, count * stride)
        mom_copies.append(pltpu.make_async_copy(mom_hbm.at[rows], mom_ref.at[rows], mom_sem.at[k]))
    for copy in w_copies + mom_copies:
        copy.start()
    e_copy.wait()
    et_ref[...] = e_ref[...].astype(F32).T.astype(BF16)
    for m in range(3):
        w_copies[2 * m].wait()
        w_copies[2 * m + 1].wait()
        m_ref[m] = dot(e_ref[...], w_ref[m]).astype(BF16)
    for (first, count, k, at), copy in zip(cuts, mom_copies):
        copy.wait()
        if k >= 0:
            narrow(mom_ref, pieces[k], stride, first, count, at, sizes[k])


def prepare(place, w_embed, mom, w, sizes, stride, skip, unit):
    _, rows, width = w.shape
    sliced = rows % HD != 0
    if sliced:
        w_embed = lax.dynamic_slice_in_dim(w_embed, place[0] * rows, rows, axis=1)
    return pl.pallas_call(
        functools.partial(prepare_kernel, sizes, stride, skip, unit, sliced),
        in_specs=[SMEM, HBM, HBM, HBM],
        out_specs=[VMEM] * (4 + len(sizes)),
        out_shape=[
            pltpu.VMEM((3, CH, width), BF16),
            pltpu.VMEM((rows, CH), BF16),
            pltpu.VMEM(w.shape, BF16),
            pltpu.VMEM(mom.shape, F32),
        ]
        + [pltpu.VMEM((stride * n, HD), BF16) for n in sizes],
        scratch_shapes=[
            pltpu.VMEM((CH, rows), BF16),
            pltpu.SemaphoreType.DMA(()),
            pltpu.SemaphoreType.DMA((6,)),
            pltpu.SemaphoreType.DMA((1 + sum(sizes) // unit,)),
        ],
        compiler_params=params(4),
        cost_estimate=cost(2 * CH * w.size, 4 * w.size + 10 * mom.size),
        name="prepare",
    )(place, in_hbm(w_embed), in_hbm(mom), in_hbm(w))


def forward_kernel(tiles, heads, ends, *refs):
    place_ref, left_ref, now_ref, right_ref, ma_ref, mb_ref, wot_ref = refs[:7]
    m_ref, win_ref, e_ref, u_ref, il_ref, pred_ref, mk_ref, att_ref, t_ref, s_ref = refs[7:]
    tok = tiles * TILE
    m_ref[...] = (ma_ref[...].astype(F32) + mb_ref[...].astype(F32)).astype(BF16)
    mk_ref[...] = jnp.zeros_like(mk_ref)
    mk_ref[0:CH, :] = m_ref[1]

    spare = left_ref.shape[1]
    left = left_ref[...].astype(F32).T[spare - TILE :]
    now = now_ref[...].astype(F32).T
    right = right_ref[...].astype(F32).T[:TILE]
    blocks = [left] + [now[j * TILE : (j + 1) * TILE] for j in range(tiles)] + [right]
    lane = lax.broadcasted_iota(jnp.int32, (TILE, CH), 1) + CH
    flags = jnp.where((lane == ONE_LANE) | (lane == LOW_LANE), 1.0, 0.0)
    seq = place_ref[0]
    for j in range(tiles):
        for k in range(3):
            extra = flags
            if j + k == 0:
                extra = jnp.where(lane == BIAS_LANE, jnp.where(seq == 0, MASKED, 0.0), flags)
            if j + k == tiles + 1:
                extra = jnp.where(lane == BIAS_LANE, jnp.where(seq == ends, MASKED, 0.0), flags)
            win_ref[j, k * TILE : (k + 1) * TILE, :] = jnp.concatenate([blocks[j + k], extra], axis=1).astype(BF16)
        pad_lane = lax.broadcasted_iota(jnp.int32, (WINDOW - 3 * TILE, HD), 1)
        win_ref[j, 3 * TILE :, :] = jnp.where(pad_lane == BIAS_LANE, MASKED, 0.0).astype(BF16)

    lane = lax.broadcasted_iota(jnp.int32, (tok, HD), 1)
    unit = jnp.where(lane == BIAS_LANE, 1.0, 0.0)
    factor = LOG2E * HD ** (-0.5)
    queries = dot(now.astype(BF16), m_ref[0]).astype(BF16)
    for h in range(heads):
        cols = slice(h * HD, (h + 1) * HD)
        t = (dot(queries[:, cols], mk_ref[:, cols], NT) * factor + unit).astype(BF16)
        for j in range(tiles):
            t_ref[j, h * TILE : (h + 1) * TILE, :] = t[j * TILE : (j + 1) * TILE]
    for j in range(tiles):
        keys = win_ref[j]
        s_ref[...] = dot(t_ref[j], keys, NT)
        for h in range(heads):
            rows = slice(h * TILE, (h + 1) * TILE)
            s = s_ref[rows, :]
            e_ref[j, rows, :] = jnp.exp2(s - jnp.max(s, axis=1, keepdims=True)).astype(BF16)
        u = dot(e_ref[j], keys)
        inv = 1.0 / u[:, ONE_LANE : ONE_LANE + 1]
        u = (u * inv).astype(BF16)
        inv = jnp.broadcast_to(inv, u.shape)
        for h in range(heads):
            rows = slice(h * TILE, (h + 1) * TILE)
            at = slice(h * tok + j * TILE, h * tok + (j + 1) * TILE)
            u_ref[at, :] = u[rows]
            il_ref[at, :] = inv[rows]
    for h in range(heads):
        cols = slice(h * HD, (h + 1) * HD)
        att_ref[:, cols] = dot(u_ref[h * tok : (h + 1) * tok, 0:CH], m_ref[2, :, cols]).astype(BF16)
    pred_ref[...] = dot(wot_ref[...], att_ref[...], NT).astype(BF16)


def forward(place, left, now, right, ma, mb, wot, tiles, heads, seq_count):
    tok = tiles * TILE
    rows = heads * tok
    width = heads * HD
    return pl.pallas_call(
        functools.partial(forward_kernel, tiles, heads, seq_count - 1),
        in_specs=[SMEM] + [VMEM] * 6,
        out_specs=[VMEM] * 6,
        out_shape=[
            pltpu.VMEM((3, CH, width), BF16),
            pltpu.VMEM((tiles, WINDOW, HD), BF16),
            pltpu.VMEM((tiles, heads * TILE, WINDOW), BF16),
            pltpu.VMEM((rows, HD), BF16),
            pltpu.VMEM((rows, HD), F32),
            pltpu.VMEM((CH, tok), BF16),
        ],
        scratch_shapes=[
            pltpu.VMEM((HD, width), BF16),
            pltpu.VMEM((tok, width), BF16),
            pltpu.VMEM((tiles, heads * TILE, HD), BF16),
            pltpu.VMEM((heads * TILE, WINDOW), F32),
        ],
        compiler_params=params(12),
        cost_estimate=cost(rows * (WINDOW + CH) * 4 * HD, 20 * rows * WINDOW, rows * WINDOW),
        name="attend",
    )(place, left, now, right, ma, mb, wot)


def backward_kernel(tiles, heads, tokens_all, *refs):
    (time_ref, rewards_ref, groups_ref, win_ref, m_ref, wot_ref, e_ref, u_ref, il_ref, now_ref, next_ref) = refs[:11]
    pred_refs = refs[11:-6]
    zy_ref, mv_ref, v_ref, t_ref, s_ref, d_ref = refs[-6:]
    tok = tiles * TILE
    mv_ref[...] = jnp.zeros_like(mv_ref)
    mv_ref[0:CH, :] = m_ref[2]
    lane = lax.broadcasted_iota(jnp.int32, (tok, HD), 1)
    scale = HD ** (-0.5)
    advantage = advantage_of(rewards_ref[...], groups_ref[...])
    index = jnp.full((1, 1), time_ref[0], jnp.int32)
    sigma_now = sigma_at(index, STEPS)
    step_size = sigma_at(index - 1, STEPS) - sigma_now
    coefficient = advantage * LOSS_SCALE * (1.0 - sigma_now) / (NOISE_LEVEL**2 * sigma_now * tokens_all)
    pred = pred_refs[0][...].astype(F32)
    for ref in pred_refs[1:]:
        pred = pred + ref[...].astype(F32)
    step_mean = now_ref[...].astype(F32) + step_size * pred
    pg_flat = coefficient * (next_ref[...].astype(F32) - step_mean)
    pg = pg_flat.T.astype(BF16)
    pg_flat = pg_flat.astype(BF16)
    ag_all = dot(pg, wot_ref[...]).astype(BF16)
    for h in range(heads):
        cols = slice(h * HD, (h + 1) * HD)
        rows = slice(h * tok, (h + 1) * tok)
        w = dot(ag_all[:, cols], mv_ref[:, cols], NT).astype(BF16).astype(F32)
        row_dot = jnp.sum(w * u_ref[rows, :].astype(F32), axis=1, keepdims=True)
        factor = scale * il_ref[rows, :]
        w = w * factor
        row_dot = row_dot * factor
        high = row_dot.astype(BF16).astype(F32)
        low = row_dot - high
        w = jnp.where(lane == ONE_LANE, -high, jnp.where(lane == LOW_LANE, -low, w)).astype(BF16)
        for j in range(tiles):
            t_ref[j, h * TILE : (h + 1) * TILE, :] = w[j * TILE : (j + 1) * TILE]
    for j in range(tiles):
        keys = win_ref[j]
        s_ref[...] = dot(t_ref[j], keys, NT)
        for h in range(heads):
            rows = slice(h * TILE, (h + 1) * TILE)
            d_ref[rows, :] = (e_ref[j, rows, :].astype(F32) * s_ref[rows, :]).astype(BF16)
        v = dot(d_ref[...], keys).astype(BF16)
        for h in range(heads):
            v_ref[h * tok + j * TILE : h * tok + (j + 1) * TILE, :] = v[h * TILE : (h + 1) * TILE]
    now = now_ref[...]
    for h in range(heads):
        rows = slice(h * tok, (h + 1) * tok)
        z = dot(now, v_ref[rows, :])
        y = dot(pg_flat, u_ref[rows, :])
        zy_ref[h * CH : (h + 1) * CH, :] = jnp.concatenate([z[:, 0:CH], y[:, 0:CH]], axis=1).astype(BF16)


def backward(timestep, rewards, group_ids, win, m, wot, e, u, il, now, later, preds, tiles, heads, tokens_all):
    width = heads * HD
    return pl.pallas_call(
        functools.partial(backward_kernel, tiles, heads, tokens_all),
        in_specs=[SMEM] + [VMEM] * (10 + len(preds)),
        out_specs=VMEM,
        out_shape=pltpu.VMEM((heads * CH, HD), BF16),
        scratch_shapes=[
            pltpu.VMEM((HD, width), BF16),
            pltpu.VMEM((heads * tiles * TILE, HD), BF16),
            pltpu.VMEM((tiles, heads * TILE, HD), BF16),
            pltpu.VMEM((heads * TILE, WINDOW), F32),
            pltpu.VMEM((heads * TILE, WINDOW), BF16),
        ],
        compiler_params=params(12),
        cost_estimate=cost(width * tiles * TILE * (WINDOW + CH) * 4, 20 * heads * tiles * TILE * WINDOW),
        name="attend_grad",
    )(timestep, rewards, group_ids, win, m, wot, e, u, il, now, later, *preds)


def update_kernel(heads, unit, sizes, *refs):
    place_ref, et_ref, mom_ref, w_ref, za_ref, zb_ref, m_ref, wot_ref = refs[:8]
    here = len(sizes) - 1
    recv_refs = refs[8 : 8 + here]
    onm_hbm, ow_hbm, base_ref, g_ref, gs_ref, fs_ref, onm_ref, ow_ref, sems = refs[8 + here :]
    stride = 3 * heads
    role = place_ref[1]
    slots = onm_ref.shape[0]
    for h in range(heads):
        cols = slice(h * HD, (h + 1) * HD)
        rows = slice(h * CH, (h + 1) * CH)
        zy = (za_ref[rows, :].astype(F32) + zb_ref[rows, :].astype(F32)).astype(BF16)
        z = zy[:, 0:CH]
        y = zy[:, CH : 2 * CH]
        g_ref[0, :, cols] = dot(z, m_ref[1, :, cols]).astype(BF16)
        g_ref[1, :, cols] = dot(z, m_ref[0, :, cols], TN).astype(BF16)
        g_ref[2, :, cols] = dot(y, wot_ref[:, cols], TN).astype(BF16)

    arrived = sum(sizes[:here])
    order = []
    pair = 0
    for k, size in enumerate(sizes):
        count = chunk_of(size, unit)
        for i in range(size // count):
            order.append((k, i * count, pair, count))
            pair += count

    def copies(k, at, pair, count, slot):
        lin = pl.ds(pair * stride, count * stride)
        rows = pl.ds(2 * pair, 2 * count)
        out = [pltpu.make_async_copy(onm_ref.at[slot, pl.ds(0, count * stride)], onm_hbm.at[lin], sems.at[0, slot])]
        if k < here:
            out.append(
                pltpu.make_async_copy(ow_ref.at[slot, :, pl.ds(0, 2 * count)], ow_hbm.at[:, rows], sems.at[1, slot])
            )
        return out

    group = -1
    for step, (k, at, pair, count) in enumerate(order):
        if group != (k == here):
            group = k == here
            origin = arrived if group else 0
            span = sizes[here] if group else arrived
            for part in range(3):
                g = dot(et_ref[2 * origin : 2 * (origin + span), :], g_ref[part])
                for b in range(heads):
                    gs_ref[part * heads + b, 0 : 2 * span, :] = g[:, b * HD : (b + 1) * HD]
        slot = step % slots
        if step >= slots:
            for copy in copies(*order[step - slots], slot):
                copy.wait()
        natural = slice(2 * pair, 2 * (pair + count))
        local = 2 * (pair - origin)
        mine = pl.ds(role, count, stride=2)
        theirs = pl.ds(1 - role, count, stride=2)
        for q in range(stride):
            part, b = divmod(q, heads)
            cols = slice(b * HD, (b + 1) * HD)
            own = MOMENTUM_DECAY * mom_ref[pl.ds(pair * stride + q, count, stride=stride), :]
            own = own + gs_ref[q, pl.ds(local + role, count, stride=2), :]
            other = gs_ref[q, pl.ds(local + 1 - role, count, stride=2), :]
            if k < here:
                row = q * sizes[k] + at
                other = other + recv_refs[k][row : row + count, :].astype(F32)
            onm_ref[slot, pl.ds(q, count, stride=stride), :] = own
            fs_ref[q, mine, :] = own
            fs_ref[q, theirs, :] = other
            new = w_ref[part, natural, cols].astype(F32) - LEARNING_RATE * fs_ref[q, 0 : 2 * count, :]
            if k < here:
                ow_ref[slot, part, 0 : 2 * count, cols] = new.astype(BF16)
            else:
                base_ref[q, local : local + 2 * count, :] = new
        for copy in copies(k, at, pair, count, slot):
            copy.start()
    for step in range(max(len(order) - slots, 0), len(order)):
        for copy in copies(*order[step], step % slots):
            copy.wait()


def update(place, et, mom, w, received, sizes, rest, unit, heads, sources):
    sizes = [*sizes, rest]
    _, rows, width = w.shape
    stride = 3 * heads
    slots = 4
    return pl.pallas_call(
        functools.partial(update_kernel, heads, unit, sizes),
        in_specs=[SMEM] + [VMEM] * (7 + len(received)),
        out_specs=[HBM, HBM, VMEM],
        out_shape=[
            jax.ShapeDtypeStruct(mom.shape, F32),
            jax.ShapeDtypeStruct(w.shape, BF16),
            pltpu.VMEM((stride, 2 * rest, HD), F32),
        ],
        scratch_shapes=[
            pltpu.VMEM((3, CH, width), BF16),
            pltpu.VMEM((stride, 2 * max(sum(sizes) - rest, rest), HD), F32),
            pltpu.VMEM((stride, 4 * unit, HD), F32),
            pltpu.VMEM((slots, 2 * unit * stride, HD), F32),
            pltpu.VMEM((slots, 3, 4 * unit, width), BF16),
            pltpu.SemaphoreType.DMA((2, slots)),
        ],
        compiler_params=params(16),
        cost_estimate=cost(4 * CH * w.size, 22 * mom.size),
        name="update",
    )(place, et, in_vmem(mom), in_vmem(w), *sources, *received)


def finish_kernel(heads, unit, first, local, place_ref, base_ref, recv_ref, old_hbm, ow_hbm, fs_ref, ow_ref, sems):
    del old_hbm
    stride = base_ref.shape[0]
    size = recv_ref.shape[0] // stride
    role = place_ref[1]
    count = chunk_of(size, unit)
    fs_ref[...] = jnp.zeros_like(fs_ref)
    copies = []
    for step in range(size // count):
        at = 2 * step * count
        for q in range(stride):
            part, b = divmod(q, heads)
            row = q * size + at // 2
            fs_ref[q, pl.ds(1 - role, count, stride=2), :] = recv_ref[row : row + count, :].astype(F32)
            new = base_ref[q, 2 * local + at : 2 * local + at + 2 * count, :] - LEARNING_RATE * fs_ref[q]
            ow_ref[part, at : at + 2 * count, b * HD : (b + 1) * HD] = new.astype(BF16)
        source = ow_ref.at[:, pl.ds(at, 2 * count)]
        target = ow_hbm.at[:, pl.ds(2 * first + at, 2 * count)]
        copies.append(pltpu.make_async_copy(source, target, sems.at[step]))
        copies[-1].start()
    for copy in copies:
        copy.wait()


def finish(place, base, recv, old, first, local, unit, heads):
    stride = base.shape[0]
    size = recv.shape[0] // stride
    count = chunk_of(size, unit)
    return pl.pallas_call(
        functools.partial(finish_kernel, heads, unit, first, local),
        in_specs=[SMEM, VMEM, VMEM, HBM],
        out_specs=HBM,
        out_shape=jax.ShapeDtypeStruct(old.shape, BF16),
        input_output_aliases={3: 0},
        scratch_shapes=[
            pltpu.VMEM((stride, 2 * count, HD), F32),
            pltpu.VMEM((3, 2 * size, heads * HD), BF16),
            pltpu.SemaphoreType.DMA((size // count,)),
        ],
        compiler_params=params(4),
        cost_estimate=cost(2 * recv.size, 14 * recv.size),
        name="finish",
    )(place, in_vmem(base), recv, old)


def exchange(x):
    return lax.ppermute(x, "role", [(0, 1), (1, 0)])


def body(rollout, w_embed, w_qkv, w_out, momentum, rewards, group_ids, timestep):
    seq_count = lax.axis_size("seq")
    seq_index = lax.axis_index("seq")
    role_index = lax.axis_index("role")
    rows_dev = w_qkv.shape[0]
    width = w_qkv.shape[2]
    heads = width // HD
    tok_dev = rollout.shape[1]
    tiles = tok_dev // TILE
    pair_rows = rows_dev // 2

    stride = 3 * heads
    unit = pair_rows // 20
    sizes = (3 * unit, 6 * unit, 6 * unit, 4 * unit, unit)
    mom = momentum.reshape(pair_rows * stride, HD)
    w = w_qkv.transpose(1, 0, 2)
    wot = w_out.T
    place = jnp.stack([seq_index, role_index])

    mine = rollout[0].T
    piece = lead(mom, mine, stride, unit, sizes[0] // unit)
    received = [exchange(piece)]
    mom, piece = lax.optimization_barrier((mom, piece))
    m, et, w, mom, *pieces = prepare(place, w_embed, mom, w, sizes[1:], stride, sizes[0], unit)
    received += [exchange(p) for p in pieces[:-1]]
    m, received[0] = lax.optimization_barrier((m, received[0]))
    ma, mb = butterfly(m, "seq")

    latent_now, latent_next, head, tail = pick(place, mine, received[0], min(2 * HD, tok_dev))
    left = lax.ppermute(tail, "seq", [(i, i + 1) for i in range(seq_count - 1)])
    right = lax.ppermute(head, "seq", [(i + 1, i) for i in range(seq_count - 1)])

    m, win, e, u, il, partial_pred = forward(place, left, latent_now, right, ma, mb, wot, tiles, heads, seq_count)
    preds = list(butterfly(partial_pred, "mp"))
    preds, received[1] = lax.optimization_barrier((preds, received[1]))
    za, zb = butterfly(
        backward(
            timestep,
            rewards[None],
            group_ids[None],
            win,
            m,
            wot,
            e,
            u,
            il,
            latent_now,
            latent_next,
            preds,
            tiles,
            heads,
            tok_dev * seq_count,
        ),
        "seq",
    )

    zb, last = lax.optimization_barrier((zb, pieces[-1]))
    received.append(exchange(last))
    rest = sizes[-2] + sizes[-1]
    nm, nw, base = update(place, et, mom, w, received[:-2], sizes[:-2], rest, unit, heads, [za, zb, m, wot])
    first = sum(sizes) - rest
    nw = finish(place, base, received[-2], nw, first, 0, unit, heads)
    nw = finish(place, base, received[-1], nw, first + sizes[-2], sizes[-2], unit, heads)
    return nm.reshape(momentum.shape), nw.transpose(1, 0, 2)


def solution(mesh):
    in_specs = (
        P("role", "seq", None),
        P(),
        P("seq", None, "mp"),
        P("mp", None),
        P("seq", "role", None, "mp"),
        P(),
        P(),
        P(),
    )
    out_specs = (P("seq", "role", None, "mp"), P("seq", None, "mp"))
    return jax.shard_map(body, mesh=mesh, in_specs=in_specs, out_specs=out_specs, check_vma=False)
```

```python
import functools

import jax
import jax.numpy as jnp
from jax import lax
from jax.experimental import pallas as pl
from jax.experimental.pallas import tpu as pltpu
from jax.sharding import PartitionSpec as P

HD = 128
TILE = 192
STEPS = 50
CH = 64
WINDOW = 640
ONE_LANE = 64
BIAS_LANE = 65
LOW_LANE = 66

SHIFT_FACTOR = 5.0
NOISE_LEVEL = 0.7
MOMENTUM_DECAY = 0.9
LEARNING_RATE = 0.004
LOSS_SCALE = 16384.0
REWARD_FLOOR = 0.1
MASKED = -1e30
LOG2E = 1.4426950408889634

F32 = jnp.float32
BF16 = jnp.bfloat16
NT = (((1,), (1,)), ((), ()))
TN = (((0,), (0,)), ((), ()))
NN = (((1,), (0,)), ((), ()))


VMEM = pl.BlockSpec(memory_space=pltpu.VMEM)
SMEM = pl.BlockSpec(memory_space=pltpu.SMEM)
HBM = pl.BlockSpec(memory_space=pltpu.HBM)
MIB = 1024 * 1024


def in_hbm(x):
    return pltpu.with_memory_space_constraint(x, pltpu.HBM)


def in_vmem(x):
    return pltpu.with_memory_space_constraint(x, pltpu.VMEM)


def params(mib):
    return pltpu.CompilerParams(vmem_limit_bytes=mib * MIB)


def cost(flops, nbytes, exps=0):
    return pl.CostEstimate(flops=flops, bytes_accessed=nbytes, transcendentals=exps)


def dot(a, b, dims=NN):
    return lax.dot_general(a, b, dims, preferred_element_type=F32)


def sigma_at(index, total_steps):
    fraction = index.astype(F32) / total_steps
    return SHIFT_FACTOR * fraction / (1.0 + (SHIFT_FACTOR - 1.0) * fraction)


def advantage_of(rewards, group_ids):
    members = (group_ids == group_ids[:, 0:1]).astype(F32)
    member_total = jnp.sum(members, axis=1, keepdims=True)
    group_mean = jnp.sum(members * rewards, axis=1, keepdims=True) / member_total
    spread = jnp.sqrt(jnp.sum(members * (rewards - group_mean) ** 2, axis=1, keepdims=True) / member_total)
    return (rewards[:, 0:1] - group_mean) / jnp.maximum(spread, REWARD_FLOOR)


def swap(x, axis, bit):
    return lax.ppermute(x, axis, [(i, i ^ bit) for i in range(lax.axis_size(axis))])


def add_kernel(a_ref, b_ref, o_ref):
    o_ref[...] = (a_ref[...].astype(F32) + b_ref[...].astype(F32)).astype(BF16)


def add(a, b):
    return pl.pallas_call(
        add_kernel,
        in_specs=[VMEM, VMEM],
        out_specs=VMEM,
        out_shape=pltpu.VMEM(a.shape, BF16),
        compiler_params=params(4),
        cost_estimate=cost(a.size, 6 * a.size),
        name="add",
    )(a, b)


def butterfly(x, axis):
    bit = 1
    while 2 * bit < lax.axis_size(axis):
        x = add(x, swap(x, axis, bit))
        bit *= 2
    return x, swap(x, axis, bit)


def pick_kernel(place_ref, mine_ref, piece_ref, now_ref, next_ref, head_ref, tail_ref):
    mine = mine_ref[...]
    tok = mine.shape[1]
    start = piece_ref.shape[0] - mine.size // HD
    sampler = place_ref[1] == 0
    spare = head_ref.shape[1]
    for k in range(tok // HD):
        cols = slice(k * HD, (k + 1) * HD)
        own = mine_ref[:, cols].astype(F32)
        other = piece_ref[start + k * CH : start + (k + 1) * CH, :].astype(F32)
        now_ref[:, cols] = jnp.where(sampler, own, other).astype(BF16)
        next_ref[:, cols] = jnp.where(sampler, other, own).astype(BF16)
    head_ref[...] = now_ref[:, :spare]
    tail_ref[...] = now_ref[:, tok - spare :]


def pick(place, mine, piece, spare):
    shape = pltpu.VMEM(mine.shape, BF16)
    edge = pltpu.VMEM((mine.shape[0], spare), BF16)
    return pl.pallas_call(
        pick_kernel,
        in_specs=[SMEM, VMEM, VMEM],
        out_specs=[VMEM] * 4,
        out_shape=[shape, shape, edge, edge],
        compiler_params=params(4),
        cost_estimate=cost(mine.size, 10 * mine.size),
        name="pick",
    )(place, mine, piece)


def chunk_of(size, unit):
    return 2 * unit if size % (2 * unit) == 0 else unit


def narrow(mom_ref, o_ref, stride, first, count, at, size):
    for q in range(stride):
        part = mom_ref[pl.ds(first * stride + q, count, stride=stride), :]
        o_ref[pl.ds(q * size + at, count), :] = (MOMENTUM_DECAY * part).astype(BF16)


def lead_kernel(stride, count, steps, mom_hbm, mine_hbm, o_ref, mom_ref, mine_ref, mine_sem, sems):
    mine_copy = pltpu.make_async_copy(mine_hbm, mine_ref, mine_sem)
    mine_copy.start()
    copies = []
    for k in range(steps):
        rows = pl.ds(k * count * stride, count * stride)
        copies.append(pltpu.make_async_copy(mom_hbm.at[rows], mom_ref.at[rows], sems.at[k]))
        copies[-1].start()
    start = stride * count * steps
    mine_copy.wait()
    for k in range(mine_ref.shape[1] // HD):
        o_ref[start + k * CH : start + (k + 1) * CH, :] = mine_ref[:, k * HD : (k + 1) * HD]
    for k in range(steps):
        copies[k].wait()
        narrow(mom_ref, o_ref, stride, k * count, count, k * count, count * steps)


def lead(mom, mine, stride, count, steps):
    pairs = count * steps
    return pl.pallas_call(
        functools.partial(lead_kernel, stride, count, steps),
        in_specs=[HBM, HBM],
        out_specs=VMEM,
        out_shape=pltpu.VMEM((stride * pairs + mine.size // HD, HD), BF16),
        scratch_shapes=[
            pltpu.VMEM((pairs * stride, HD), F32),
            pltpu.VMEM(mine.shape, BF16),
            pltpu.SemaphoreType.DMA(()),
            pltpu.SemaphoreType.DMA((steps,)),
        ],
        compiler_params=params(4),
        cost_estimate=cost(pairs * stride * HD, 6 * pairs * stride * HD),
        name="lead",
    )(in_hbm(mom), in_hbm(mine))


def prepare_kernel(sizes, stride, skip, unit, sliced, place_ref, e_hbm, mom_hbm, w_hbm, m_ref, et_ref, w_ref, mom_ref, *rest):
    pieces = rest[: len(sizes)]
    e_ref, e_sem, w_sem, mom_sem = rest[len(sizes) :]
    rows = w_ref.shape[1]
    half = rows // 2
    if sliced:
        e_src = e_hbm
    else:
        e_src = e_hbm.at[:, pl.ds(pl.multiple_of(place_ref[0] * rows, HD), rows)]
    e_copy = pltpu.make_async_copy(e_src, e_ref, e_sem)
    e_copy.start()
    w_copies = []
    for m in range(3):
        for k in range(2):
            at = pl.ds(k * half, half)
            w_copies.append(pltpu.make_async_copy(w_hbm.at[m, at], w_ref.at[m, at], w_sem.at[2 * m + k]))
    cuts = [(0, skip, -1, 0)]
    first = skip
    for k, size in enumerate(sizes):
        step = chunk_of(size, unit)
        cuts += [(first + at, step, k, at) for at in range(0, size, step)]
        first += size
    mom_copies = []
    for k, (first, count, _, _) in enumerate(cuts):
        rows = pl.ds(first * stride, count * stride)
        mom_copies.append(pltpu.make_async_copy(mom_hbm.at[rows], mom_ref.at[rows], mom_sem.at[k]))
    for copy in w_copies + mom_copies:
        copy.start()
    e_copy.wait()
    et_ref[...] = e_ref[...].astype(F32).T.astype(BF16)
    for m in range(3):
        w_copies[2 * m].wait()
        w_copies[2 * m + 1].wait()
        m_ref[m] = dot(e_ref[...], w_ref[m]).astype(BF16)
    for (first, count, k, at), copy in zip(cuts, mom_copies):
        copy.wait()
        if k >= 0:
            narrow(mom_ref, pieces[k], stride, first, count, at, sizes[k])


def prepare(place, w_embed, mom, w, sizes, stride, skip, unit):
    _, rows, width = w.shape
    sliced = rows % HD != 0
    if sliced:
        w_embed = lax.dynamic_slice_in_dim(w_embed, place[0] * rows, rows, axis=1)
    return pl.pallas_call(
        functools.partial(prepare_kernel, sizes, stride, skip, unit, sliced),
        in_specs=[SMEM, HBM, HBM, HBM],
        out_specs=[VMEM] * (4 + len(sizes)),
        out_shape=[
            pltpu.VMEM((3, CH, width), BF16),
            pltpu.VMEM((rows, CH), BF16),
            pltpu.VMEM(w.shape, BF16),
            pltpu.VMEM(mom.shape, F32),
        ]
        + [pltpu.VMEM((stride * n, HD), BF16) for n in sizes],
        scratch_shapes=[
            pltpu.VMEM((CH, rows), BF16),
            pltpu.SemaphoreType.DMA(()),
            pltpu.SemaphoreType.DMA((6,)),
            pltpu.SemaphoreType.DMA((1 + sum(sizes) // unit,)),
        ],
        compiler_params=params(4),
        cost_estimate=cost(2 * CH * w.size, 4 * w.size + 10 * mom.size),
        name="prepare",
    )(place, in_hbm(w_embed), in_hbm(mom), in_hbm(w))


def forward_kernel(tiles, heads, ends, *refs):
    place_ref, left_ref, now_ref, right_ref, ma_ref, mb_ref, wot_ref = refs[:7]
    m_ref, win_ref, e_ref, u_ref, il_ref, pred_ref, mk_ref, att_ref, t_ref, s_ref = refs[7:]
    tok = tiles * TILE
    m_ref[...] = (ma_ref[...].astype(F32) + mb_ref[...].astype(F32)).astype(BF16)
    mk_ref[...] = jnp.zeros_like(mk_ref)
    mk_ref[0:CH, :] = m_ref[1]

    spare = left_ref.shape[1]
    left = left_ref[...].astype(F32).T[spare - TILE :]
    now = now_ref[...].astype(F32).T
    right = right_ref[...].astype(F32).T[:TILE]
    blocks = [left] + [now[j * TILE : (j + 1) * TILE] for j in range(tiles)] + [right]
    lane = lax.broadcasted_iota(jnp.int32, (TILE, CH), 1) + CH
    flags = jnp.where((lane == ONE_LANE) | (lane == LOW_LANE), 1.0, 0.0)
    seq = place_ref[0]
    for j in range(tiles):
        for k in range(3):
            extra = flags
            if j + k == 0:
                extra = jnp.where(lane == BIAS_LANE, jnp.where(seq == 0, MASKED, 0.0), flags)
            if j + k == tiles + 1:
                extra = jnp.where(lane == BIAS_LANE, jnp.where(seq == ends, MASKED, 0.0), flags)
            win_ref[j, k * TILE : (k + 1) * TILE, :] = jnp.concatenate([blocks[j + k], extra], axis=1).astype(BF16)
        pad_lane = lax.broadcasted_iota(jnp.int32, (WINDOW - 3 * TILE, HD), 1)
        win_ref[j, 3 * TILE :, :] = jnp.where(pad_lane == BIAS_LANE, MASKED, 0.0).astype(BF16)

    lane = lax.broadcasted_iota(jnp.int32, (tok, HD), 1)
    unit = jnp.where(lane == BIAS_LANE, 1.0, 0.0)
    factor = LOG2E * HD ** (-0.5)
    queries = dot(now.astype(BF16), m_ref[0]).astype(BF16)
    for h in range(heads):
        cols = slice(h * HD, (h + 1) * HD)
        t = (dot(queries[:, cols], mk_ref[:, cols], NT) * factor + unit).astype(BF16)
        for j in range(tiles):
            t_ref[j, h * TILE : (h + 1) * TILE, :] = t[j * TILE : (j + 1) * TILE]
    for j in range(tiles):
        keys = win_ref[j]
        s_ref[...] = dot(t_ref[j], keys, NT)
        for h in range(heads):
            rows = slice(h * TILE, (h + 1) * TILE)
            s = s_ref[rows, :]
            e_ref[j, rows, :] = jnp.exp2(s - jnp.max(s, axis=1, keepdims=True)).astype(BF16)
        u = dot(e_ref[j], keys)
        inv = 1.0 / u[:, ONE_LANE : ONE_LANE + 1]
        u = (u * inv).astype(BF16)
        inv = jnp.broadcast_to(inv, u.shape)
        for h in range(heads):
            rows = slice(h * TILE, (h + 1) * TILE)
            at = slice(h * tok + j * TILE, h * tok + (j + 1) * TILE)
            u_ref[at, :] = u[rows]
            il_ref[at, :] = inv[rows]
    for h in range(heads):
        cols = slice(h * HD, (h + 1) * HD)
        att_ref[:, cols] = dot(u_ref[h * tok : (h + 1) * tok, 0:CH], m_ref[2, :, cols]).astype(BF16)
    pred_ref[...] = dot(wot_ref[...], att_ref[...], NT).astype(BF16)


def forward(place, left, now, right, ma, mb, wot, tiles, heads, seq_count):
    tok = tiles * TILE
    rows = heads * tok
    width = heads * HD
    return pl.pallas_call(
        functools.partial(forward_kernel, tiles, heads, seq_count - 1),
        in_specs=[SMEM] + [VMEM] * 6,
        out_specs=[VMEM] * 6,
        out_shape=[
            pltpu.VMEM((3, CH, width), BF16),
            pltpu.VMEM((tiles, WINDOW, HD), BF16),
            pltpu.VMEM((tiles, heads * TILE, WINDOW), BF16),
            pltpu.VMEM((rows, HD), BF16),
            pltpu.VMEM((rows, HD), F32),
            pltpu.VMEM((CH, tok), BF16),
        ],
        scratch_shapes=[
            pltpu.VMEM((HD, width), BF16),
            pltpu.VMEM((tok, width), BF16),
            pltpu.VMEM((tiles, heads * TILE, HD), BF16),
            pltpu.VMEM((heads * TILE, WINDOW), F32),
        ],
        compiler_params=params(12),
        cost_estimate=cost(rows * (WINDOW + CH) * 4 * HD, 20 * rows * WINDOW, rows * WINDOW),
        name="attend",
    )(place, left, now, right, ma, mb, wot)


def backward_kernel(tiles, heads, tokens_all, *refs):
    (time_ref, rewards_ref, groups_ref, win_ref, m_ref, wot_ref, e_ref, u_ref, il_ref, now_ref, next_ref) = refs[:11]
    pred_refs = refs[11:-6]
    zy_ref, mv_ref, v_ref, t_ref, s_ref, d_ref = refs[-6:]
    tok = tiles * TILE
    mv_ref[...] = jnp.zeros_like(mv_ref)
    mv_ref[0:CH, :] = m_ref[2]
    lane = lax.broadcasted_iota(jnp.int32, (tok, HD), 1)
    scale = HD ** (-0.5)
    advantage = advantage_of(rewards_ref[...], groups_ref[...])
    index = jnp.full((1, 1), time_ref[0], jnp.int32)
    sigma_now = sigma_at(index, STEPS)
    step_size = sigma_at(index - 1, STEPS) - sigma_now
    coefficient = advantage * LOSS_SCALE * (1.0 - sigma_now) / (NOISE_LEVEL**2 * sigma_now * tokens_all)
    pred = pred_refs[0][...].astype(F32)
    for ref in pred_refs[1:]:
        pred = pred + ref[...].astype(F32)
    step_mean = now_ref[...].astype(F32) + step_size * pred
    pg_flat = coefficient * (next_ref[...].astype(F32) - step_mean)
    pg = pg_flat.T.astype(BF16)
    pg_flat = pg_flat.astype(BF16)
    ag_all = dot(pg, wot_ref[...]).astype(BF16)
    for h in range(heads):
        cols = slice(h * HD, (h + 1) * HD)
        rows = slice(h * tok, (h + 1) * tok)
        w = dot(ag_all[:, cols], mv_ref[:, cols], NT).astype(BF16).astype(F32)
        row_dot = jnp.sum(w * u_ref[rows, :].astype(F32), axis=1, keepdims=True)
        factor = scale * il_ref[rows, :]
        w = w * factor
        row_dot = row_dot * factor
        high = row_dot.astype(BF16).astype(F32)
        low = row_dot - high
        w = jnp.where(lane == ONE_LANE, -high, jnp.where(lane == LOW_LANE, -low, w)).astype(BF16)
        for j in range(tiles):
            t_ref[j, h * TILE : (h + 1) * TILE, :] = w[j * TILE : (j + 1) * TILE]
    for j in range(tiles):
        keys = win_ref[j]
        s_ref[...] = dot(t_ref[j], keys, NT)
        for h in range(heads):
            rows = slice(h * TILE, (h + 1) * TILE)
            d_ref[rows, :] = (e_ref[j, rows, :].astype(F32) * s_ref[rows, :]).astype(BF16)
        v = dot(d_ref[...], keys).astype(BF16)
        for h in range(heads):
            v_ref[h * tok + j * TILE : h * tok + (j + 1) * TILE, :] = v[h * TILE : (h + 1) * TILE]
    now = now_ref[...]
    for h in range(heads):
        rows = slice(h * tok, (h + 1) * tok)
        z = dot(now, v_ref[rows, :])
        y = dot(pg_flat, u_ref[rows, :])
        zy_ref[h * CH : (h + 1) * CH, :] = jnp.concatenate([z[:, 0:CH], y[:, 0:CH]], axis=1).astype(BF16)


def backward(timestep, rewards, group_ids, win, m, wot, e, u, il, now, later, preds, tiles, heads, tokens_all):
    width = heads * HD
    return pl.pallas_call(
        functools.partial(backward_kernel, tiles, heads, tokens_all),
        in_specs=[SMEM] + [VMEM] * (10 + len(preds)),
        out_specs=VMEM,
        out_shape=pltpu.VMEM((heads * CH, HD), BF16),
        scratch_shapes=[
            pltpu.VMEM((HD, width), BF16),
            pltpu.VMEM((heads * tiles * TILE, HD), BF16),
            pltpu.VMEM((tiles, heads * TILE, HD), BF16),
            pltpu.VMEM((heads * TILE, WINDOW), F32),
            pltpu.VMEM((heads * TILE, WINDOW), BF16),
        ],
        compiler_params=params(12),
        cost_estimate=cost(width * tiles * TILE * (WINDOW + CH) * 4, 20 * heads * tiles * TILE * WINDOW),
        name="attend_grad",
    )(timestep, rewards, group_ids, win, m, wot, e, u, il, now, later, *preds)


def update_kernel(heads, unit, sizes, *refs):
    place_ref, et_ref, mom_ref, w_ref, za_ref, zb_ref, m_ref, wot_ref = refs[:8]
    here = len(sizes) - 1
    recv_refs = refs[8 : 8 + here]
    onm_hbm, ow_hbm, base_ref, g_ref, gs_ref, fs_ref, onm_ref, ow_ref, sems = refs[8 + here :]
    stride = 3 * heads
    role = place_ref[1]
    slots = onm_ref.shape[0]
    for h in range(heads):
        cols = slice(h * HD, (h + 1) * HD)
        rows = slice(h * CH, (h + 1) * CH)
        zy = (za_ref[rows, :].astype(F32) + zb_ref[rows, :].astype(F32)).astype(BF16)
        z = zy[:, 0:CH]
        y = zy[:, CH : 2 * CH]
        g_ref[0, :, cols] = dot(z, m_ref[1, :, cols]).astype(BF16)
        g_ref[1, :, cols] = dot(z, m_ref[0, :, cols], TN).astype(BF16)
        g_ref[2, :, cols] = dot(y, wot_ref[:, cols], TN).astype(BF16)

    arrived = sum(sizes[:here])
    order = []
    pair = 0
    for k, size in enumerate(sizes):
        count = chunk_of(size, unit)
        for i in range(size // count):
            order.append((k, i * count, pair, count))
            pair += count

    def copies(k, at, pair, count, slot):
        lin = pl.ds(pair * stride, count * stride)
        rows = pl.ds(2 * pair, 2 * count)
        out = [pltpu.make_async_copy(onm_ref.at[slot, pl.ds(0, count * stride)], onm_hbm.at[lin], sems.at[0, slot])]
        if k < here:
            out.append(
                pltpu.make_async_copy(ow_ref.at[slot, :, pl.ds(0, 2 * count)], ow_hbm.at[:, rows], sems.at[1, slot])
            )
        return out

    group = -1
    for step, (k, at, pair, count) in enumerate(order):
        if group != (k == here):
            group = k == here
            origin = arrived if group else 0
            span = sizes[here] if group else arrived
            for part in range(3):
                g = dot(et_ref[2 * origin : 2 * (origin + span), :], g_ref[part])
                for b in range(heads):
                    gs_ref[part * heads + b, 0 : 2 * span, :] = g[:, b * HD : (b + 1) * HD]
        slot = step % slots
        if step >= slots:
            for copy in copies(*order[step - slots], slot):
                copy.wait()
        natural = slice(2 * pair, 2 * (pair + count))
        local = 2 * (pair - origin)
        mine = pl.ds(role, count, stride=2)
        theirs = pl.ds(1 - role, count, stride=2)
        for q in range(stride):
            part, b = divmod(q, heads)
            cols = slice(b * HD, (b + 1) * HD)
            own = MOMENTUM_DECAY * mom_ref[pl.ds(pair * stride + q, count, stride=stride), :]
            own = own + gs_ref[q, pl.ds(local + role, count, stride=2), :]
            other = gs_ref[q, pl.ds(local + 1 - role, count, stride=2), :]
            if k < here:
                row = q * sizes[k] + at
                other = other + recv_refs[k][row : row + count, :].astype(F32)
            onm_ref[slot, pl.ds(q, count, stride=stride), :] = own
            fs_ref[q, mine, :] = own
            fs_ref[q, theirs, :] = other
            new = w_ref[part, natural, cols].astype(F32) - LEARNING_RATE * fs_ref[q, 0 : 2 * count, :]
            if k < here:
                ow_ref[slot, part, 0 : 2 * count, cols] = new.astype(BF16)
            else:
                base_ref[q, local : local + 2 * count, :] = new
        for copy in copies(k, at, pair, count, slot):
            copy.start()
    for step in range(max(len(order) - slots, 0), len(order)):
        for copy in copies(*order[step], step % slots):
            copy.wait()


def update(place, et, mom, w, received, sizes, rest, unit, heads, sources):
    sizes = [*sizes, rest]
    _, rows, width = w.shape
    stride = 3 * heads
    slots = 4
    return pl.pallas_call(
        functools.partial(update_kernel, heads, unit, sizes),
        in_specs=[SMEM] + [VMEM] * (7 + len(received)),
        out_specs=[HBM, HBM, VMEM],
        out_shape=[
            jax.ShapeDtypeStruct(mom.shape, F32),
            jax.ShapeDtypeStruct(w.shape, BF16),
            pltpu.VMEM((stride, 2 * rest, HD), F32),
        ],
        scratch_shapes=[
            pltpu.VMEM((3, CH, width), BF16),
            pltpu.VMEM((stride, 2 * max(sum(sizes) - rest, rest), HD), F32),
            pltpu.VMEM((stride, 4 * unit, HD), F32),
            pltpu.VMEM((slots, 2 * unit * stride, HD), F32),
            pltpu.VMEM((slots, 3, 4 * unit, width), BF16),
            pltpu.SemaphoreType.DMA((2, slots)),
        ],
        compiler_params=params(16),
        cost_estimate=cost(4 * CH * w.size, 22 * mom.size),
        name="update",
    )(place, et, in_vmem(mom), in_vmem(w), *sources, *received)


def finish_kernel(heads, unit, first, local, place_ref, base_ref, recv_ref, old_hbm, ow_hbm, fs_ref, ow_ref, sems):
    del old_hbm
    stride = base_ref.shape[0]
    size = recv_ref.shape[0] // stride
    role = place_ref[1]
    count = chunk_of(size, unit)
    fs_ref[...] = jnp.zeros_like(fs_ref)
    copies = []
    for step in range(size // count):
        at = 2 * step * count
        for q in range(stride):
            part, b = divmod(q, heads)
            row = q * size + at // 2
            fs_ref[q, pl.ds(1 - role, count, stride=2), :] = recv_ref[row : row + count, :].astype(F32)
            new = base_ref[q, 2 * local + at : 2 * local + at + 2 * count, :] - LEARNING_RATE * fs_ref[q]
            ow_ref[part, at : at + 2 * count, b * HD : (b + 1) * HD] = new.astype(BF16)
            if b == heads - 1:
                source = ow_ref.at[part, pl.ds(at, 2 * count)]
                target = ow_hbm.at[part, pl.ds(2 * first + at, 2 * count)]
                copies.append(pltpu.make_async_copy(source, target, sems.at[3 * step + part]))
                copies[-1].start()
    for copy in copies:
        copy.wait()


def finish(place, base, recv, old, first, local, unit, heads):
    stride = base.shape[0]
    size = recv.shape[0] // stride
    count = chunk_of(size, unit)
    return pl.pallas_call(
        functools.partial(finish_kernel, heads, unit, first, local),
        in_specs=[SMEM, VMEM, VMEM, HBM],
        out_specs=HBM,
        out_shape=jax.ShapeDtypeStruct(old.shape, BF16),
        input_output_aliases={3: 0},
        scratch_shapes=[
            pltpu.VMEM((stride, 2 * count, HD), F32),
            pltpu.VMEM((3, 2 * size, heads * HD), BF16),
            pltpu.SemaphoreType.DMA((3 * size // count,)),
        ],
        compiler_params=params(4),
        cost_estimate=cost(2 * recv.size, 14 * recv.size),
        name="finish",
    )(place, in_vmem(base), recv, old)


def exchange(x):
    return lax.ppermute(x, "role", [(0, 1), (1, 0)])


def body(rollout, w_embed, w_qkv, w_out, momentum, rewards, group_ids, timestep):
    seq_count = lax.axis_size("seq")
    seq_index = lax.axis_index("seq")
    role_index = lax.axis_index("role")
    rows_dev = w_qkv.shape[0]
    width = w_qkv.shape[2]
    heads = width // HD
    tok_dev = rollout.shape[1]
    tiles = tok_dev // TILE
    pair_rows = rows_dev // 2

    stride = 3 * heads
    unit = pair_rows // 20
    sizes = (3 * unit, 6 * unit, 6 * unit, 4 * unit, unit)
    mom = momentum.reshape(pair_rows * stride, HD)
    w = w_qkv.transpose(1, 0, 2)
    wot = w_out.T
    place = jnp.stack([seq_index, role_index])

    mine = rollout[0].T
    piece = lead(mom, mine, stride, unit, sizes[0] // unit)
    received = [exchange(piece)]
    mom, piece = lax.optimization_barrier((mom, piece))
    m, et, w, mom, *pieces = prepare(place, w_embed, mom, w, sizes[1:], stride, sizes[0], unit)
    received += [exchange(p) for p in pieces[:-1]]
    m, received[0] = lax.optimization_barrier((m, received[0]))
    ma, mb = butterfly(m, "seq")

    latent_now, latent_next, head, tail = pick(place, mine, received[0], min(2 * HD, tok_dev))
    left = lax.ppermute(tail, "seq", [(i, i + 1) for i in range(seq_count - 1)])
    right = lax.ppermute(head, "seq", [(i + 1, i) for i in range(seq_count - 1)])

    m, win, e, u, il, partial_pred = forward(place, left, latent_now, right, ma, mb, wot, tiles, heads, seq_count)
    preds = list(butterfly(partial_pred, "mp"))
    preds, received[1], last = lax.optimization_barrier((preds, received[1], pieces[-1]))
    received.append(exchange(last))
    za, zb = butterfly(
        backward(
            timestep,
            rewards[None],
            group_ids[None],
            win,
            m,
            wot,
            e,
            u,
            il,
            latent_now,
            latent_next,
            preds,
            tiles,
            heads,
            tok_dev * seq_count,
        ),
        "seq",
    )

    rest = sizes[-2] + sizes[-1]
    nm, nw, base = update(place, et, mom, w, received[:-2], sizes[:-2], rest, unit, heads, [za, zb, m, wot])
    first = sum(sizes) - rest
    nw = finish(place, base, received[-2], nw, first, 0, unit, heads)
    nw = finish(place, base, received[-1], nw, first + sizes[-2], sizes[-2], unit, heads)
    return nm.reshape(momentum.shape), nw.transpose(1, 0, 2)


def solution(mesh):
    in_specs = (
        P("role", "seq", None),
        P(),
        P("seq", None, "mp"),
        P("mp", None),
        P("seq", "role", None, "mp"),
        P(),
        P(),
        P(),
    )
    out_specs = (P("seq", "role", None, "mp"), P("seq", None, "mp"))
    return jax.shard_map(body, mesh=mesh, in_specs=in_specs, out_specs=out_specs, check_vma=False)
```
